32 devices in a mesh: dp: 8 (over y, x, core), chan: 4 (over z).
Axes of the slice: x: 2, y: 2, z: 4, core: 2. Of those that a mesh axis runs over, the one named last changes fastest.
Arguments:
- signal: bfloat16 [8, 512, 8192], P('dp', 'chan'), may hold values from -6 to 6
- signal_grad: bfloat16 [8, 512, 8192], P('dp', 'chan'), may hold values from -6 to 6
- embed_weight: float32 [64, 33], replicated, may hold values from -1 to 1
- embed_bias: float32 [64], replicated, may hold values from -3.140625 to 3.140625
- hidden_weight: float32 [64, 64], replicated, may hold values from -0.75 to 0.75
- frequency: float32 [2, 64], replicated, may hold values from 0.5 to 2
- output_weight: float32 [512, 64], replicated, may hold values from -0.75 to 0.75
- decay_rate: float32 [512], replicated, may hold values from 0.3 to 30
Outputs:
- filter_grad: float32 [512, 16384], P(None, ('dp', 'chan'))
- embed_grad: float32 [64, 33], replicated
- bias_grad: float32 [64], replicated
- hidden_grad: float32 [64, 64], replicated
- frequency_grad: float32 [2, 64], replicated
- output_grad: float32 [512, 64], replicated
- decay_grad: float32 [512], replicated
The draws below stay inside these ranges and needn't reach their ends.
All inputs are finite; a program needn't handle non-finite values.
Results may differ from the reference program's by a relative error of at most 0.0003.
Values may be sent and summed in bfloat16 or wider, within the bound.
No kernel may reach another device: no remote copies, remote signals or barrier semaphores. Data moves between devices by JAX's collectives and lax.ppermute only.
A program may use at most 64 MiB of HBM per device.

```python
import math
import jax
import jax.numpy as jnp
from jax import lax

CH = 512
HID = 64
L = 8192
EMB = 33
SEQS = 8


def shard_levels(own_key, shape, shards, least, top_value):
    level, own = 1.0, jax.random.fold_in(own_key, 6)
    for axis_at, blocks in shards:
        steps = jnp.exp(jax.random.uniform(jax.random.fold_in(own, axis_at), (blocks,), jnp.float32, least / len(shards), top_value / len(shards)))
        level = level * jnp.repeat(steps, shape[axis_at] // blocks).reshape([-1 if axis == axis_at else 1 for axis in range(len(shape))])
    return level


def noise(stream_key, shape, width, most, split=(), kind=jnp.bfloat16):
    values = width * jax.random.normal(stream_key, shape, jnp.float32)
    if split:
        values = values * shard_levels(stream_key, shape, split, -0.22, 0.18)
    return jnp.clip(values, -most, most).astype(kind)


def setup_inputs(seed: int = 0) -> dict:
    keys = jax.random.split(jax.random.key(seed), 9)
    signal = noise(keys[0], (SEQS, CH, L), 1.0, 6.0, ((0, 8), (1, 4)))
    signal_grad = noise(keys[1], (SEQS, CH, L), 1.0, 6.0, ((0, 8), (1, 4)))
    embed_weight = noise(keys[2], (HID, EMB), EMB ** -0.5, 1.0, (), jnp.float32)
    embed_bias = jnp.clip(jax.random.uniform(keys[3], (HID,), jnp.float32, -3.140625, 3.140625), -3.140625, 3.140625)
    hidden_weight = noise(keys[4], (HID, HID), HID ** -0.5, 0.75, (), jnp.float32)
    frequency = jnp.clip(jnp.exp(jax.random.uniform(keys[5], (2, HID), jnp.float32, math.log(0.5), math.log(2.0))), 0.5, 2.0)
    output_weight = noise(keys[6], (CH, HID), HID ** -0.5, 0.75, (), jnp.float32)
    decay_rate = jnp.clip(jnp.exp(jax.random.uniform(keys[7], (CH,), jnp.float32, math.log(0.3), math.log(30.0))), 0.3, 30.0)
    return dict(signal=signal, signal_grad=signal_grad, embed_weight=embed_weight, embed_bias=embed_bias, hidden_weight=hidden_weight, frequency=frequency, output_weight=output_weight, decay_rate=decay_rate)


def lag_features(lag, length, bands):
    total = 2 * length
    scaled = lag.astype(jnp.float32) / length
    sines = []
    cosines = []
    for band in range(bands):
        factor = max(1, int(0.45 * total * 10000.0 ** (-band / bands)))
        phase = (lag * factor % total).astype(jnp.float32) * (2.0 * math.pi / total)
        sines.append(jnp.sin(phase))
        cosines.append(jnp.cos(phase))
    return jnp.stack([scaled] + sines + cosines)

def filter_loss(params, lag, cotangent, length):
    embed_weight, embed_bias, hidden_weight, frequency, output_weight, decay_rate = params
    bands = (embed_weight.shape[1] - 1) // 2
    exact = lax.Precision.HIGHEST
    table = lag_features(lag, length, bands)
    first = jnp.sin(frequency[0][:, None] * (jnp.dot(embed_weight, table, precision=exact, preferred_element_type=jnp.float32) + embed_bias[:, None]))
    second = jnp.sin(frequency[1][:, None] * jnp.dot(hidden_weight, first, precision=exact, preferred_element_type=jnp.float32))
    shaped = jnp.dot(output_weight, second, precision=exact, preferred_element_type=jnp.float32)
    window = jnp.exp(-decay_rate[:, None] * jnp.abs(lag).astype(jnp.float32)[None, :] / length)
    return jnp.sum(shaped * window * cotangent) / math.sqrt(2 * length)

def reference(signal, signal_grad, embed_weight, embed_bias, hidden_weight, frequency, output_weight, decay_rate):
    total = 2 * L
    block = 32 if CH % 32 == 0 else CH

    def one_block(index):
        start = index * block
        inputs = lax.dynamic_slice_in_dim(signal, start, block, 1).astype(jnp.float32)
        grads = lax.dynamic_slice_in_dim(signal_grad, start, block, 1).astype(jnp.float32)
        spectrum_in = jnp.fft.rfft(inputs, n=total, axis=-1)
        spectrum_grad = jnp.fft.rfft(grads, n=total, axis=-1)
        cross = lax.optimization_barrier(jnp.sum(jnp.conj(spectrum_in) * spectrum_grad, axis=0))
        return jnp.fft.irfft(cross, n=total, axis=-1)
    blocks = lax.map(one_block, jnp.arange(CH // block, dtype=jnp.int32))
    filter_grad = blocks.reshape(CH, total) / math.sqrt(SEQS * L)
    position = jnp.arange(total, dtype=jnp.int32)
    lag = jnp.where(position < L, position, position - total)
    params = (embed_weight, embed_bias, hidden_weight, frequency, output_weight, decay_rate)
    grads = jax.grad(filter_loss)(params, lag, filter_grad, L)
    return (filter_grad, grads[0], grads[1], grads[2], grads[3], grads[4], grads[5])
```

```python
import functools
import math

import jax
import jax.numpy as jnp
import numpy as np
from jax import lax
from jax.experimental import pallas as pl
from jax.experimental.pallas import tpu as pltpu
from jax.sharding import PartitionSpec as P

LANES = 128
F32 = jnp.float32
BF16 = jnp.bfloat16


def lag_features(lag, length, bands):
    total = 2 * length
    scaled = lag.astype(jnp.float32) / length
    sines = []
    cosines = []
    for band in range(bands):
        factor = max(1, int(0.45 * total * 10000.0 ** (-band / bands)))
        phase = (lag * factor % total).astype(jnp.float32) * (2.0 * math.pi / total)
        sines.append(jnp.sin(phase))
        cosines.append(jnp.cos(phase))
    return jnp.stack([scaled] + sines + cosines)


def filter_loss(params, lag, cotangent, length):
    embed_weight, embed_bias, hidden_weight, frequency, output_weight, decay_rate = params
    bands = (embed_weight.shape[1] - 1) // 2
    exact = lax.Precision.HIGHEST
    table = lag_features(lag, length, bands)
    first = jnp.sin(
        frequency[0][:, None]
        * (
            jnp.dot(embed_weight, table, precision=exact, preferred_element_type=jnp.float32)
            + embed_bias[:, None]
        )
    )
    second = jnp.sin(
        frequency[1][:, None]
        * jnp.dot(hidden_weight, first, precision=exact, preferred_element_type=jnp.float32)
    )
    shaped = jnp.dot(output_weight, second, precision=exact, preferred_element_type=jnp.float32)
    window = jnp.exp(-decay_rate[:, None] * jnp.abs(lag).astype(jnp.float32)[None, :] / length)
    return jnp.sum(shaped * window * cotangent) / math.sqrt(2 * length)


def split(values):
    high = values.astype(BF16)
    return high, (values - high.astype(F32)).astype(BF16)


def split_table(values):
    high = values.astype(BF16)
    return high, (values - high.astype(np.float64)).astype(BF16)


def tables(rows, scale):
    total = 2 * rows * LANES
    odd = 2 * np.arange(rows) + 1
    angle = np.pi * (odd[:, None] * np.arange(2 * rows)[None, :] % (4 * rows)) / (2 * rows)
    first = np.concatenate([np.cos(angle[:, :rows]), -np.sin(angle[:, :rows])], axis=0)
    first = np.concatenate(split_table(first), axis=1)
    turn = np.pi * (odd[:, None] * np.arange(LANES)[None, :]) / total
    twist = np.stack([np.cos(turn), -np.sin(turn)]).astype(np.float32)
    untwist = (np.stack([np.cos(turn), np.sin(turn)]) * scale).astype(np.float32)
    fine = 2 * np.pi * (np.arange(LANES)[:, None] * np.arange(LANES)[None, :] % LANES) / LANES
    cosine, sine = np.cos(fine), np.sin(fine)
    second = np.block([[cosine, -sine], [sine, cosine]])
    sign = np.where(np.arange(2 * rows) < rows, 1.0, -1.0)[:, None]
    last = np.concatenate([np.cos(angle).T, -np.sin(angle).T], axis=1) * sign
    last_high, last_low = split_table(last)
    last = np.concatenate([last_high, last_low, last_high], axis=1)
    second_high, second_low = split_table(second)
    back_high, back_low = split_table(second.T)
    return first, twist, untwist, second_high, second_low, back_high, back_low, last


def dot(a, b):
    return jnp.dot(a, b, preferred_element_type=F32)


def correlate_kernel(
    x_ref, g_ref, first_ref, twist_ref, untwist_ref, sh_ref, sl_ref, bh_ref, bl_ref, last_ref,
    out_ref, high_ref, low_ref, spec_ref,
):
    seqs, _, rows, _ = x_ref.shape
    cosine = jnp.concatenate([twist_ref[0]] * 2, axis=1)
    sine = jnp.concatenate([twist_ref[1]] * 2, axis=1)
    first = first_ref[...]
    for s in range(seqs):
        pair = jnp.concatenate([x_ref[s, 0], g_ref[s, 0]], axis=1)
        both = dot(first, jnp.concatenate([pair, pair], axis=0))
        real, imag = both[:rows], both[rows:]
        real, imag = real * cosine - imag * sine, real * sine + imag * cosine
        for at, part in ((0, slice(0, LANES)), (1, slice(LANES, 2 * LANES))):
            line = pl.ds((at * seqs + s) * rows, rows)
            row = jnp.concatenate([real[:, part], imag[:, part]], axis=1)
            high_ref[line, :], low_ref[line, :] = split(row)
    spec_ref[...] = (
        dot(high_ref[...], sh_ref[...])
        + dot(low_ref[...], sh_ref[...])
        + dot(high_ref[...], sl_ref[...])
    )
    real = jnp.zeros((rows, LANES), F32)
    imag = jnp.zeros((rows, LANES), F32)
    for s in range(seqs):
        a = spec_ref[pl.ds(s * rows, rows), :]
        b = spec_ref[pl.ds((seqs + s) * rows, rows), :]
        a_real, a_imag, b_real, b_imag = a[:, :LANES], a[:, LANES:], b[:, :LANES], b[:, LANES:]
        real = real + (a_real * b_real + a_imag * b_imag)
        imag = imag + (a_real * b_imag - a_imag * b_real)
    high, low = split(jnp.concatenate([real, imag], axis=1))
    back = dot(high, bh_ref[...]) + dot(low, bh_ref[...]) + dot(high, bl_ref[...])
    real, imag = back[:, :LANES], back[:, LANES:]
    cosine, sine = untwist_ref[0], untwist_ref[1]
    turned = jnp.concatenate([real * cosine - imag * sine, real * sine + imag * cosine], axis=0)
    high, low = split(turned)
    out_ref[0] = dot(last_ref[...], jnp.concatenate([high, high, low], axis=0))


def correlate(x, g, scale):
    seqs, channels, rows, lanes = x.shape
    total = 2 * rows * lanes
    consts = [jnp.asarray(t) for t in tables(rows, 2.0 * scale / total)]
    block = pl.BlockSpec((seqs, 1, rows, lanes), lambda c: (0, c, 0, 0))
    whole = [
        pl.BlockSpec(t.shape, functools.partial(lambda n, c: (0,) * n, t.ndim)) for t in consts
    ]
    return pl.pallas_call(
        correlate_kernel,
        grid=(channels,),
        in_specs=[block, block] + whole,
        out_specs=pl.BlockSpec((1, 2 * rows, lanes), lambda c: (c, 0, 0)),
        out_shape=jax.ShapeDtypeStruct((channels, 2 * rows, lanes), F32),
        scratch_shapes=[
            pltpu.VMEM((2 * seqs * rows, 2 * lanes), BF16),
            pltpu.VMEM((2 * seqs * rows, 2 * lanes), BF16),
            pltpu.VMEM((2 * seqs * rows, 2 * lanes), F32),
        ],
        name="correlate",
    )(x, g, *consts)


def sum_everywhere(parts, axes, count):
    flat = jnp.concatenate([p.reshape(-1) for p in parts])
    unit = count * 8 * LANES
    padded = -(-flat.shape[0] // unit) * unit
    flat = jnp.pad(flat, (0, padded - flat.shape[0])).reshape(count, -1, LANES)
    pieces = lax.all_to_all(flat, axes, 0, 0, tiled=True)
    mine = jnp.sum(pieces, axis=0)
    sums = lax.all_to_all(
        jnp.broadcast_to(mine[None], flat.shape), axes, 0, 0, tiled=True
    ).reshape(-1)
    out, at = [], 0
    for p in parts:
        out.append(sums[at : at + p.size].reshape(p.shape))
        at += p.size
    return out


def local(
    signal,
    signal_grad,
    embed_weight,
    embed_bias,
    hidden_weight,
    frequency,
    output_weight,
    decay_rate,
):
    seq_local, chan_local, length = signal.shape
    total = 2 * length
    dp, chan = lax.axis_size("dp"), lax.axis_size("chan")
    rows = length // LANES
    own = chan_local // dp
    axes = ("dp", "chan")
    scale = 1.0 / math.sqrt(seq_local * dp * length)

    def gather(values):
        values = values.reshape(seq_local, dp, own, rows, LANES)
        values = jnp.swapaxes(values, 0, 1)
        values = lax.all_to_all(values, "dp", 0, 0, tiled=True)
        return values.reshape(dp * seq_local, own, rows, LANES)

    lags = correlate(gather(signal), gather(signal_grad), scale)
    count = dp * chan
    lag_count = total // count
    lags = jnp.swapaxes(lags.reshape(own, count, lag_count), 0, 1)
    shared = lax.all_to_all(lags, axes, 0, 0, tiled=True)
    filter_grad = jnp.swapaxes(shared.reshape(dp, chan, own, lag_count), 0, 1).reshape(
        chan * chan_local, lag_count
    )
    device_rank = lax.axis_index("dp") * chan + lax.axis_index("chan")
    position = device_rank * lag_count + jnp.arange(lag_count, dtype=jnp.int32)
    lag = jnp.where(position < length, position, position - total)
    params = (embed_weight, embed_bias, hidden_weight, frequency, output_weight, decay_rate)
    local_grads = jax.grad(filter_loss)(params, lag, filter_grad, length)
    summed = sum_everywhere(local_grads, axes, count)
    return (filter_grad, *summed)


def solution(mesh):
    placed = (P("dp", "chan", None), P("dp", "chan", None), P(), P(), P(), P(), P(), P())
    return jax.shard_map(
        local,
        mesh=mesh,
        in_specs=placed,
        out_specs=(P(None, ("dp", "chan")), P(), P(), P(), P(), P(), P()),
        check_vma=False,
    )
```

```python
import functools
import math

import jax
import jax.numpy as jnp
import numpy as np
from jax import lax
from jax.experimental import pallas as pl
from jax.experimental.pallas import tpu as pltpu
from jax.sharding import PartitionSpec as P


LANES = 128
F32 = jnp.float32
BF16 = jnp.bfloat16


def split(values):
    high = values.astype(BF16)
    return high, (values - high.astype(F32)).astype(BF16)


def split_table(values):
    high = values.astype(BF16)
    return high, (values - high.astype(np.float64)).astype(BF16)


def tables(rows, scale):
    total = 2 * rows * LANES
    odd = 2 * np.arange(rows) + 1
    angle = np.pi * (odd[:, None] * np.arange(2 * rows)[None, :] % (4 * rows)) / (2 * rows)
    first = np.concatenate([np.cos(angle[:, :rows]), -np.sin(angle[:, :rows])], axis=0)
    first = np.concatenate(split_table(first), axis=1)
    turn = np.pi * (odd[:, None] * np.arange(LANES)[None, :]) / total
    twist = np.stack([np.cos(turn), -np.sin(turn)]).astype(np.float32)
    untwist = (np.stack([np.cos(turn), np.sin(turn)]) * scale).astype(np.float32)
    fine = 2 * np.pi * (np.arange(LANES)[:, None] * np.arange(LANES)[None, :] % LANES) / LANES
    cosine, sine = np.cos(fine), np.sin(fine)
    second = np.block([[cosine, -sine], [sine, cosine]])
    sign = np.where(np.arange(2 * rows) < rows, 1.0, -1.0)[:, None]
    last = np.concatenate([np.cos(angle).T, -np.sin(angle).T], axis=1) * sign
    last_high, last_low = split_table(last)
    last = np.concatenate([last_high, last_low, last_high], axis=1)
    second, back = (
        np.concatenate([high, high, low], axis=0)
        for high, low in (split_table(second), split_table(second.T))
    )
    return first, twist, untwist, second, back, last


def dot(a, b):
    return jnp.dot(a, b, preferred_element_type=F32)


def stacked(values, axis):
    high, low = split(values)
    return jnp.concatenate([high, low], axis=axis)


def narrow(values, axis):
    high = lax.reduce_precision(values, 8, 7)
    low = (values - high).astype(BF16)
    high = high.astype(BF16)
    return jnp.concatenate([high, low, high], axis=axis)


def wide(values, axis):
    high, low = split(values)
    return jnp.concatenate([high, high, low], axis=axis)


def dot_lanes(a, b):
    return lax.dot_general(a, b, (((1,), (1,)), ((), ())), preferred_element_type=F32)


def sine_cosine(angle):
    turns = jnp.round(angle * (2.0 / math.pi))
    rest = angle - turns * 1.5703125
    rest = rest - turns * 4.837512969970703125e-4
    rest = rest - turns * 7.54978995489188216e-8
    square = rest * rest
    odd = ((-1.9515295891e-4 * square + 8.3321608736e-3) * square - 1.6666654611e-1) * square
    odd = odd * rest + rest
    even = (2.443315711809948e-5 * square - 1.388731625493765e-3) * square + 4.166664568298827e-2
    even = even * square * square - 0.5 * square + 1.0
    quarter = turns.astype(jnp.int32)
    swap = (quarter & 1) != 0
    sine = jnp.where(swap, even, odd)
    cosine = jnp.where(swap, odd, even)
    sine = jnp.where((quarter & 2) != 0, -sine, sine)
    cosine = jnp.where(((quarter + 1) & 2) != 0, -cosine, cosine)
    return sine, cosine


def pick(x, g, block, own, start, count):
    first = block * own + start
    return jnp.stack([lax.dynamic_slice_in_dim(v, first, count, 1) for v in (x, g)])


def correlate_kernel(*refs, pieces):
    piece_refs = refs[:pieces]
    (
        first_ref, twist_ref, untwist_ref, second_ref, back_ref, last_ref,
        out_ref, turn_ref, high_ref, low_ref, spec_ref, lag_ref,
    ) = refs[pieces:]
    _, seqs_each, channels, length = piece_refs[0].shape
    rows = length // LANES
    seqs = pieces * seqs_each
    c = pl.program_id(0)

    @pl.when(c == 0)
    def _():
        for s in range(seqs):
            for at in range(2):
                for row in range(rows):
                    turn_ref[at * seqs + s, pl.ds(row * channels, channels), :] = piece_refs[
                        s // seqs_each
                    ][at, s % seqs_each, :, pl.ds(row * LANES, LANES)].astype(F32)

    def samples(at, s):
        return turn_ref[at * seqs + s, pl.ds(c, rows, stride=channels), :].astype(BF16)

    cosine = jnp.concatenate([twist_ref[0]] * 2, axis=1)
    sine = jnp.concatenate([twist_ref[1]] * 2, axis=1)
    first = first_ref[...]
    for s in range(seqs):
        pair = jnp.concatenate([samples(0, s), samples(1, s)], axis=1)
        both = dot(first, jnp.concatenate([pair, pair], axis=0))
        real, imag = both[:rows], both[rows:]
        real, imag = real * cosine - imag * sine, real * sine + imag * cosine
        for at, part in ((0, slice(0, LANES)), (1, slice(LANES, 2 * LANES))):
            line = pl.ds((at * seqs + s) * rows, rows)
            row = jnp.concatenate([real[:, part], imag[:, part]], axis=1)
            high_ref[line, :], low_ref[line, :] = split(row)
    spec_ref[...] = dot(
        jnp.concatenate([high_ref[...], low_ref[...], high_ref[...]], axis=1), second_ref[...]
    )
    real = jnp.zeros((rows, LANES), F32)
    imag = jnp.zeros((rows, LANES), F32)
    for s in range(seqs):
        a = spec_ref[pl.ds(s * rows, rows), :]
        b = spec_ref[pl.ds((seqs + s) * rows, rows), :]
        a_real, a_imag, b_real, b_imag = a[:, :LANES], a[:, LANES:], b[:, :LANES], b[:, LANES:]
        real = real + (a_real * b_real + a_imag * b_imag)
        imag = imag + (a_real * b_imag - a_imag * b_real)
    high, low = split(jnp.concatenate([real, imag], axis=1))
    back = dot(jnp.concatenate([high, low, high], axis=1), back_ref[...])
    real, imag = back[:, :LANES], back[:, LANES:]
    cosine, sine = untwist_ref[0], untwist_ref[1]
    turned = jnp.concatenate([real * cosine - imag * sine, real * sine + imag * cosine], axis=0)
    high, low = split(turned)
    lag_ref[pl.ds(pl.multiple_of(c * 2 * rows, 2 * rows), 2 * rows), :] = dot(
        last_ref[...], jnp.concatenate([high, high, low], axis=0)
    )

    @pl.when(c == pl.num_programs(0) - 1)
    def _():
        owners, channels, lag_count = out_ref.shape
        each = lag_count // LANES
        for owner in range(owners):
            for k in range(each):
                out_ref[owner, :, pl.ds(k * LANES, LANES)] = lag_ref[
                    pl.ds(owner * each + k, channels, stride=2 * rows), :
                ]


def correlate(pieces, scale, owners):
    _, seqs_each, channels, length = pieces[0].shape
    lanes, rows = LANES, length // LANES
    seqs = seqs_each * len(pieces)
    total = 2 * rows * lanes
    consts = [jnp.asarray(t) for t in tables(rows, 2.0 * scale / total)]
    block = pl.BlockSpec(pieces[0].shape, lambda c: (0, 0, 0, 0))
    whole = [
        pl.BlockSpec(t.shape, functools.partial(lambda n, c: (0,) * n, t.ndim)) for t in consts
    ]
    shape = (owners, channels, total // owners)
    return pl.pallas_call(
        functools.partial(correlate_kernel, pieces=len(pieces)),
        grid=(channels,),
        in_specs=[block] * len(pieces) + whole,
        out_specs=pl.BlockSpec(shape, lambda c: (0, 0, 0)),
        out_shape=jax.ShapeDtypeStruct(shape, F32),
        scratch_shapes=[
            pltpu.VMEM((2 * seqs, rows * channels, lanes), F32),
            pltpu.VMEM((2 * seqs * rows, 2 * lanes), BF16),
            pltpu.VMEM((2 * seqs * rows, 2 * lanes), BF16),
            pltpu.VMEM((2 * seqs * rows, 2 * lanes), F32),
            pltpu.VMEM((channels * 2 * rows, lanes), F32),
        ],
        cost_estimate=pl.CostEstimate(
            flops=channels * seqs * 2 * rows * lanes * lanes * 36,
            bytes_accessed=channels * (seqs * rows * lanes * 4 + total * 4),
            transcendentals=0,
        ),
        name="correlate",
    )(*pieces, *consts)


STEP = 1024
BANDS_PAD = 8


def lag_row(step, total):
    position = step * STEP + lax.broadcasted_iota(jnp.int32, (1, STEP), 1)
    return jnp.where(position < total // 2, position, position - total)


def network_kernel(
    factor_ref, embed_ref, hidden_ref, freq_ref, table_ref, first_ref, second_ref, cos1_ref, cos2_ref, *, total
):
    lag = lag_row(pl.program_id(0), total)
    length = total // 2
    phase = ((factor_ref[...] * lag) & (total - 1)).astype(F32) * (2.0 * math.pi / total)
    sine, cosine = sine_cosine(phase)
    scaled = lag.astype(F32) / length
    row = lax.broadcasted_iota(jnp.int32, (BANDS_PAD, STEP), 0)
    extra = jnp.where(row == 0, scaled, jnp.where(row == 1, 1.0, 0.0))
    table = jnp.concatenate([sine, cosine, extra], axis=0)
    table_ref[...] = stacked(table, 0)
    first, cos1 = sine_cosine(freq_ref[:, :1] * dot(embed_ref[...], wide(table, 0)))
    first_ref[...] = stacked(first, 0)
    cos1_ref[...] = cos1
    second, cos2 = sine_cosine(freq_ref[:, 1:] * dot(hidden_ref[...], wide(first, 0)))
    second_ref[...] = stacked(second, 0)
    cos2_ref[...] = cos2


def network(embed_weight, embed_bias, hidden_weight, frequency, total):
    hidden, features = embed_weight.shape
    bands = (features - 1) // 2
    factors = np.array(
        [[max(1, int(0.45 * total * 10000.0 ** (-band / bands)))] for band in range(bands)], np.int32
    )
    embed = jnp.concatenate(
        [
            embed_weight[:, 1:],
            embed_weight[:, :1],
            embed_bias[:, None],
            jnp.zeros((hidden, BANDS_PAD - 2), F32),
        ],
        axis=1,
    )
    args = (jnp.asarray(factors), narrow(embed, 1), narrow(hidden_weight, 1), frequency.T)
    whole = [pl.BlockSpec(a.shape, lambda i: (0, 0)) for a in args]
    heights = ((2 * (2 * bands + BANDS_PAD), BF16), (2 * hidden, BF16), (2 * hidden, BF16), (hidden, F32), (hidden, F32))
    return pl.pallas_call(
        functools.partial(network_kernel, total=total),
        grid=(total // STEP,),
        in_specs=whole,
        out_specs=[pl.BlockSpec((h, STEP), lambda i: (0, i)) for h, _ in heights],
        out_shape=[jax.ShapeDtypeStruct((h, total), t) for h, t in heights],
        cost_estimate=pl.CostEstimate(
            flops=total * hidden * 600, bytes_accessed=total * hidden * 20, transcendentals=0
        ),
        name="network",
    )(*args)


def backward_kernel(*refs, chunks, total):
    lag_refs = refs[:chunks]
    (
        table_ref, first_ref, second_ref, cos1_ref, cos2_ref, decay_ref, output_ref, hidden_ref,
        own_ref, net_ref, sum1_ref, sum3_ref, sum5_ref,
    ) = refs[chunks:]
    step = pl.program_id(0)

    @pl.when(step == 0)
    def _():
        for ref in (sum1_ref, sum3_ref, sum5_ref):
            ref[...] = jnp.zeros_like(ref)

    lags = jnp.concatenate(
        [
            jnp.concatenate([ref[k] for k in range(ref.shape[0])], axis=1)
            for ref in lag_refs
        ],
        axis=0,
    )
    length = total // 2
    distance = jnp.abs(lag_row(step, total)).astype(F32)
    window = jnp.exp(-decay_ref[...] * distance / length)
    shaped = lags * window * (1.0 / math.sqrt(total))
    far = shaped * (distance / length)
    sum1_ref[...] += dot_lanes(stacked(jnp.concatenate([shaped, far], axis=0), 0), second_ref[...])
    second = dot(output_ref[...], wide(shaped, 0)) * cos2_ref[...]
    high, low = split(second)
    sum3_ref[...] += dot_lanes(jnp.concatenate([high, low], axis=0), first_ref[...])
    first = dot(hidden_ref[...], jnp.concatenate([high, high, low], axis=0)) * cos1_ref[...]
    sum5_ref[...] += dot_lanes(stacked(first, 0), table_ref[...])

    @pl.when(step == pl.num_programs(0) - 1)
    def _():
        def joined(ref):
            rows, cols = ref.shape[0] // 2, ref.shape[1] // 2
            return ref[:rows, :cols] + ref[:rows, cols:] + ref[rows:, :cols]

        own_ref[...] = joined(sum1_ref)
        net = jnp.concatenate([joined(sum3_ref), joined(sum5_ref)], axis=1)
        net_ref[:, : net.shape[1]] = net
        net_ref[:, net.shape[1] :] = jnp.zeros((net.shape[0], LANES - net.shape[1]), F32)


def backward(lags, saved, decay, output_weight, hidden_weight, frequency, total):
    _, _, lag_count = lags[0].shape
    own = output_weight.shape[0]
    hidden = hidden_weight.shape[0]
    table, _, _, _, _ = saved
    args = (
        decay[:, None],
        narrow(output_weight.T, 1),
        narrow((hidden_weight * frequency[1][:, None]).T, 1),
    )
    specs = [pl.BlockSpec((STEP // lag_count, a.shape[1], lag_count), lambda i: (i, 0, 0)) for a in lags]
    specs += [pl.BlockSpec((a.shape[0], STEP), lambda i: (0, i)) for a in saved]
    specs += [pl.BlockSpec(a.shape, lambda i: (0, 0)) for a in args]
    return pl.pallas_call(
        functools.partial(backward_kernel, chunks=len(lags), total=total),
        grid=(total // STEP,),
        in_specs=specs,
        out_specs=[
            pl.BlockSpec((2 * own, hidden), lambda i: (0, 0)),
            pl.BlockSpec((hidden, LANES), lambda i: (0, 0)),
        ],
        out_shape=[
            jax.ShapeDtypeStruct((2 * own, hidden), F32),
            jax.ShapeDtypeStruct((hidden, LANES), F32),
        ],
        scratch_shapes=[
            pltpu.VMEM((4 * own, 2 * hidden), F32),
            pltpu.VMEM((2 * hidden, 2 * hidden), F32),
            pltpu.VMEM((2 * hidden, table.shape[0]), F32),
        ],
        cost_estimate=pl.CostEstimate(
            flops=total * hidden * 2000, bytes_accessed=total * hidden * 20, transcendentals=0
        ),
        name="backward",
    )(*lags, *saved, *args)


def share(net, own):
    own = own[None]
    for axis in ("chan", "dp"):
        size = lax.axis_size(axis)
        place = lax.axis_index(axis)
        bit = size // 2
        lead = own.shape[0] if axis == "dp" else 1
        own = own.reshape(lead, 1, *own.shape[-2:])
        while bit:
            swap = [(i, i ^ bit) for i in range(size)]
            got_net, got = lax.ppermute((net, own), axis, swap)
            net = net + got_net
            upper = (place & bit) != 0
            own = jnp.stack(
                [jnp.where(upper, got, own), jnp.where(upper, own, got)], axis=2
            ).reshape(lead, -1, *own.shape[-2:])
            bit //= 2
        own = own.reshape(-1, *own.shape[-2:])
    return net, own.reshape(-1, own.shape[-1])


def work(
    signal,
    signal_grad,
    embed_weight,
    embed_bias,
    hidden_weight,
    frequency,
    output_weight,
    decay_rate,
):
    seq_local, chan_local, length = signal.shape
    total = 2 * length
    dp, chan = lax.axis_size("dp"), lax.axis_size("chan")
    own = chan_local // dp
    count = dp * chan
    lag_count = total // count
    hidden, features = embed_weight.shape
    scale = 1.0 / math.sqrt(seq_local * dp * length)
    at_dp, at_chan = lax.axis_index("dp"), lax.axis_index("chan")

    chunks = 2 if own % 16 == 0 else 1
    per = own // chunks
    order = sorted(range(1, dp), key=lambda p: -bin(p).count("1"))
    lags = []
    for q in range(chunks):
        pieces = []
        for p in order:
            sent = pick(signal, signal_grad, at_dp ^ p, own, q * per, per)
            pieces.append(lax.ppermute(sent, "dp", [(i, i ^ p) for i in range(dp)]))
        pieces.append(pick(signal, signal_grad, at_dp, own, q * per, per))
        lags.append(correlate(pieces, scale, count))

    saved = network(embed_weight, embed_bias, hidden_weight, frequency, total)
    first_own = at_chan * chan_local + at_dp * own
    my_output = lax.dynamic_slice_in_dim(output_weight, first_own, own, 0)
    my_decay = lax.dynamic_slice_in_dim(decay_rate, first_own, own, 0)
    shared = []
    for q in range(chunks):
        shared.append(lax.all_to_all(lags[q], ("dp", "chan"), 0, 0, tiled=True))
    sums, net = backward(lags, saved, my_decay, my_output, hidden_weight, frequency, total)
    my_decay_grad = -jnp.sum(my_output * sums[own:], axis=1, keepdims=True)
    mine = jnp.concatenate(
        [sums[:own], my_decay_grad, jnp.zeros((own, LANES - hidden - 1), F32)], axis=1
    )
    net, rows = share(net, mine)

    shared = jnp.stack([part.reshape(dp, chan, per, lag_count) for part in shared], axis=2)
    filter_grad = jnp.swapaxes(shared, 0, 1).reshape(chan * chan_local, lag_count)

    hidden_sums = net[:, :hidden]
    table_sums = net[:, hidden : hidden + features + 1]
    embed_sums = jnp.concatenate([table_sums[:, features - 1 : features], table_sums[:, : features - 1]], axis=1)
    bias_sums = table_sums[:, features]
    embed_grad = frequency[0][:, None] * embed_sums
    bias_grad = frequency[0] * bias_sums
    hidden_grad = frequency[1][:, None] * hidden_sums
    frequency_grad = jnp.stack(
        [
            jnp.sum(embed_weight * embed_sums, axis=1) + embed_bias * bias_sums,
            jnp.sum(hidden_weight * hidden_sums, axis=1),
        ]
    )
    return (
        filter_grad,
        embed_grad,
        bias_grad,
        hidden_grad,
        frequency_grad,
        rows[:, :hidden],
        rows[:, hidden],
    )


def solution(mesh):
    placed = (P("dp", "chan", None), P("dp", "chan", None), P(), P(), P(), P(), P(), P())
    return jax.shard_map(
        work,
        mesh=mesh,
        in_specs=placed,
        out_specs=(P(None, ("dp", "chan")), P(), P(), P(), P(), P(), P()),
        check_vma=False,
    )
```

```python
import functools
import math

import jax
import jax.numpy as jnp
import numpy as np
from jax import lax
from jax.experimental import pallas as pl
from jax.experimental.pallas import tpu as pltpu
from jax.sharding import PartitionSpec as P


LANES = 128
F32 = jnp.float32
BF16 = jnp.bfloat16


def split(values):
    high = values.astype(BF16)
    return high, (values - high.astype(F32)).astype(BF16)


def split_table(values):
    high = values.astype(BF16)
    return high, (values - high.astype(np.float64)).astype(BF16)


def tables(rows, scale):
    total = 2 * rows * LANES
    odd = 2 * np.arange(rows) + 1
    angle = np.pi * (odd[:, None] * np.arange(2 * rows)[None, :] % (4 * rows)) / (2 * rows)
    first = np.concatenate([np.cos(angle[:, :rows]), -np.sin(angle[:, :rows])], axis=0)
    first = np.concatenate(split_table(first), axis=1)
    turn = np.pi * (odd[:, None] * np.arange(LANES)[None, :]) / total
    twist = np.stack([np.cos(turn), -np.sin(turn)]).astype(np.float32)
    untwist = (np.stack([np.cos(turn), np.sin(turn)]) * scale).astype(np.float32)
    fine = 2 * np.pi * (np.arange(LANES)[:, None] * np.arange(LANES)[None, :] % LANES) / LANES
    cosine, sine = np.cos(fine), np.sin(fine)
    second = np.block([[cosine, -sine], [sine, cosine]])
    sign = np.where(np.arange(2 * rows) < rows, 1.0, -1.0)[:, None]
    last = np.concatenate([np.cos(angle).T, -np.sin(angle).T], axis=1) * sign
    last_high, last_low = split_table(last)
    last = np.concatenate([last_high, last_low, last_high], axis=1)
    second, back = (
        np.concatenate([high, high, low], axis=0)
        for high, low in (split_table(second), split_table(second.T))
    )
    return first, twist, untwist, second, back, last


def dot(a, b):
    return jnp.dot(a, b, preferred_element_type=F32)


def stacked(values, axis):
    high, low = split(values)
    return jnp.concatenate([high, low], axis=axis)


def narrow(values, axis):
    high, low = split(values)
    return jnp.concatenate([high, low, high], axis=axis)


def wide(values, axis):
    high, low = split(values)
    return jnp.concatenate([high, high, low], axis=axis)


def dot_lanes(a, b):
    return lax.dot_general(a, b, (((1,), (1,)), ((), ())), preferred_element_type=F32)


def sine_cosine(angle):
    turns = (angle * (1.0 / math.pi) + 12582912.0) - 12582912.0
    rest = (angle - turns * 3.140625) - turns * 9.67653589793e-4
    sign = jnp.where((turns.astype(jnp.int32) & 1) != 0, -1.0, 1.0)
    square = rest * rest
    rest = rest * sign
    sine = (2.6000244184306192e-6 * square - 1.9806601562034863e-4) * square + 8.333017104043598e-3
    sine = (sine * square - 0.1666665708890745) * square * rest + rest
    cosine = (-2.6076816602017467e-7 * square + 2.4761870623092258e-5) * square
    cosine = ((cosine - 1.3888403220356624e-3) * square + 4.1666640707487275e-2) * square
    cosine = (cosine - 0.49999999549109586) * square + 1.0
    return sine, cosine * sign


def column(row):
    size = row.shape[1]
    at = [lax.broadcasted_iota(jnp.int32, (size, size), d) for d in (0, 1)]
    return jnp.sum(jnp.where(at[0] == at[1], row, 0.0), axis=1, keepdims=True)


def pick_kernel(x_ref, g_ref, *refs, partners, own, start):
    outs, (held_ref, in_sem, out_sem) = refs[: len(partners)], refs[len(partners) :]
    per = outs[0].shape[2]
    arrivals, departures = [], []
    for k, partner in enumerate(partners):
        first = pl.multiple_of((lax.axis_index("dp") ^ partner) * own + start, per)
        for at, ref in enumerate((x_ref, g_ref)):
            arrivals.append(
                pltpu.make_async_copy(
                    ref.at[:, pl.ds(first, per), :], held_ref.at[k, at], in_sem.at[k, at]
                )
            )
            arrivals[-1].start()
    for k in range(len(partners)):
        arrivals[2 * k].wait()
        arrivals[2 * k + 1].wait()
        departures.append(pltpu.make_async_copy(held_ref.at[k], outs[k], out_sem.at[k]))
        departures[-1].start()
    for departure in departures:
        departure.wait()


def pick(x, g, partners, own, start, count):
    seqs, _, length = x.shape
    shape = (2, seqs, count, length)
    if count % 8:
        firsts = [(lax.axis_index("dp") ^ p) * own + start for p in partners]
        return [
            jnp.stack([lax.dynamic_slice_in_dim(v, first, count, 1) for v in (x, g)])
            for first in firsts
        ]
    anywhere = pl.BlockSpec(memory_space=pl.ANY)
    return pl.pallas_call(
        functools.partial(pick_kernel, partners=partners, own=own, start=start),
        in_specs=[anywhere, anywhere],
        out_specs=[anywhere] * len(partners),
        out_shape=[jax.ShapeDtypeStruct(shape, BF16)] * len(partners),
        scratch_shapes=[
            pltpu.VMEM((len(partners), *shape), BF16),
            pltpu.SemaphoreType.DMA((len(partners), 2)),
            pltpu.SemaphoreType.DMA((len(partners),)),
        ],
        cost_estimate=pl.CostEstimate(
            flops=0, bytes_accessed=4 * len(partners) * math.prod(shape), transcendentals=0
        ),
        name="pick",
    )(x, g)


def correlate_kernel(*refs, pieces, held):
    piece_refs = refs[:pieces]
    refs = refs[:pieces] + refs[pieces + held :]
    (
        first_ref, twist_ref, untwist_ref, second_ref, back_ref, last_ref,
        out_ref, turn_ref, high_ref, low_ref, spec_ref, lag_ref,
    ) = refs[pieces:]
    _, seqs_each, channels, length = piece_refs[0].shape
    rows = length // LANES
    seqs = pieces * seqs_each
    c = pl.program_id(0)

    @pl.when(c == 0)
    def _():
        for s in range(seqs):
            for at in range(2):
                for row in range(rows):
                    turn_ref[at * seqs + s, pl.ds(row * channels, channels), :] = piece_refs[
                        s // seqs_each
                    ][at, s % seqs_each, :, pl.ds(row * LANES, LANES)].astype(F32)

    def samples(at, s):
        return turn_ref[at * seqs + s, pl.ds(c, rows, stride=channels), :].astype(BF16)

    cosine = jnp.concatenate([twist_ref[0]] * 2, axis=1)
    sine = jnp.concatenate([twist_ref[1]] * 2, axis=1)
    first = first_ref[...]
    for s in range(seqs):
        pair = jnp.concatenate([samples(0, s), samples(1, s)], axis=1)
        both = dot(first, jnp.concatenate([pair, pair], axis=0))
        real, imag = both[:rows], both[rows:]
        real, imag = real * cosine - imag * sine, real * sine + imag * cosine
        for at, part in ((0, slice(0, LANES)), (1, slice(LANES, 2 * LANES))):
            line = pl.ds((at * seqs + s) * rows, rows)
            row = jnp.concatenate([real[:, part], imag[:, part]], axis=1)
            high_ref[line, :], low_ref[line, :] = split(row)
    spec_ref[...] = dot(
        jnp.concatenate([high_ref[...], low_ref[...], high_ref[...]], axis=1), second_ref[...]
    )
    real = jnp.zeros((rows, LANES), F32)
    imag = jnp.zeros((rows, LANES), F32)
    for s in range(seqs):
        a = spec_ref[pl.ds(s * rows, rows), :]
        b = spec_ref[pl.ds((seqs + s) * rows, rows), :]
        a_real, a_imag, b_real, b_imag = a[:, :LANES], a[:, LANES:], b[:, :LANES], b[:, LANES:]
        real = real + (a_real * b_real + a_imag * b_imag)
        imag = imag + (a_real * b_imag - a_imag * b_real)
    high, low = split(jnp.concatenate([real, imag], axis=1))
    back = dot(jnp.concatenate([high, low, high], axis=1), back_ref[...])
    real, imag = back[:, :LANES], back[:, LANES:]
    cosine, sine = untwist_ref[0], untwist_ref[1]
    turned = jnp.concatenate([real * cosine - imag * sine, real * sine + imag * cosine], axis=0)
    high, low = split(turned)
    lag_ref[pl.ds(pl.multiple_of(c * 2 * rows, 2 * rows), 2 * rows), :] = dot(
        last_ref[...], jnp.concatenate([high, high, low], axis=0)
    )

    @pl.when(c == pl.num_programs(0) - 1)
    def _():
        owners, channels, lag_count = out_ref.shape
        each = lag_count // LANES
        for owner in range(owners):
            for k in range(each):
                out_ref[owner, :, pl.ds(k * LANES, LANES)] = lag_ref[
                    pl.ds(owner * each + k, channels, stride=2 * rows), :
                ]


def correlate(pieces, scale, owners, held, chunk, chunks):
    _, seqs_each, channels, length = pieces[0].shape
    lanes, rows = LANES, length // LANES
    seqs = seqs_each * len(pieces)
    total = 2 * rows * lanes
    consts = [jnp.asarray(t) for t in tables(rows, 2.0 * scale / total)]
    block = pl.BlockSpec(pieces[0].shape, lambda c: (0, 0, 0, 0))
    whole = [
        pl.BlockSpec(t.shape, functools.partial(lambda n, c: (0,) * n, t.ndim)) for t in consts
    ]
    held = [] if held is None else [held]
    return pl.pallas_call(
        functools.partial(correlate_kernel, pieces=len(pieces), held=len(held)),
        grid=(channels,),
        in_specs=[block] * len(pieces) + [pl.BlockSpec(memory_space=pl.ANY)] * len(held) + whole,
        out_specs=pl.BlockSpec((owners, channels, total // owners), lambda c: (0, chunk, 0)),
        out_shape=jax.ShapeDtypeStruct((owners, channels * chunks, total // owners), F32),
        input_output_aliases={len(pieces): 0} if held else {},
        scratch_shapes=[
            pltpu.VMEM((2 * seqs, rows * channels, lanes), F32),
            pltpu.VMEM((2 * seqs * rows, 2 * lanes), BF16),
            pltpu.VMEM((2 * seqs * rows, 2 * lanes), BF16),
            pltpu.VMEM((2 * seqs * rows, 2 * lanes), F32),
            pltpu.VMEM((channels * 2 * rows, lanes), F32),
        ],
        cost_estimate=pl.CostEstimate(
            flops=channels * seqs * 2 * rows * lanes * lanes * 36,
            bytes_accessed=channels * (seqs * rows * lanes * 4 + total * 4),
            transcendentals=0,
        ),
        name="correlate",
    )(*pieces, *held, *consts)


STEP = 2048
BANDS_PAD = 8


def lag_row(step, total):
    position = step * STEP + lax.broadcasted_iota(jnp.int32, (1, STEP), 1)
    return jnp.where(position < total // 2, position, position - total)


def network_kernel(
    factor_ref, embed_ref, bias_ref, hidden_ref, freq_ref,
    table_ref, first_ref, second_ref, cos1_ref, cos2_ref,
    embed_parts, hidden_parts, freq_cols, *, total,
):
    hidden = hidden_ref.shape[0]
    step = pl.program_id(0)

    @pl.when(step == 0)
    def _():
        embed = jnp.concatenate(
            [
                embed_ref[1:],
                embed_ref[:1],
                bias_ref[...],
                jnp.zeros((BANDS_PAD - 2, hidden), F32),
            ],
            axis=0,
        )
        embed_parts[...] = narrow(embed.T, 1)
        hidden_parts[...] = narrow(hidden_ref[...], 1)
        for k in range(2):
            freq_cols[k] = column(freq_ref[k : k + 1, :])

    lag = lag_row(step, total)
    length = total // 2
    phase = ((factor_ref[...] * lag) & (total - 1)).astype(F32) * (2.0 * math.pi / total)
    sine, cosine = sine_cosine(phase)
    scaled = lag.astype(F32) / length
    row = lax.broadcasted_iota(jnp.int32, (BANDS_PAD, STEP), 0)
    extra = jnp.where(row == 0, scaled, jnp.where(row == 1, 1.0, 0.0))
    table = jnp.concatenate([sine, cosine, extra], axis=0)
    table_ref[...] = stacked(table, 0)
    first, cos1 = sine_cosine(freq_cols[0] * dot(embed_parts[...], wide(table, 0)))
    first_ref[...] = stacked(first, 0)
    cos1_ref[...] = cos1
    second, cos2 = sine_cosine(freq_cols[1] * dot(hidden_parts[...], wide(first, 0)))
    second_ref[...] = stacked(second, 0)
    cos2_ref[...] = cos2


def network(embed_weight, embed_bias, hidden_weight, frequency, total):
    hidden, features = embed_weight.shape
    bands = (features - 1) // 2
    factors = np.array(
        [[max(1, int(0.45 * total * 10000.0 ** (-band / bands)))] for band in range(bands)], np.int32
    )
    args = (jnp.asarray(factors), embed_weight.T, embed_bias[None], hidden_weight, frequency)
    whole = [pl.BlockSpec(a.shape, lambda i: (0, 0)) for a in args]
    depth = 2 * bands + BANDS_PAD
    heights = ((2 * depth, BF16), (2 * hidden, BF16), (2 * hidden, BF16), (hidden, F32), (hidden, F32))
    return pl.pallas_call(
        functools.partial(network_kernel, total=total),
        grid=(total // STEP,),
        in_specs=whole,
        out_specs=[pl.BlockSpec((h, STEP), lambda i: (0, i)) for h, _ in heights],
        out_shape=[jax.ShapeDtypeStruct((h, total), t) for h, t in heights],
        scratch_shapes=[
            pltpu.VMEM((hidden, 3 * depth), BF16),
            pltpu.VMEM((hidden, 3 * hidden), BF16),
            pltpu.VMEM((2, hidden, 1), F32),
        ],
        cost_estimate=pl.CostEstimate(
            flops=total * hidden * 600, bytes_accessed=total * hidden * 20, transcendentals=0
        ),
        name="network",
    )(*args)


def backward_kernel(
    first_ref, lags_ref, table_ref, layer1_ref, layer2_ref, cos1_ref, cos2_ref,
    decay_ref, output_ref, hidden_ref, freq_ref,
    out_ref, output_parts, hidden_parts, decay_col, own_ref, sum1_ref, sum3_ref, sum5_ref, *, total,
):
    step = pl.program_id(0)
    owners, own, _ = lags_ref.shape
    hidden = hidden_ref.shape[0]

    @pl.when(step == 0)
    def _():
        for ref in (sum1_ref, sum3_ref, sum5_ref):
            ref[...] = jnp.zeros_like(ref)
        channels = output_ref.shape[1]
        own_ref[...] = pltpu.roll(output_ref[...], channels - first_ref[0], 1)[:, :own]
        output_parts[...] = narrow(own_ref[...], 1)
        hidden_parts[...] = narrow((hidden_ref[...] * column(freq_ref[1:2, :])).T, 1)
        place = [lax.broadcasted_iota(jnp.int32, (own, channels), d) for d in (0, 1)]
        decay_col[...] = jnp.sum(
            jnp.where(place[1] == place[0] + first_ref[0], decay_ref[...], 0.0), axis=1, keepdims=True
        )

    lags = jnp.concatenate([lags_ref[k] for k in range(owners)], axis=1)
    length = total // 2
    distance = jnp.abs(lag_row(step, total)).astype(F32)
    window = jnp.exp(-decay_col[...] * distance / length)
    shaped = lags * window * (1.0 / math.sqrt(total))
    far = shaped * (distance / length)
    sum1_ref[...] += dot_lanes(stacked(jnp.concatenate([shaped, far], axis=0), 0), layer2_ref[...])
    second = dot(output_parts[...], wide(shaped, 0)) * cos2_ref[...]
    high, low = split(second)
    sum3_ref[...] += dot_lanes(jnp.concatenate([high, low], axis=0), layer1_ref[...])
    first = dot(hidden_parts[...], jnp.concatenate([high, high, low], axis=0)) * cos1_ref[...]
    sum5_ref[...] += dot_lanes(stacked(first, 0), table_ref[...])

    @pl.when(step == pl.num_programs(0) - 1)
    def _():
        def joined(ref):
            rows, cols = ref.shape[0] // 2, ref.shape[1] // 2
            return ref[:rows, :cols] + ref[:rows, cols:] + ref[rows:, :cols]

        net = jnp.concatenate([joined(sum3_ref), joined(sum5_ref)], axis=1)
        out_ref[:hidden] = jnp.concatenate(
            [net, jnp.zeros((hidden, LANES - net.shape[1]), F32)], axis=1
        )
        sums = joined(sum1_ref)
        decay_grad = -jnp.sum(own_ref[...].T * sums[own:], axis=1, keepdims=True)
        out_ref[hidden:] = jnp.concatenate(
            [sums[:own], decay_grad, jnp.zeros((own, LANES - hidden - 1), F32)], axis=1
        )


def backward(first_own, lags, saved, decay_rate, output_weight, hidden_weight, frequency, total):
    _, own, lag_count = lags.shape
    hidden = hidden_weight.shape[0]
    args = (decay_rate[None], output_weight.T, hidden_weight, frequency)
    specs = [pl.BlockSpec((STEP // lag_count, own, lag_count), lambda i, first: (i, 0, 0))]
    specs += [pl.BlockSpec((a.shape[0], STEP), lambda i, first: (0, i)) for a in saved]
    specs += [pl.BlockSpec(a.shape, lambda i, first: (0, 0)) for a in args]
    return pl.pallas_call(
        functools.partial(backward_kernel, total=total),
        grid_spec=pltpu.PrefetchScalarGridSpec(
            num_scalar_prefetch=1,
            grid=(total // STEP,),
            in_specs=specs,
            out_specs=pl.BlockSpec((hidden + own, LANES), lambda i, first: (0, 0)),
            scratch_shapes=[
                pltpu.VMEM((hidden, 3 * own), BF16),
                pltpu.VMEM((hidden, 3 * hidden), BF16),
                pltpu.VMEM((own, 1), F32),
                pltpu.VMEM((hidden, own), F32),
                pltpu.VMEM((4 * own, 2 * hidden), F32),
                pltpu.VMEM((2 * hidden, 2 * hidden), F32),
                pltpu.VMEM((2 * hidden, saved[0].shape[0]), F32),
            ],
        ),
        out_shape=jax.ShapeDtypeStruct((hidden + own, LANES), F32),
        cost_estimate=pl.CostEstimate(
            flops=total * hidden * 2000, bytes_accessed=total * hidden * 20, transcendentals=0
        ),
        name="backward",
    )(first_own.reshape(1), lags, *saved, *args)


def share(both, hidden):
    own = both.shape[0] - hidden
    count = 1
    for axis in ("chan", "dp"):
        size = lax.axis_size(axis)
        place = lax.axis_index(axis)
        lead = count
        bit = size // 2
        while bit:
            got = lax.ppermute(both, axis, [(i, i ^ bit) for i in range(size)])
            mine, theirs = (v[hidden:].reshape(lead, -1, own, LANES) for v in (both, got))
            upper = (place & bit) != 0
            rows = jnp.stack(
                [jnp.where(upper, theirs, mine), jnp.where(upper, mine, theirs)], axis=2
            )
            both = jnp.concatenate([both[:hidden] + got[:hidden], rows.reshape(-1, LANES)], axis=0)
            count *= 2
            bit //= 2
    return both


def finish_kernel(
    both_ref, embed_ref, bias_ref, hidden_ref, freq_ref,
    embed_grad, bias_grad, hidden_grad, frequency_grad, output_grad, decay_grad,
):
    hidden, features = hidden_ref.shape[0], embed_ref.shape[0]
    net = both_ref[:hidden]
    turned = net.T
    rows = both_ref[hidden:].T
    output_grad[...] = rows[:hidden]
    decay_grad[...] = rows[hidden : hidden + 1]
    table = turned[hidden:]
    embed = jnp.concatenate([table[features - 1 : features], table[: features - 1]], axis=0)
    bias = table[features : features + 1]
    embed_grad[...] = freq_ref[:1] * embed
    bias_grad[...] = freq_ref[:1] * bias
    hidden_grad[...] = column(freq_ref[1:2, :]) * net[:, :hidden]
    frequency_grad[:1] = (
        jnp.sum(embed_ref[...] * embed, axis=0, keepdims=True) + bias_ref[...] * bias
    )
    frequency_grad[1:2] = jnp.sum(hidden_ref[...].T * turned[:hidden], axis=0, keepdims=True)


def finish(both, embed_weight, embed_bias, hidden_weight, frequency, channels):
    hidden, features = embed_weight.shape
    shapes = ((features, hidden), (1, hidden), (hidden, hidden), (2, hidden), (hidden, channels), (1, channels))
    embed, bias, hid, freq, output, decay = pl.pallas_call(
        finish_kernel,
        out_shape=[jax.ShapeDtypeStruct(shape, F32) for shape in shapes],
        name="finish",
    )(both, embed_weight.T, embed_bias[None], hidden_weight, frequency)
    return embed.T, bias[0], hid, freq, output.T, decay[0]


def work(
    signal,
    signal_grad,
    embed_weight,
    embed_bias,
    hidden_weight,
    frequency,
    output_weight,
    decay_rate,
):
    seq_local, chan_local, length = signal.shape
    total = 2 * length
    dp, chan = lax.axis_size("dp"), lax.axis_size("chan")
    own = chan_local // dp
    count = dp * chan
    hidden = hidden_weight.shape[0]
    channels = chan * chan_local
    scale = 1.0 / math.sqrt(seq_local * dp * length)
    at_dp, at_chan = lax.axis_index("dp"), lax.axis_index("chan")

    chunks = 2 if own % 16 == 0 else 1
    per = own // chunks
    partners = sorted(range(1, dp), key=lambda p: -bin(p).count("1"))
    lags = None
    for q in range(chunks):
        sent = pick(signal, signal_grad, (*partners, 0), own, q * per, per)
        pieces = []
        for k, p in enumerate(partners):
            pieces.append(lax.ppermute(sent[k], "dp", [(i, i ^ p) for i in range(dp)]))
        lags = correlate([*pieces, sent[-1]], scale, count, lags, q, chunks)

    saved = network(embed_weight, embed_bias, hidden_weight, frequency, total)
    shared = lax.all_to_all(lags, ("dp", "chan"), 0, 0, tiled=True)
    first_own = at_chan * chan_local + at_dp * own
    both = backward(
        first_own, lags, saved, decay_rate, output_weight, hidden_weight, frequency, total
    )
    both = share(both, hidden)
    filter_grad = jnp.swapaxes(shared.reshape(dp, chan, own, -1), 0, 1).reshape(channels, -1)
    return (
        filter_grad,
        *finish(both, embed_weight, embed_bias, hidden_weight, frequency, channels),
    )


def solution(mesh):
    placed = (P("dp", "chan", None), P("dp", "chan", None), P(), P(), P(), P(), P(), P())
    return jax.shard_map(
        work,
        mesh=mesh,
        in_specs=placed,
        out_specs=(P(None, ("dp", "chan")), P(), P(), P(), P(), P(), P()),
        check_vma=False,
    )
```

```python
import functools
import math

import jax
import jax.numpy as jnp
import numpy as np
from jax import lax
from jax.experimental import pallas as pl
from jax.experimental.pallas import tpu as pltpu
from jax.sharding import PartitionSpec as P


LANES = 128
F32 = jnp.float32
BF16 = jnp.bfloat16


def split(values):
    high = values.astype(BF16)
    return high, (values - high.astype(F32)).astype(BF16)


def split_table(values):
    high = values.astype(BF16)
    return high, (values - high.astype(np.float64)).astype(BF16)


def tables(rows, scale):
    total = 2 * rows * LANES
    odd = 2 * np.arange(rows) + 1
    angle = np.pi * (odd[:, None] * np.arange(2 * rows)[None, :] % (4 * rows)) / (2 * rows)
    first = np.concatenate([np.cos(angle[:, :rows]), -np.sin(angle[:, :rows])], axis=0)
    first = np.concatenate(split_table(first), axis=1)
    turn = np.pi * (odd[:, None] * np.arange(LANES)[None, :]) / total
    twist = np.stack([np.cos(turn), -np.sin(turn)]).astype(np.float32)
    untwist = (np.stack([np.cos(turn), np.sin(turn)]) * scale).astype(np.float32)
    fine = 2 * np.pi * (np.arange(LANES)[:, None] * np.arange(LANES)[None, :] % LANES) / LANES
    cosine, sine = np.cos(fine), np.sin(fine)
    second = np.block([[cosine, -sine], [sine, cosine]])
    sign = np.where(np.arange(2 * rows) < rows, 1.0, -1.0)[:, None]
    last = np.concatenate([np.cos(angle).T, -np.sin(angle).T], axis=1) * sign
    last_high, last_low = split_table(last)
    last = np.concatenate([last_high, last_low, last_high], axis=1)
    second, back = (
        np.concatenate([high, high, low], axis=0)
        for high, low in (split_table(second), split_table(second.T))
    )
    return first, twist, untwist, second, back, last


def dot(a, b):
    return jnp.dot(a, b, preferred_element_type=F32)


def stacked(values, axis):
    high, low = split(values)
    return jnp.concatenate([high, low], axis=axis)


def narrow(values, axis):
    high, low = split(values)
    return jnp.concatenate([high, low, high], axis=axis)


def wide(values, axis):
    high, low = split(values)
    return jnp.concatenate([high, high, low], axis=axis)


def dot_lanes(a, b):
    return lax.dot_general(a, b, (((1,), (1,)), ((), ())), preferred_element_type=F32)


def sine_cosine(angle):
    turns = (angle * (1.0 / math.pi) + 12582912.0) - 12582912.0
    rest = (angle - turns * 3.140625) - turns * 9.67653589793e-4
    sign = jnp.where((turns.astype(jnp.int32) & 1) != 0, -1.0, 1.0)
    square = rest * rest
    rest = rest * sign
    sine = (2.6000244184306192e-6 * square - 1.9806601562034863e-4) * square + 8.333017104043598e-3
    sine = (sine * square - 0.1666665708890745) * square * rest + rest
    cosine = (-2.6076816602017467e-7 * square + 2.4761870623092258e-5) * square
    cosine = ((cosine - 1.3888403220356624e-3) * square + 4.1666640707487275e-2) * square
    cosine = (cosine - 0.49999999549109586) * square + 1.0
    return sine, cosine * sign


def column(row):
    size = row.shape[1]
    at = [lax.broadcasted_iota(jnp.int32, (size, size), d) for d in (0, 1)]
    return jnp.sum(jnp.where(at[0] == at[1], row, 0.0), axis=1, keepdims=True)


def pick_kernel(x_ref, g_ref, *refs, partners, own, start, after):
    refs = refs[after:]
    outs, (held_ref, in_sem, out_sem) = refs[: len(partners)], refs[len(partners) :]
    per = outs[0].shape[2]
    arrivals, departures = [], []
    for k, partner in enumerate(partners):
        first = pl.multiple_of((lax.axis_index("dp") ^ partner) * own + start, per)
        for at, ref in enumerate((x_ref, g_ref)):
            arrivals.append(
                pltpu.make_async_copy(
                    ref.at[:, pl.ds(first, per), :], held_ref.at[k, at], in_sem.at[k, at]
                )
            )
            arrivals[-1].start()
    for k in range(len(partners)):
        arrivals[2 * k].wait()
        arrivals[2 * k + 1].wait()
        departures.append(pltpu.make_async_copy(held_ref.at[k], outs[k], out_sem.at[k]))
        departures[-1].start()
    for departure in departures:
        departure.wait()


def pick(x, g, partners, own, start, count, after=()):
    seqs, _, length = x.shape
    shape = (2, seqs, count, length)
    if count % 8:
        firsts = [(lax.axis_index("dp") ^ p) * own + start for p in partners]
        return [
            jnp.stack([lax.dynamic_slice_in_dim(v, first, count, 1) for v in (x, g)])
            for first in firsts
        ]
    anywhere = pl.BlockSpec(memory_space=pl.ANY)
    return pl.pallas_call(
        functools.partial(
            pick_kernel, partners=partners, own=own, start=start, after=len(after)
        ),
        in_specs=[anywhere] * (2 + len(after)),
        out_specs=[anywhere] * len(partners),
        out_shape=[jax.ShapeDtypeStruct(shape, BF16)] * len(partners),
        scratch_shapes=[
            pltpu.VMEM((len(partners), *shape), BF16),
            pltpu.SemaphoreType.DMA((len(partners), 2)),
            pltpu.SemaphoreType.DMA((len(partners),)),
        ],
        cost_estimate=pl.CostEstimate(
            flops=0, bytes_accessed=4 * len(partners) * math.prod(shape), transcendentals=0
        ),
        name="pick",
    )(x, g, *after)


def correlate_kernel(*refs, pieces, held, last):
    piece_refs, refs = refs[:pieces], refs[pieces:]
    held_ref, refs = (refs[0], refs[1:]) if held else (None, refs)
    first_ref, twist_ref, second_ref = refs[:3]
    if last:
        untwist_ref, back_ref, last_ref, out_ref, lag_ref, cross_ref = refs[3:9]
    else:
        out_ref = refs[3]
    turn_ref, high_ref, low_ref, spec_ref = refs[-4:]
    _, seqs_each, channels, length = piece_refs[0].shape
    rows = length // LANES
    seqs = pieces * seqs_each
    step = pl.program_id(0)
    each = high_ref.shape[0] // (2 * seqs * rows)

    @pl.when(step == 0)
    def _():
        for s in range(seqs):
            for at in range(2):
                for row in range(rows):
                    turn_ref[at * seqs + s, pl.ds(row * channels, channels), :] = piece_refs[
                        s // seqs_each
                    ][at, s % seqs_each, :, pl.ds(row * LANES, LANES)].astype(F32)

    cosine = jnp.concatenate([twist_ref[0]] * 2, axis=1)
    sine = jnp.concatenate([twist_ref[1]] * 2, axis=1)
    first = first_ref[...]

    def line(at, s, k):
        return pl.ds(((k * 2 + at) * seqs + s) * rows, rows)

    for k in range(each):
        for s in range(seqs):
            pair = jnp.concatenate(
                [
                    turn_ref[
                        at * seqs + s, pl.ds(step * each + k, rows, stride=channels), :
                    ].astype(BF16)
                    for at in range(2)
                ],
                axis=1,
            )
            both = dot(first, jnp.concatenate([pair, pair], axis=0))
            real, imag = both[:rows], both[rows:]
            real, imag = real * cosine - imag * sine, real * sine + imag * cosine
            for at, part in ((0, slice(0, LANES)), (1, slice(LANES, 2 * LANES))):
                row = jnp.concatenate([real[:, part], imag[:, part]], axis=1)
                high_ref[line(at, s, k), :], low_ref[line(at, s, k), :] = split(row)
    spec_ref[...] = dot(
        jnp.concatenate([high_ref[...], low_ref[...], high_ref[...]], axis=1), second_ref[...]
    )
    for k in range(each):
        if held:
            real, imag = held_ref[k, :, :LANES], held_ref[k, :, LANES:]
        else:
            real = imag = jnp.zeros((rows, LANES), F32)
        for s in range(seqs):
            a, b = spec_ref[line(0, s, k), :], spec_ref[line(1, s, k), :]
            a_real, a_imag, b_real, b_imag = a[:, :LANES], a[:, LANES:], b[:, :LANES], b[:, LANES:]
            real = real + (a_real * b_real + a_imag * b_imag)
            imag = imag + (a_real * b_imag - a_imag * b_real)
        if last:
            cross_line = pl.ds(pl.multiple_of((step * each + k) * rows, rows), rows)
            cross_ref[cross_line, :LANES] = real
            cross_ref[cross_line, LANES:] = imag
        else:
            out_ref[k, :, :LANES] = real
            out_ref[k, :, LANES:] = imag
    if not last:
        return

    @pl.when(step == pl.num_programs(0) - 1)
    def _():
        owners, channels, lag_count = out_ref.shape
        back_cos, back_sin = untwist_ref[0], untwist_ref[1]
        group = math.gcd(channels, 4)
        for start in range(0, channels, group):
            high, low = split(cross_ref[pl.ds(start * rows, group * rows), :])
            back = dot(jnp.concatenate([high, low, high], axis=1), back_ref[...])
            for c in range(0, group, 2):
                turned = []
                for k in range(c, c + 2):
                    real = back[k * rows : (k + 1) * rows, :LANES]
                    imag = back[k * rows : (k + 1) * rows, LANES:]
                    turned.append(
                        jnp.concatenate(
                            [real * back_cos - imag * back_sin, real * back_sin + imag * back_cos],
                            axis=0,
                        )
                    )
                lags = dot(last_ref[...], wide(jnp.concatenate(turned, axis=1), 0))
                for k in range(2):
                    lag_ref[pl.ds((start + c + k) * 2 * rows, 2 * rows), :] = lags[
                        :, k * LANES : (k + 1) * LANES
                    ]
        wide_rows = lag_count // LANES
        for owner in range(owners):
            for k in range(wide_rows):
                out_ref[owner, :, pl.ds(k * LANES, LANES)] = lag_ref[
                    pl.ds(owner * wide_rows + k, channels, stride=2 * rows), :
                ]


def correlate(pieces, held, scale, owners):
    _, seqs_each, channels, length = pieces[0].shape
    lanes, rows = LANES, length // LANES
    seqs = seqs_each * len(pieces)
    total = 2 * length
    each = max(1, min(channels, 8 // seqs))
    first, twist, untwist, second, back, last = (
        jnp.asarray(t) for t in tables(rows, 2.0 * scale / total)
    )
    consts = [first, twist, second] + ([untwist, back, last] if owners else [])
    spectrum = pl.BlockSpec((each, rows, 2 * lanes), lambda c: (c, 0, 0))
    held = [] if held is None else [held]
    block = pl.BlockSpec(pieces[0].shape, lambda c: (0, 0, 0, 0))
    whole = [
        pl.BlockSpec(t.shape, functools.partial(lambda n, c: (0,) * n, t.ndim)) for t in consts
    ]
    if owners:
        shape = (owners, channels, total // owners)
        out_spec = pl.BlockSpec(shape, lambda c: (0, 0, 0))
    else:
        shape = (channels, rows, 2 * lanes)
        out_spec = spectrum
    scratch = []
    if owners:
        scratch = [
            pltpu.VMEM((channels * 2 * rows, lanes), F32),
            pltpu.VMEM((channels * rows, 2 * lanes), F32),
        ]
    scratch += [
        pltpu.VMEM((2 * seqs, rows * channels, lanes), F32),
        pltpu.VMEM((each * 2 * seqs * rows, 2 * lanes), BF16),
        pltpu.VMEM((each * 2 * seqs * rows, 2 * lanes), BF16),
        pltpu.VMEM((each * 2 * seqs * rows, 2 * lanes), F32),
    ]
    return pl.pallas_call(
        functools.partial(
            correlate_kernel, pieces=len(pieces), held=len(held), last=bool(owners)
        ),
        grid=(channels // each,),
        in_specs=[block] * len(pieces) + [spectrum] * len(held) + whole,
        out_specs=out_spec,
        out_shape=jax.ShapeDtypeStruct(shape, F32),
        scratch_shapes=scratch,
        cost_estimate=pl.CostEstimate(
            flops=channels * seqs * 2 * rows * lanes * lanes * 36,
            bytes_accessed=channels * (seqs * rows * lanes * 4 + total * 4),
            transcendentals=0,
        ),
        compiler_params=pltpu.CompilerParams(vmem_limit_bytes=24 * 2**20),
        name="correlate",
    )(*pieces, *held, *consts)


STEP = 2048
BANDS_PAD = 8


def lag_row(step, total):
    position = step * STEP + lax.broadcasted_iota(jnp.int32, (1, STEP), 1)
    return jnp.where(position < total // 2, position, position - total)


def network_kernel(
    factor_ref, embed_ref, bias_ref, hidden_ref, freq_ref,
    table_ref, first_ref, second_ref, cos1_ref, cos2_ref,
    embed_parts, hidden_parts, freq_cols, *, total,
):
    hidden = hidden_ref.shape[0]
    step = pl.program_id(0)

    @pl.when(step == 0)
    def _():
        embed = jnp.concatenate(
            [
                embed_ref[1:],
                embed_ref[:1],
                bias_ref[...],
                jnp.zeros((BANDS_PAD - 2, hidden), F32),
            ],
            axis=0,
        )
        embed_parts[...] = narrow(embed.T, 1)
        hidden_parts[...] = narrow(hidden_ref[...], 1)
        for k in range(2):
            freq_cols[k] = column(freq_ref[k : k + 1, :])

    lag = lag_row(step, total)
    length = total // 2
    phase = ((factor_ref[...] * lag) & (total - 1)).astype(F32) * (2.0 * math.pi / total)
    sine, cosine = sine_cosine(phase)
    scaled = lag.astype(F32) / length
    row = lax.broadcasted_iota(jnp.int32, (BANDS_PAD, STEP), 0)
    extra = jnp.where(row == 0, scaled, jnp.where(row == 1, 1.0, 0.0))
    table = jnp.concatenate([sine, cosine, extra], axis=0)
    table_ref[...] = stacked(table, 0)
    first, cos1 = sine_cosine(freq_cols[0] * dot(embed_parts[...], wide(table, 0)))
    first_ref[...] = stacked(first, 0)
    cos1_ref[...] = cos1
    second, cos2 = sine_cosine(freq_cols[1] * dot(hidden_parts[...], wide(first, 0)))
    second_ref[...] = stacked(second, 0)
    cos2_ref[...] = cos2


def network(embed_weight, embed_bias, hidden_weight, frequency, total):
    hidden, features = embed_weight.shape
    bands = (features - 1) // 2
    factors = np.array(
        [[max(1, int(0.45 * total * 10000.0 ** (-band / bands)))] for band in range(bands)], np.int32
    )
    args = (jnp.asarray(factors), embed_weight.T, embed_bias[None], hidden_weight, frequency)
    whole = [pl.BlockSpec(a.shape, lambda i: (0, 0)) for a in args]
    depth = 2 * bands + BANDS_PAD
    heights = ((2 * depth, BF16), (2 * hidden, BF16), (2 * hidden, BF16), (hidden, F32), (hidden, F32))
    return pl.pallas_call(
        functools.partial(network_kernel, total=total),
        grid=(total // STEP,),
        in_specs=whole,
        out_specs=[pl.BlockSpec((h, STEP), lambda i: (0, i)) for h, _ in heights],
        out_shape=[jax.ShapeDtypeStruct((h, total), t) for h, t in heights],
        scratch_shapes=[
            pltpu.VMEM((hidden, 3 * depth), BF16),
            pltpu.VMEM((hidden, 3 * hidden), BF16),
            pltpu.VMEM((2, hidden, 1), F32),
        ],
        cost_estimate=pl.CostEstimate(
            flops=total * hidden * 600, bytes_accessed=total * hidden * 20, transcendentals=0
        ),
        name="network",
    )(*args)


def backward_kernel(
    first_ref, lags_ref, table_ref, layer1_ref, layer2_ref, cos1_ref, cos2_ref,
    decay_ref, output_ref, hidden_ref, freq_ref,
    out_ref, output_parts, hidden_parts, decay_col, own_ref, sum1_ref, sum3_ref, sum5_ref, *, total, pack,
):
    step = pl.program_id(0)
    owners, own, _ = lags_ref.shape
    hidden = hidden_ref.shape[0]

    @pl.when(step == 0)
    def _():
        for ref in (sum1_ref, sum3_ref, sum5_ref):
            ref[...] = jnp.zeros_like(ref)
        channels = output_ref.shape[1]
        own_ref[...] = pltpu.roll(output_ref[...], channels - first_ref[0], 1)[:, :own]
        output_parts[...] = narrow(own_ref[...], 1)
        hidden_parts[...] = narrow((hidden_ref[...] * column(freq_ref[1:2, :])).T, 1)
        place = [lax.broadcasted_iota(jnp.int32, (own, channels), d) for d in (0, 1)]
        decay_col[...] = jnp.sum(
            jnp.where(place[1] == place[0] + first_ref[0], decay_ref[...], 0.0), axis=1, keepdims=True
        )

    lags = jnp.concatenate([lags_ref[k] for k in range(owners)], axis=1)
    length = total // 2
    distance = jnp.abs(lag_row(step, total)).astype(F32)
    window = jnp.exp(-decay_col[...] * distance / length)
    shaped = lags * window * (1.0 / math.sqrt(total))
    far = shaped * (distance / length)
    sum1_ref[...] += dot_lanes(stacked(jnp.concatenate([shaped, far], axis=0), 0), layer2_ref[...])
    second = dot(output_parts[...], wide(shaped, 0)) * cos2_ref[...]
    high, low = split(second)
    sum3_ref[...] += dot_lanes(jnp.concatenate([high, low], axis=0), layer1_ref[...])
    first = dot(hidden_parts[...], jnp.concatenate([high, high, low], axis=0)) * cos1_ref[...]
    sum5_ref[...] += dot_lanes(stacked(first, 0), table_ref[...])

    @pl.when(step == pl.num_programs(0) - 1)
    def _():
        def joined(ref):
            rows, cols = ref.shape[0] // 2, ref.shape[1] // 2
            return ref[:rows, :cols] + ref[:rows, cols:] + ref[rows:, :cols]

        net = jnp.concatenate([joined(sum3_ref), joined(sum5_ref)], axis=1)
        out_ref[:hidden] = jnp.concatenate(
            [net, jnp.zeros((hidden, LANES - net.shape[1]), F32)], axis=1
        )
        sums = joined(sum1_ref)
        decay_grad = -jnp.sum(own_ref[...].T * sums[own:], axis=1, keepdims=True)
        height = out_ref.shape[0] - hidden - own // pack
        place = lax.broadcasted_iota(jnp.int32, (height, LANES), 0) * LANES
        place = place + lax.broadcasted_iota(jnp.int32, (height, LANES), 1) - first_ref[0]
        decays = jnp.zeros((height, LANES), F32)
        for c in range(own):
            decays = jnp.where(place == c, decay_grad[c : c + 1], decays)
        out_ref[pl.ds(hidden, height), :] = decays
        per = own // pack
        parts = [sums[k * per : (k + 1) * per] for k in range(pack)]
        parts += [jnp.zeros((per, LANES - pack * hidden), F32)] if pack * hidden < LANES else []
        out_ref[hidden + height :] = jnp.concatenate(parts, axis=1)


def packing(own, hidden):
    return 2 if own % 16 == 0 and 2 * hidden <= LANES else 1


def summed_rows(hidden, channels):
    return hidden + -(-channels // (8 * LANES)) * 8


def backward(first_own, lags, saved, decay_rate, output_weight, hidden_weight, frequency, total):
    _, own, lag_count = lags.shape
    hidden = hidden_weight.shape[0]
    pack = packing(own, hidden)
    height = summed_rows(hidden, decay_rate.shape[0]) + own // pack
    args = (decay_rate[None], output_weight.T, hidden_weight, frequency)
    specs = [pl.BlockSpec((STEP // lag_count, own, lag_count), lambda i, first: (i, 0, 0))]
    specs += [pl.BlockSpec((a.shape[0], STEP), lambda i, first: (0, i)) for a in saved]
    specs += [pl.BlockSpec(a.shape, lambda i, first: (0, 0)) for a in args]
    return pl.pallas_call(
        functools.partial(backward_kernel, total=total, pack=pack),
        grid_spec=pltpu.PrefetchScalarGridSpec(
            num_scalar_prefetch=1,
            grid=(total // STEP,),
            in_specs=specs,
            out_specs=pl.BlockSpec((height, LANES), lambda i, first: (0, 0)),
            scratch_shapes=[
                pltpu.VMEM((hidden, 3 * own), BF16),
                pltpu.VMEM((hidden, 3 * hidden), BF16),
                pltpu.VMEM((own, 1), F32),
                pltpu.VMEM((hidden, own), F32),
                pltpu.VMEM((4 * own, 2 * hidden), F32),
                pltpu.VMEM((2 * hidden, 2 * hidden), F32),
                pltpu.VMEM((2 * hidden, saved[0].shape[0]), F32),
            ],
        ),
        out_shape=jax.ShapeDtypeStruct((height, LANES), F32),
        cost_estimate=pl.CostEstimate(
            flops=total * hidden * 2000, bytes_accessed=total * hidden * 20, transcendentals=0
        ),
        name="backward",
    )(first_own.reshape(1), lags, *saved, *args)


def rounds():
    sizes = ((axis, lax.axis_size(axis)) for axis in ("dp", "chan"))
    return [(axis, 1 << b) for axis, size in sizes for b in reversed(range(size.bit_length() - 1))]


def share(both, summed):
    for axis, bit in rounds():
        size = lax.axis_size(axis)
        got = lax.ppermute(both, axis, [(i, i ^ bit) for i in range(size)])
        last = both, got
        both = jnp.concatenate([both[:summed] + got[:summed], both[summed:], got[summed:]], axis=0)
    return last


def finish_kernel(
    both_ref, got_ref, embed_ref, bias_ref, hidden_ref, freq_ref,
    embed_grad, bias_grad, hidden_grad, frequency_grad, output_grad, decay_grad, rows_ref, *, own, pack,
):
    hidden, features = hidden_ref.shape[0], embed_ref.shape[0]
    summed = summed_rows(hidden, output_grad.shape[1])
    total = both_ref[:summed] + got_ref[:summed]
    net = total[:hidden]
    turned = net.T
    decay_grad[...] = total[hidden : hidden + decay_grad.shape[0]]
    unit = own // pack
    count = output_grad.shape[1] // own
    here = {axis: lax.axis_index(axis) for axis in ("dp", "chan")}
    steps = rounds()
    for k in range(count):
        there = dict(here)
        for n, (axis, bit) in enumerate(steps):
            if k >> n & 1:
                there[axis] = there[axis] ^ bit
        place = there["chan"] * lax.axis_size("dp") + there["dp"]
        ref, at = (both_ref, k) if k < count // 2 else (got_ref, k - count // 2)
        for n in range(pack):
            rows_ref[pl.ds(pl.multiple_of(place * own + n * unit, unit), unit), :] = ref[
                pl.ds(summed + at * unit, unit), n * hidden : (n + 1) * hidden
            ]
    output_grad[...] = rows_ref[...].T
    table = turned[hidden:]
    embed = jnp.concatenate([table[features - 1 : features], table[: features - 1]], axis=0)
    bias = table[features : features + 1]
    embed_grad[...] = freq_ref[:1] * embed
    bias_grad[...] = freq_ref[:1] * bias
    hidden_grad[...] = column(freq_ref[1:2, :]) * net[:, :hidden]
    frequency_grad[:1] = (
        jnp.sum(embed_ref[...] * embed, axis=0, keepdims=True) + bias_ref[...] * bias
    )
    frequency_grad[1:2] = jnp.sum(hidden_ref[...].T * turned[:hidden], axis=0, keepdims=True)


def finish(both, got, embed_weight, embed_bias, hidden_weight, frequency, channels, own):
    hidden, features = embed_weight.shape
    shapes = (
        (features, hidden), (1, hidden), (hidden, hidden), (2, hidden), (hidden, channels),
        (-(-channels // LANES), LANES),
    )
    embed, bias, hid, freq, output, decay = pl.pallas_call(
        functools.partial(finish_kernel, own=own, pack=packing(own, hidden)),
        out_shape=[jax.ShapeDtypeStruct(shape, F32) for shape in shapes],
        scratch_shapes=[pltpu.VMEM((channels, hidden), F32)],
        compiler_params=pltpu.CompilerParams(vmem_limit_bytes=8 * 2**20),
        name="finish",
    )(both, got, embed_weight.T, embed_bias[None], hidden_weight, frequency)
    return embed.T, bias[0], hid, freq, output.T, decay.reshape(-1)[:channels]


def work(
    signal,
    signal_grad,
    embed_weight,
    embed_bias,
    hidden_weight,
    frequency,
    output_weight,
    decay_rate,
):
    seq_local, chan_local, length = signal.shape
    total = 2 * length
    dp, chan = lax.axis_size("dp"), lax.axis_size("chan")
    own = chan_local // dp
    count = dp * chan
    hidden = hidden_weight.shape[0]
    channels = chan * chan_local
    scale = 1.0 / math.sqrt(seq_local * dp * length)
    at_dp, at_chan = lax.axis_index("dp"), lax.axis_index("chan")

    partners = sorted(
        range(1, dp), key=lambda p: (p != 1, -bin(p >> 1).count("1"), p & 1, p)
    )
    pieces = [None] * dp
    made = []
    for some in (tuple(partners[1:3]), (partners[0], *partners[3:], 0)):
        made = pick(signal, signal_grad, some, own, 0, own, made[:1])
        for p, sent in zip(some, made):
            pieces[p] = lax.ppermute(sent, "dp", [(i, i ^ p) for i in range(dp)]) if p else sent
    order = [0, *partners]
    spectrum = None
    cuts = (*range(0, dp, max(2, dp // 4)), dp)
    for q in range(len(cuts) - 1):
        some = [pieces[p] for p in order[cuts[q] : cuts[q + 1]]]
        spectrum = correlate(some, spectrum, scale, count if q == len(cuts) - 2 else 0)
    lags = spectrum

    saved = network(embed_weight, embed_bias, hidden_weight, frequency, total)
    shared = lax.all_to_all(lags, ("dp", "chan"), 0, 0, tiled=True)
    first_own = at_chan * chan_local + at_dp * own
    both = backward(
        first_own, lags, saved, decay_rate, output_weight, hidden_weight, frequency, total
    )
    both, got = share(both, summed_rows(hidden, channels))
    filter_grad = jnp.swapaxes(shared.reshape(dp, chan, own, -1), 0, 1)
    filter_grad = filter_grad.reshape(channels, -1)
    return (
        filter_grad,
        *finish(both, got, embed_weight, embed_bias, hidden_weight, frequency, channels, own),
    )


def solution(mesh):
    placed = (P("dp", "chan", None), P("dp", "chan", None), P(), P(), P(), P(), P(), P())
    return jax.shard_map(
        work,
        mesh=mesh,
        in_specs=placed,
        out_specs=(P(None, ("dp", "chan")), P(), P(), P(), P(), P(), P()),
        check_vma=False,
    )
```

```python
import functools
import math

import jax
import jax.numpy as jnp
import numpy as np
from jax import lax
from jax.experimental import pallas as pl
from jax.experimental.pallas import tpu as pltpu
from jax.sharding import PartitionSpec as P


LANES = 128
F32 = jnp.float32
BF16 = jnp.bfloat16


def split(values):
    high = values.astype(BF16)
    return high, (values - high.astype(F32)).astype(BF16)


def split_table(values):
    high = values.astype(BF16)
    return high, (values - high.astype(np.float64)).astype(BF16)


def tables(rows, scale):
    total = 2 * rows * LANES
    odd = 2 * np.arange(rows) + 1
    angle = np.pi * (odd[:, None] * np.arange(2 * rows)[None, :] % (4 * rows)) / (2 * rows)
    first = np.concatenate([np.cos(angle[:, :rows]), -np.sin(angle[:, :rows])], axis=0)
    first = np.concatenate(split_table(first), axis=1)
    turn = np.pi * (odd[:, None] * np.arange(LANES)[None, :]) / total
    twist = np.stack([np.cos(turn), -np.sin(turn)]).astype(np.float32)
    untwist = (np.stack([np.cos(turn), np.sin(turn)]) * scale).astype(np.float32)
    fine = 2 * np.pi * (np.arange(LANES)[:, None] * np.arange(LANES)[None, :] % LANES) / LANES
    cosine, sine = np.cos(fine), np.sin(fine)
    second = np.block([[cosine, -sine], [sine, cosine]])
    sign = np.where(np.arange(2 * rows) < rows, 1.0, -1.0)[:, None]
    last = np.concatenate([np.cos(angle).T, -np.sin(angle).T], axis=1) * sign
    last_high, last_low = split_table(last)
    last = np.concatenate([last_high, last_low, last_high], axis=1)
    second, back = (
        np.concatenate([high, high, low], axis=0)
        for high, low in (split_table(second), split_table(second.T))
    )
    return first, twist, untwist, second, back, last


def dot(a, b):
    return jnp.dot(a, b, preferred_element_type=F32)


def stacked(values, axis):
    high, low = split(values)
    return jnp.concatenate([high, low], axis=axis)


def narrow(values, axis):
    high, low = split(values)
    return jnp.concatenate([high, low, high], axis=axis)


def wide(values, axis):
    high, low = split(values)
    return jnp.concatenate([high, high, low], axis=axis)


def dot_lanes(a, b):
    return lax.dot_general(a, b, (((1,), (1,)), ((), ())), preferred_element_type=F32)


def sine_cosine(angle):
    turns = (angle * (1.0 / math.pi) + 12582912.0) - 12582912.0
    rest = (angle - turns * 3.140625) - turns * 9.67653589793e-4
    sign = jnp.where((turns.astype(jnp.int32) & 1) != 0, -1.0, 1.0)
    square = rest * rest
    rest = rest * sign
    sine = (2.6000244184306192e-6 * square - 1.9806601562034863e-4) * square + 8.333017104043598e-3
    sine = (sine * square - 0.1666665708890745) * square * rest + rest
    cosine = (-2.6076816602017467e-7 * square + 2.4761870623092258e-5) * square
    cosine = ((cosine - 1.3888403220356624e-3) * square + 4.1666640707487275e-2) * square
    cosine = (cosine - 0.49999999549109586) * square + 1.0
    return sine, cosine * sign


def column(row):
    size = row.shape[1]
    at = [lax.broadcasted_iota(jnp.int32, (size, size), d) for d in (0, 1)]
    return jnp.sum(jnp.where(at[0] == at[1], row, 0.0), axis=1, keepdims=True)


def pick_kernel(x_ref, g_ref, *refs, items, own, after):
    refs = refs[after:]
    outs, held = refs[: len(items)], refs[len(items) : 2 * len(items)]
    in_sem, out_sem = refs[2 * len(items) :]
    arrivals, departures = [], []
    for k, (partner, start, count) in enumerate(items):
        first = pl.multiple_of((lax.axis_index("dp") ^ partner) * own + start, count)
        for at, ref in enumerate((x_ref, g_ref)):
            arrivals.append(
                pltpu.make_async_copy(
                    ref.at[:, pl.ds(first, count), :], held[k].at[at], in_sem.at[k, at]
                )
            )
            arrivals[-1].start()
    for k in range(len(items)):
        arrivals[2 * k].wait()
        arrivals[2 * k + 1].wait()
        departures.append(pltpu.make_async_copy(held[k], outs[k], out_sem.at[k]))
        departures[-1].start()
    for departure in departures:
        departure.wait()


def pick(x, g, items, own, after=()):
    seqs, _, length = x.shape
    if own % 8:
        return [
            jnp.stack(
                [
                    lax.dynamic_slice_in_dim(
                        v, (lax.axis_index("dp") ^ partner) * own + start, count, 1
                    )
                    for v in (x, g)
                ]
            )
            for partner, start, count in items
        ]
    shapes = [(2, seqs, count, length) for _, _, count in items]
    anywhere = pl.BlockSpec(memory_space=pl.ANY)
    return pl.pallas_call(
        functools.partial(pick_kernel, items=items, own=own, after=len(after)),
        in_specs=[anywhere] * (2 + len(after)),
        out_specs=[anywhere] * len(items),
        out_shape=[jax.ShapeDtypeStruct(shape, BF16) for shape in shapes],
        scratch_shapes=[
            *[pltpu.VMEM(shape, BF16) for shape in shapes],
            pltpu.SemaphoreType.DMA((len(items), 2)),
            pltpu.SemaphoreType.DMA((len(items),)),
        ],
        cost_estimate=pl.CostEstimate(
            flops=0, bytes_accessed=4 * sum(math.prod(shape) for shape in shapes), transcendentals=0
        ),
        name="pick",
    )(x, g, *after)


def correlate_kernel(*refs, pieces, held, lags, last):
    piece_refs, refs = refs[:pieces], refs[pieces:]
    held_ref, refs = (refs[0], refs[1:]) if held else (None, refs)
    refs = refs[lags:]
    first_ref, twist_ref, second_ref = refs[:3]
    if last:
        untwist_ref, back_ref, last_ref, out_ref, lag_ref, cross_ref = refs[3:9]
    else:
        out_ref = refs[3]
    turn_ref, high_ref, low_ref, spec_ref = refs[-4:]
    _, seqs_each, channels, length = piece_refs[0].shape
    rows = length // LANES
    seqs = pieces * seqs_each
    step = pl.program_id(0)
    each = high_ref.shape[0] // (2 * seqs * rows)

    @pl.when(step == 0)
    def _():
        for s in range(seqs):
            for at in range(2):
                for row in range(rows):
                    turn_ref[at * seqs + s, pl.ds(row * channels, channels), :] = piece_refs[
                        s // seqs_each
                    ][at, s % seqs_each, :, pl.ds(row * LANES, LANES)].astype(F32)

    cosine = jnp.concatenate([twist_ref[0]] * 2, axis=1)
    sine = jnp.concatenate([twist_ref[1]] * 2, axis=1)
    first = first_ref[...]

    def line(at, s, k):
        return pl.ds(((k * 2 + at) * seqs + s) * rows, rows)

    for k in range(each):
        for s in range(seqs):
            pair = jnp.concatenate(
                [
                    turn_ref[
                        at * seqs + s, pl.ds(step * each + k, rows, stride=channels), :
                    ].astype(BF16)
                    for at in range(2)
                ],
                axis=1,
            )
            both = dot(first, jnp.concatenate([pair, pair], axis=0))
            real, imag = both[:rows], both[rows:]
            real, imag = real * cosine - imag * sine, real * sine + imag * cosine
            for at, part in ((0, slice(0, LANES)), (1, slice(LANES, 2 * LANES))):
                row = jnp.concatenate([real[:, part], imag[:, part]], axis=1)
                high_ref[line(at, s, k), :], low_ref[line(at, s, k), :] = split(row)
    spec_ref[...] = dot(
        jnp.concatenate([high_ref[...], low_ref[...], high_ref[...]], axis=1), second_ref[...]
    )
    for k in range(each):
        if held:
            real, imag = held_ref[k, :, :LANES], held_ref[k, :, LANES:]
        else:
            real = imag = jnp.zeros((rows, LANES), F32)
        for s in range(seqs):
            a, b = spec_ref[line(0, s, k), :], spec_ref[line(1, s, k), :]
            a_real, a_imag, b_real, b_imag = a[:, :LANES], a[:, LANES:], b[:, :LANES], b[:, LANES:]
            real = real + (a_real * b_real + a_imag * b_imag)
            imag = imag + (a_real * b_imag - a_imag * b_real)
        if last:
            cross_line = pl.ds(pl.multiple_of((step * each + k) * rows, rows), rows)
            cross_ref[cross_line, :LANES] = real
            cross_ref[cross_line, LANES:] = imag
        else:
            out_ref[k, :, :LANES] = real
            out_ref[k, :, LANES:] = imag
    if not last:
        return

    @pl.when(step == pl.num_programs(0) - 1)
    def _():
        owners, channels, lag_count = out_ref.shape
        back_cos, back_sin = untwist_ref[0], untwist_ref[1]
        group = math.gcd(channels, 4)
        for start in range(0, channels, group):
            high, low = split(cross_ref[pl.ds(start * rows, group * rows), :])
            back = dot(jnp.concatenate([high, low, high], axis=1), back_ref[...])
            for c in range(0, group, 2):
                turned = []
                for k in range(c, c + 2):
                    real = back[k * rows : (k + 1) * rows, :LANES]
                    imag = back[k * rows : (k + 1) * rows, LANES:]
                    turned.append(
                        jnp.concatenate(
                            [real * back_cos - imag * back_sin, real * back_sin + imag * back_cos],
                            axis=0,
                        )
                    )
                lags = dot(last_ref[...], wide(jnp.concatenate(turned, axis=1), 0))
                for k in range(2):
                    lag_ref[pl.ds((start + c + k) * 2 * rows, 2 * rows), :] = lags[
                        :, k * LANES : (k + 1) * LANES
                    ]
        wide_rows = lag_count // LANES
        for owner in range(owners):
            for k in range(wide_rows):
                out_ref[owner, :, pl.ds(k * LANES, LANES)] = lag_ref[
                    pl.ds(owner * wide_rows + k, channels, stride=2 * rows), :
                ]


def correlate(pieces, held, scale, owners, lags=None, chunk=0, chunks=1):
    _, seqs_each, channels, length = pieces[0].shape
    lanes, rows = LANES, length // LANES
    seqs = seqs_each * len(pieces)
    total = 2 * length
    each = max(1, min(channels, 8 // seqs))
    first, twist, untwist, second, back, last = (
        jnp.asarray(t) for t in tables(rows, 2.0 * scale / total)
    )
    consts = [first, twist, second] + ([untwist, back, last] if owners else [])
    skip = chunk * (channels // each)
    spectrum = pl.BlockSpec((each, rows, 2 * lanes), lambda c: (c + skip, 0, 0))
    lags = [] if lags is None else [lags]
    held = [] if held is None else [held]
    block = pl.BlockSpec(pieces[0].shape, lambda c: (0, 0, 0, 0))
    whole = [
        pl.BlockSpec(t.shape, functools.partial(lambda n, c: (0,) * n, t.ndim)) for t in consts
    ]
    if owners:
        shape = (owners, channels * chunks, total // owners)
        out_spec = pl.BlockSpec((owners, channels, total // owners), lambda c: (0, chunk, 0))
    else:
        shape = (channels, rows, 2 * lanes)
        out_spec = spectrum
    scratch = []
    if owners:
        scratch = [
            pltpu.VMEM((channels * 2 * rows, lanes), F32),
            pltpu.VMEM((channels * rows, 2 * lanes), F32),
        ]
    scratch += [
        pltpu.VMEM((2 * seqs, rows * channels, lanes), F32),
        pltpu.VMEM((each * 2 * seqs * rows, 2 * lanes), BF16),
        pltpu.VMEM((each * 2 * seqs * rows, 2 * lanes), BF16),
        pltpu.VMEM((each * 2 * seqs * rows, 2 * lanes), F32),
    ]
    return pl.pallas_call(
        functools.partial(
            correlate_kernel,
            pieces=len(pieces),
            held=len(held),
            lags=len(lags),
            last=bool(owners),
        ),
        grid=(channels // each,),
        in_specs=[block] * len(pieces)
        + [spectrum] * len(held)
        + [pl.BlockSpec(memory_space=pl.ANY)] * len(lags)
        + whole,
        input_output_aliases={len(pieces) + len(held): 0} if lags else {},
        out_specs=out_spec,
        out_shape=jax.ShapeDtypeStruct(shape, F32),
        scratch_shapes=scratch,
        cost_estimate=pl.CostEstimate(
            flops=channels * seqs * 2 * rows * lanes * lanes * 36,
            bytes_accessed=channels * (seqs * rows * lanes * 4 + total * 4),
            transcendentals=0,
        ),
        compiler_params=pltpu.CompilerParams(vmem_limit_bytes=24 * 2**20),
        name="correlate",
    )(*pieces, *held, *lags, *consts)


STEP = 2048
BANDS_PAD = 8


def lag_row(step, total):
    position = step * STEP + lax.broadcasted_iota(jnp.int32, (1, STEP), 1)
    return jnp.where(position < total // 2, position, position - total)


def network_kernel(
    factor_ref, embed_ref, bias_ref, hidden_ref, freq_ref,
    table_ref, first_ref, second_ref, cos1_ref, cos2_ref,
    embed_parts, hidden_parts, freq_cols, *, total,
):
    hidden = hidden_ref.shape[0]
    step = pl.program_id(0)

    @pl.when(step == 0)
    def _():
        embed = jnp.concatenate(
            [
                embed_ref[1:],
                embed_ref[:1],
                bias_ref[...],
                jnp.zeros((BANDS_PAD - 2, hidden), F32),
            ],
            axis=0,
        )
        embed_parts[...] = narrow(embed.T, 1)
        hidden_parts[...] = narrow(hidden_ref[...], 1)
        for k in range(2):
            freq_cols[k] = column(freq_ref[k : k + 1, :])

    lag = lag_row(step, total)
    length = total // 2
    phase = ((factor_ref[...] * lag) & (total - 1)).astype(F32) * (2.0 * math.pi / total)
    sine, cosine = sine_cosine(phase)
    scaled = lag.astype(F32) / length
    row = lax.broadcasted_iota(jnp.int32, (BANDS_PAD, STEP), 0)
    extra = jnp.where(row == 0, scaled, jnp.where(row == 1, 1.0, 0.0))
    table = jnp.concatenate([sine, cosine, extra], axis=0)
    table_ref[...] = stacked(table, 0)
    first, cos1 = sine_cosine(freq_cols[0] * dot(embed_parts[...], wide(table, 0)))
    first_ref[...] = stacked(first, 0)
    cos1_ref[...] = cos1
    second, cos2 = sine_cosine(freq_cols[1] * dot(hidden_parts[...], wide(first, 0)))
    second_ref[...] = stacked(second, 0)
    cos2_ref[...] = cos2


def network(embed_weight, embed_bias, hidden_weight, frequency, total):
    hidden, features = embed_weight.shape
    bands = (features - 1) // 2
    factors = np.array(
        [[max(1, int(0.45 * total * 10000.0 ** (-band / bands)))] for band in range(bands)], np.int32
    )
    args = (jnp.asarray(factors), embed_weight.T, embed_bias[None], hidden_weight, frequency)
    whole = [pl.BlockSpec(a.shape, lambda i: (0, 0)) for a in args]
    depth = 2 * bands + BANDS_PAD
    heights = ((2 * depth, BF16), (2 * hidden, BF16), (2 * hidden, BF16), (hidden, F32), (hidden, F32))
    return pl.pallas_call(
        functools.partial(network_kernel, total=total),
        grid=(total // STEP,),
        in_specs=whole,
        out_specs=[pl.BlockSpec((h, STEP), lambda i: (0, i)) for h, _ in heights],
        out_shape=[jax.ShapeDtypeStruct((h, total), t) for h, t in heights],
        scratch_shapes=[
            pltpu.VMEM((hidden, 3 * depth), BF16),
            pltpu.VMEM((hidden, 3 * hidden), BF16),
            pltpu.VMEM((2, hidden, 1), F32),
        ],
        cost_estimate=pl.CostEstimate(
            flops=total * hidden * 600, bytes_accessed=total * hidden * 20, transcendentals=0
        ),
        name="network",
    )(*args)


def backward_kernel(
    first_ref, lags_ref, table_ref, layer1_ref, layer2_ref, cos1_ref, cos2_ref,
    decay_ref, output_ref, hidden_ref, freq_ref,
    out_ref, output_parts, hidden_parts, decay_col, own_ref, sum1_ref, sum3_ref, sum5_ref, *, total, pack,
):
    step = pl.program_id(0)
    owners, own, _ = lags_ref.shape
    hidden = hidden_ref.shape[0]

    @pl.when(step == 0)
    def _():
        for ref in (sum1_ref, sum3_ref, sum5_ref):
            ref[...] = jnp.zeros_like(ref)
        channels = output_ref.shape[1]
        own_ref[...] = pltpu.roll(output_ref[...], channels - first_ref[0], 1)[:, :own]
        output_parts[...] = narrow(own_ref[...], 1)
        hidden_parts[...] = narrow((hidden_ref[...] * column(freq_ref[1:2, :])).T, 1)
        place = [lax.broadcasted_iota(jnp.int32, (own, channels), d) for d in (0, 1)]
        decay_col[...] = jnp.sum(
            jnp.where(place[1] == place[0] + first_ref[0], decay_ref[...], 0.0), axis=1, keepdims=True
        )

    lags = jnp.concatenate([lags_ref[k] for k in range(owners)], axis=1)
    length = total // 2
    distance = jnp.abs(lag_row(step, total)).astype(F32)
    window = jnp.exp(-decay_col[...] * distance / length)
    shaped = lags * window * (1.0 / math.sqrt(total))
    far = shaped * (distance / length)
    sum1_ref[...] += dot_lanes(stacked(jnp.concatenate([shaped, far], axis=0), 0), layer2_ref[...])
    second = dot(output_parts[...], wide(shaped, 0)) * cos2_ref[...]
    high, low = split(second)
    sum3_ref[...] += dot_lanes(jnp.concatenate([high, low], axis=0), layer1_ref[...])
    first = dot(hidden_parts[...], jnp.concatenate([high, high, low], axis=0)) * cos1_ref[...]
    sum5_ref[...] += dot_lanes(stacked(first, 0), table_ref[...])

    @pl.when(step == pl.num_programs(0) - 1)
    def _():
        def joined(ref):
            rows, cols = ref.shape[0] // 2, ref.shape[1] // 2
            return ref[:rows, :cols] + ref[:rows, cols:] + ref[rows:, :cols]

        net = jnp.concatenate([joined(sum3_ref), joined(sum5_ref)], axis=1)
        out_ref[:hidden] = jnp.concatenate(
            [net, jnp.zeros((hidden, LANES - net.shape[1]), F32)], axis=1
        )
        sums = joined(sum1_ref)
        decay_grad = -jnp.sum(own_ref[...].T * sums[own:], axis=1, keepdims=True)
        height = out_ref.shape[0] - hidden - own // pack
        place = lax.broadcasted_iota(jnp.int32, (height, LANES), 0) * LANES
        place = place + lax.broadcasted_iota(jnp.int32, (height, LANES), 1) - first_ref[0]
        decays = jnp.zeros((height, LANES), F32)
        for c in range(own):
            decays = jnp.where(place == c, decay_grad[c : c + 1], decays)
        out_ref[pl.ds(hidden, height), :] = decays
        per = own // pack
        parts = [sums[k * per : (k + 1) * per] for k in range(pack)]
        parts += [jnp.zeros((per, LANES - pack * hidden), F32)] if pack * hidden < LANES else []
        out_ref[hidden + height :] = jnp.concatenate(parts, axis=1)


def packing(own, hidden):
    return 2 if own % 16 == 0 and 2 * hidden <= LANES else 1


def summed_rows(hidden, channels):
    return hidden + -(-channels // (8 * LANES)) * 8


def backward(first_own, lags, saved, decay_rate, output_weight, hidden_weight, frequency, total):
    _, own, lag_count = lags.shape
    hidden = hidden_weight.shape[0]
    pack = packing(own, hidden)
    height = summed_rows(hidden, decay_rate.shape[0]) + own // pack
    args = (decay_rate[None], output_weight.T, hidden_weight, frequency)
    specs = [pl.BlockSpec((STEP // lag_count, own, lag_count), lambda i, first: (i, 0, 0))]
    specs += [pl.BlockSpec((a.shape[0], STEP), lambda i, first: (0, i)) for a in saved]
    specs += [pl.BlockSpec(a.shape, lambda i, first: (0, 0)) for a in args]
    return pl.pallas_call(
        functools.partial(backward_kernel, total=total, pack=pack),
        grid_spec=pltpu.PrefetchScalarGridSpec(
            num_scalar_prefetch=1,
            grid=(total // STEP,),
            in_specs=specs,
            out_specs=pl.BlockSpec((height, LANES), lambda i, first: (0, 0)),
            scratch_shapes=[
                pltpu.VMEM((hidden, 3 * own), BF16),
                pltpu.VMEM((hidden, 3 * hidden), BF16),
                pltpu.VMEM((own, 1), F32),
                pltpu.VMEM((hidden, own), F32),
                pltpu.VMEM((4 * own, 2 * hidden), F32),
                pltpu.VMEM((2 * hidden, 2 * hidden), F32),
                pltpu.VMEM((2 * hidden, saved[0].shape[0]), F32),
            ],
        ),
        out_shape=jax.ShapeDtypeStruct((height, LANES), F32),
        cost_estimate=pl.CostEstimate(
            flops=total * hidden * 2000, bytes_accessed=total * hidden * 20, transcendentals=0
        ),
        name="backward",
    )(first_own.reshape(1), lags, *saved, *args)


def rounds():
    steps = []
    for axis in ("dp", "chan"):
        bits = [1 << b for b in range(lax.axis_size(axis).bit_length() - 1)]
        alone = 1 if axis == "dp" else 0
        for group in [bits[:alone]] + [bits[b : b + 2] for b in range(alone, len(bits), 2)]:
            masks = [0]
            for bit in group:
                masks += [mask | bit for mask in masks]
            if len(masks) > 1:
                steps.append((axis, masks))
    return steps


def share(both, summed):
    steps = rounds()
    for axis, masks in steps:
        size = lax.axis_size(axis)
        parts = [both]
        for mask in masks[1:]:
            parts.append(lax.ppermute(both, axis, [(i, i ^ mask) for i in range(size)]))
        total = sum(part[:summed] for part in parts)
        both = jnp.concatenate([total, *(part[summed:] for part in parts)], axis=0)
    return parts


def finish_kernel(*refs, own, pack):
    steps = rounds()
    part_refs, refs = refs[: len(steps[-1][1])], refs[len(steps[-1][1]) :]
    embed_ref, bias_ref, hidden_ref, freq_ref = refs[:4]
    embed_grad, bias_grad, hidden_grad, frequency_grad, output_grad, decay_grad, rows_ref = refs[4:]
    hidden, features = hidden_ref.shape[0], embed_ref.shape[0]
    summed = summed_rows(hidden, output_grad.shape[1])
    total = sum(ref[:summed] for ref in part_refs)
    net = total[:hidden]
    turned = net.T
    decay_grad[...] = total[hidden : hidden + decay_grad.shape[0]]
    unit = own // pack
    count = output_grad.shape[1] // own
    here = {axis: lax.axis_index(axis) for axis in ("dp", "chan")}
    each = count // len(part_refs)
    for k in range(count):
        there, rest = dict(here), k
        for axis, masks in steps:
            there[axis] = there[axis] ^ masks[rest % len(masks)]
            rest //= len(masks)
        place = there["chan"] * lax.axis_size("dp") + there["dp"]
        for n in range(pack):
            rows_ref[pl.ds(pl.multiple_of(place * own + n * unit, unit), unit), :] = part_refs[
                k // each
            ][pl.ds(summed + k % each * unit, unit), n * hidden : (n + 1) * hidden]
    output_grad[...] = rows_ref[...].T
    table = turned[hidden:]
    embed = jnp.concatenate([table[features - 1 : features], table[: features - 1]], axis=0)
    bias = table[features : features + 1]
    embed_grad[...] = freq_ref[:1] * embed
    bias_grad[...] = freq_ref[:1] * bias
    hidden_grad[...] = column(freq_ref[1:2, :]) * net[:, :hidden]
    frequency_grad[:1] = (
        jnp.sum(embed_ref[...] * embed, axis=0, keepdims=True) + bias_ref[...] * bias
    )
    frequency_grad[1:2] = jnp.sum(hidden_ref[...].T * turned[:hidden], axis=0, keepdims=True)


def finish(parts, embed_weight, embed_bias, hidden_weight, frequency, channels, own):
    hidden, features = embed_weight.shape
    shapes = (
        (features, hidden), (1, hidden), (hidden, hidden), (2, hidden), (hidden, channels),
        (-(-channels // LANES), LANES),
    )
    embed, bias, hid, freq, output, decay = pl.pallas_call(
        functools.partial(finish_kernel, own=own, pack=packing(own, hidden)),
        out_shape=[jax.ShapeDtypeStruct(shape, F32) for shape in shapes],
        scratch_shapes=[pltpu.VMEM((channels, hidden), F32)],
        compiler_params=pltpu.CompilerParams(vmem_limit_bytes=8 * 2**20),
        name="finish",
    )(*parts, embed_weight.T, embed_bias[None], hidden_weight, frequency)
    return embed.T, bias[0], hid, freq, output.T, decay.reshape(-1)[:channels]


def work(
    signal,
    signal_grad,
    embed_weight,
    embed_bias,
    hidden_weight,
    frequency,
    output_weight,
    decay_rate,
):
    seq_local, chan_local, length = signal.shape
    total = 2 * length
    dp, chan = lax.axis_size("dp"), lax.axis_size("chan")
    own = chan_local // dp
    count = dp * chan
    hidden = hidden_weight.shape[0]
    channels = chan * chan_local
    scale = 1.0 / math.sqrt(seq_local * dp * length)
    at_dp, at_chan = lax.axis_index("dp"), lax.axis_index("chan")

    partners = sorted(
        range(1, dp), key=lambda p: (p != 1, -bin(p >> 1).count("1"), p & 1, p)
    )
    chunks = 2 if own % 16 == 0 and dp > 2 else 1
    per = own // chunks
    late = partners[-2:] if chunks > 1 else []
    soon = [p for p in (0, *partners) if p not in late]
    items = [(p, 0, own) for p in (*partners[1:3], partners[0], *soon[4:], 0)]
    items += [(p, q * per, per) for q in range(chunks) for p in late]
    made, pieces = [], {}
    for some in (tuple(items[:2]), tuple(items[2:])):
        made = pick(signal, signal_grad, some, own, made[:1])
        for (p, start, _), sent in zip(some, made):
            swap = [(i, i ^ p) for i in range(dp)]
            pieces[p, start] = lax.ppermute(sent, "dp", swap) if p else sent
    lags = spectrum = None
    step = max(2, dp // 4)
    for at in range(0, len(soon), step):
        end = not late and at + step >= len(soon)
        spectrum = correlate(
            [pieces[p, 0] for p in soon[at : at + step]], spectrum, scale, count if end else 0
        )
    lags = spectrum
    for q in range(chunks if late else 0):
        lags = correlate(
            [pieces[p, q * per] for p in late], spectrum, scale, count, lags if q else None, q, chunks
        )

    saved = network(embed_weight, embed_bias, hidden_weight, frequency, total)
    shared = lax.all_to_all(lags, ("dp", "chan"), 0, 0, tiled=True)
    first_own = at_chan * chan_local + at_dp * own
    both = backward(
        first_own, lags, saved, decay_rate, output_weight, hidden_weight, frequency, total
    )
    parts = share(both, summed_rows(hidden, channels))
    filter_grad = jnp.swapaxes(shared.reshape(dp, chan, own, -1), 0, 1)
    filter_grad = filter_grad.reshape(channels, -1)
    return (
        filter_grad,
        *finish(parts, embed_weight, embed_bias, hidden_weight, frequency, channels, own),
    )


def solution(mesh):
    placed = (P("dp", "chan", None), P("dp", "chan", None), P(), P(), P(), P(), P(), P())
    return jax.shard_map(
        work,
        mesh=mesh,
        in_specs=placed,
        out_specs=(P(None, ("dp", "chan")), P(), P(), P(), P(), P(), P()),
        check_vma=False,
    )
```

```python
import functools
import math

import jax
import jax.numpy as jnp
import numpy as np
from jax import lax
from jax.experimental import pallas as pl
from jax.experimental.pallas import tpu as pltpu
from jax.sharding import PartitionSpec as P


LANES = 128
F32 = jnp.float32
BF16 = jnp.bfloat16


def split(values):
    high = values.astype(BF16)
    return high, (values - high.astype(F32)).astype(BF16)


def split_table(values):
    high = values.astype(BF16)
    return high, (values - high.astype(np.float64)).astype(BF16)


def tables(rows, scale):
    total = 2 * rows * LANES
    odd = 2 * np.arange(rows) + 1
    angle = np.pi * (odd[:, None] * np.arange(2 * rows)[None, :] % (4 * rows)) / (2 * rows)
    first = np.concatenate([np.cos(angle[:, :rows]), -np.sin(angle[:, :rows])], axis=0)
    first = np.concatenate(split_table(first), axis=1)
    turn = np.pi * (odd[:, None] * np.arange(LANES)[None, :]) / total
    twist = np.stack([np.cos(turn), -np.sin(turn)]).astype(np.float32)
    untwist = (np.stack([np.cos(turn), np.sin(turn)]) * scale).astype(np.float32)
    fine = 2 * np.pi * (np.arange(LANES)[:, None] * np.arange(LANES)[None, :] % LANES) / LANES
    cosine, sine = np.cos(fine), np.sin(fine)
    second = np.block([[cosine, -sine], [sine, cosine]])
    sign = np.where(np.arange(2 * rows) < rows, 1.0, -1.0)[:, None]
    last = np.concatenate([np.cos(angle).T, -np.sin(angle).T], axis=1) * sign
    last_high, last_low = split_table(last)
    last = np.concatenate([last_high, last_low, last_high], axis=1)
    second, back = (
        np.concatenate([high, high, low], axis=0)
        for high, low in (split_table(second), split_table(second.T))
    )
    return first, twist, untwist, second, back, last


def dot(a, b):
    return jnp.dot(a, b, preferred_element_type=F32)


def stacked(values, axis):
    high, low = split(values)
    return jnp.concatenate([high, low], axis=axis)


def narrow(values, axis):
    high, low = split(values)
    return jnp.concatenate([high, low, high], axis=axis)


def wide(values, axis):
    high, low = split(values)
    return jnp.concatenate([high, high, low], axis=axis)


def dot_lanes(a, b):
    return lax.dot_general(a, b, (((1,), (1,)), ((), ())), preferred_element_type=F32)


def sine_cosine(angle):
    turns = (angle * (1.0 / math.pi) + 12582912.0) - 12582912.0
    rest = (angle - turns * 3.140625) - turns * 9.67653589793e-4
    sign = jnp.where((turns.astype(jnp.int32) & 1) != 0, -1.0, 1.0)
    square = rest * rest
    rest = rest * sign
    sine = (2.6000244184306192e-6 * square - 1.9806601562034863e-4) * square + 8.333017104043598e-3
    sine = (sine * square - 0.1666665708890745) * square * rest + rest
    cosine = (-2.6076816602017467e-7 * square + 2.4761870623092258e-5) * square
    cosine = ((cosine - 1.3888403220356624e-3) * square + 4.1666640707487275e-2) * square
    cosine = (cosine - 0.49999999549109586) * square + 1.0
    return sine, cosine * sign


def column(row):
    size = row.shape[1]
    at = [lax.broadcasted_iota(jnp.int32, (size, size), d) for d in (0, 1)]
    return jnp.sum(jnp.where(at[0] == at[1], row, 0.0), axis=1, keepdims=True)


def pick_kernel(x_ref, g_ref, *refs, items, own, after):
    refs = refs[after:]
    outs, held = refs[: len(items)], refs[len(items) : 2 * len(items)]
    in_sem, out_sem = refs[2 * len(items) :]
    arrivals, departures = [], []
    for k, (partner, start, count) in enumerate(items):
        first = pl.multiple_of((lax.axis_index("dp") ^ partner) * own + start, count)
        for at, ref in enumerate((x_ref, g_ref)):
            arrivals.append(
                pltpu.make_async_copy(
                    ref.at[:, pl.ds(first, count), :], held[k].at[at], in_sem.at[k, at]
                )
            )
            arrivals[-1].start()
    for k in range(len(items)):
        arrivals[2 * k].wait()
        arrivals[2 * k + 1].wait()
        departures.append(pltpu.make_async_copy(held[k], outs[k], out_sem.at[k]))
        departures[-1].start()
    for departure in departures:
        departure.wait()


def pick(x, g, items, own, after=()):
    seqs, _, length = x.shape
    if own % 8:
        return [
            jnp.stack(
                [
                    lax.dynamic_slice_in_dim(
                        v, (lax.axis_index("dp") ^ partner) * own + start, count, 1
                    )
                    for v in (x, g)
                ]
            )
            for partner, start, count in items
        ]
    shapes = [(2, seqs, count, length) for _, _, count in items]
    anywhere = pl.BlockSpec(memory_space=pl.ANY)
    return pl.pallas_call(
        functools.partial(pick_kernel, items=items, own=own, after=len(after)),
        in_specs=[anywhere] * (2 + len(after)),
        out_specs=[anywhere] * len(items),
        out_shape=[jax.ShapeDtypeStruct(shape, BF16) for shape in shapes],
        scratch_shapes=[
            *[pltpu.VMEM(shape, BF16) for shape in shapes],
            pltpu.SemaphoreType.DMA((len(items), 2)),
            pltpu.SemaphoreType.DMA((len(items),)),
        ],
        cost_estimate=pl.CostEstimate(
            flops=0, bytes_accessed=4 * sum(math.prod(shape) for shape in shapes), transcendentals=0
        ),
        name="pick",
    )(x, g, *after)


def correlate_kernel(*refs, pieces, held, lags, last):
    piece_refs, refs = refs[:pieces], refs[pieces:]
    held_ref, refs = (refs[0], refs[1:]) if held else (None, refs)
    refs = refs[lags:]
    first_ref, twist_ref, second_ref = refs[:3]
    if last:
        untwist_ref, back_ref, last_ref, out_ref, other_ref, lag_ref, cross_ref = refs[3:10]
    else:
        out_ref = refs[3]
    turn_ref, high_ref, low_ref, spec_ref = refs[-4:]
    _, seqs_each, channels, length = piece_refs[0].shape
    rows = length // LANES
    seqs = pieces * seqs_each
    step = pl.program_id(0)
    each = high_ref.shape[0] // (2 * seqs * rows)

    @pl.when(step == 0)
    def _():
        for s in range(seqs):
            for at in range(2):
                for row in range(rows):
                    turn_ref[at * seqs + s, pl.ds(row * channels, channels), :] = piece_refs[
                        s // seqs_each
                    ][at, s % seqs_each, :, pl.ds(row * LANES, LANES)].astype(F32)

    cosine = jnp.concatenate([twist_ref[0]] * 2, axis=1)
    sine = jnp.concatenate([twist_ref[1]] * 2, axis=1)
    first = first_ref[...]

    def line(at, s, k):
        return pl.ds(((k * 2 + at) * seqs + s) * rows, rows)

    for k in range(each):
        for s in range(seqs):
            pair = jnp.concatenate(
                [
                    turn_ref[
                        at * seqs + s, pl.ds(step * each + k, rows, stride=channels), :
                    ].astype(BF16)
                    for at in range(2)
                ],
                axis=1,
            )
            both = dot(first, jnp.concatenate([pair, pair], axis=0))
            real, imag = both[:rows], both[rows:]
            real, imag = real * cosine - imag * sine, real * sine + imag * cosine
            for at, part in ((0, slice(0, LANES)), (1, slice(LANES, 2 * LANES))):
                row = jnp.concatenate([real[:, part], imag[:, part]], axis=1)
                high_ref[line(at, s, k), :], low_ref[line(at, s, k), :] = split(row)
    spec_ref[...] = dot(
        jnp.concatenate([high_ref[...], low_ref[...], high_ref[...]], axis=1), second_ref[...]
    )
    for k in range(each):
        if held:
            real, imag = held_ref[k, :, :LANES], held_ref[k, :, LANES:]
        else:
            real = imag = jnp.zeros((rows, LANES), F32)
        for s in range(seqs):
            a, b = spec_ref[line(0, s, k), :], spec_ref[line(1, s, k), :]
            a_real, a_imag, b_real, b_imag = a[:, :LANES], a[:, LANES:], b[:, :LANES], b[:, LANES:]
            real = real + (a_real * b_real + a_imag * b_imag)
            imag = imag + (a_real * b_imag - a_imag * b_real)
        if last:
            cross_line = pl.ds(pl.multiple_of((step * each + k) * rows, rows), rows)
            cross_ref[cross_line, :LANES] = real
            cross_ref[cross_line, LANES:] = imag
        else:
            out_ref[k, :, :LANES] = real
            out_ref[k, :, LANES:] = imag
    if not last:
        return

    @pl.when(step == pl.num_programs(0) - 1)
    def _():
        owners, channels, lag_count = out_ref.shape
        back_cos, back_sin = untwist_ref[0], untwist_ref[1]
        group = math.gcd(channels, 4)
        for start in range(0, channels, group):
            high, low = split(cross_ref[pl.ds(start * rows, group * rows), :])
            back = dot(jnp.concatenate([high, low, high], axis=1), back_ref[...])
            for c in range(0, group, 2):
                turned = []
                for k in range(c, c + 2):
                    real = back[k * rows : (k + 1) * rows, :LANES]
                    imag = back[k * rows : (k + 1) * rows, LANES:]
                    turned.append(
                        jnp.concatenate(
                            [real * back_cos - imag * back_sin, real * back_sin + imag * back_cos],
                            axis=0,
                        )
                    )
                lags = dot(last_ref[...], wide(jnp.concatenate(turned, axis=1), 0))
                for k in range(2):
                    lag_ref[pl.ds((start + c + k) * 2 * rows, 2 * rows), :] = lags[
                        :, k * LANES : (k + 1) * LANES
                    ]
        wide_rows = lag_count // LANES
        for owner in range(owners):
            for k in range(wide_rows):
                out_ref[owner, :, pl.ds(k * LANES, LANES)] = lag_ref[
                    pl.ds(owner * wide_rows + k, channels, stride=2 * rows), :
                ]
        skip = (1 - (lax.axis_index("dp") & 1)) * (owners // 2 * wide_rows)
        for owner in range(owners // 2):
            for k in range(wide_rows):
                other_ref[owner, :, pl.ds(k * LANES, LANES)] = lag_ref[
                    pl.ds(skip + owner * wide_rows + k, channels, stride=2 * rows), :
                ]


def correlate(pieces, held, scale, owners, lags=None, chunk=0, chunks=1):
    _, seqs_each, channels, length = pieces[0].shape
    lanes, rows = LANES, length // LANES
    seqs = seqs_each * len(pieces)
    total = 2 * length
    each = max(1, min(channels, 8 // seqs))
    first, twist, untwist, second, back, last = (
        jnp.asarray(t) for t in tables(rows, 2.0 * scale / total)
    )
    consts = [first, twist, second] + ([untwist, back, last] if owners else [])
    skip = chunk * (channels // each)
    spectrum = pl.BlockSpec((each, rows, 2 * lanes), lambda c: (c + skip, 0, 0))
    lags = [] if lags is None else [lags]
    held = [] if held is None else [held]
    block = pl.BlockSpec(pieces[0].shape, lambda c: (0, 0, 0, 0))
    whole = [
        pl.BlockSpec(t.shape, functools.partial(lambda n, c: (0,) * n, t.ndim)) for t in consts
    ]
    if owners:
        shape = (owners, channels * chunks, total // owners)
        part = (owners // 2, channels, total // owners)
        out_spec = [
            pl.BlockSpec((owners, channels, total // owners), lambda c: (0, chunk, 0)),
            pl.BlockSpec(part, lambda c: (0, 0, 0)),
        ]
        out_shape = [jax.ShapeDtypeStruct(shape, F32), jax.ShapeDtypeStruct(part, F32)]
    else:
        shape = (channels, rows, 2 * lanes)
        out_spec = spectrum
        out_shape = jax.ShapeDtypeStruct(shape, F32)
    scratch = []
    if owners:
        scratch = [
            pltpu.VMEM((channels * 2 * rows, lanes), F32),
            pltpu.VMEM((channels * rows, 2 * lanes), F32),
        ]
    scratch += [
        pltpu.VMEM((2 * seqs, rows * channels, lanes), F32),
        pltpu.VMEM((each * 2 * seqs * rows, 2 * lanes), BF16),
        pltpu.VMEM((each * 2 * seqs * rows, 2 * lanes), BF16),
        pltpu.VMEM((each * 2 * seqs * rows, 2 * lanes), F32),
    ]
    return pl.pallas_call(
        functools.partial(
            correlate_kernel,
            pieces=len(pieces),
            held=len(held),
            lags=len(lags),
            last=bool(owners),
        ),
        grid=(channels // each,),
        in_specs=[block] * len(pieces)
        + [spectrum] * len(held)
        + [pl.BlockSpec(memory_space=pl.ANY)] * len(lags)
        + whole,
        input_output_aliases={len(pieces) + len(held): 0} if lags else {},
        out_specs=out_spec,
        out_shape=out_shape,
        scratch_shapes=scratch,
        cost_estimate=pl.CostEstimate(
            flops=channels * seqs * 2 * rows * lanes * lanes * 36,
            bytes_accessed=channels * (seqs * rows * lanes * 4 + total * 4),
            transcendentals=0,
        ),
        compiler_params=pltpu.CompilerParams(vmem_limit_bytes=24 * 2**20),
        name="correlate",
    )(*pieces, *held, *lags, *consts)


STEP = 2048
BANDS_PAD = 8


def lag_row(step, second, total):
    return step * STEP + lax.broadcasted_iota(jnp.int32, (1, STEP), 1) - second * (total // 2)


def network_kernel(
    factor_ref, embed_ref, bias_ref, hidden_ref, freq_ref,
    table_ref, first_ref, second_ref, cos1_ref, cos2_ref,
    embed_parts, hidden_parts, freq_cols, *, total,
):
    hidden = hidden_ref.shape[0]
    step = pl.program_id(0)

    @pl.when(step == 0)
    def _():
        embed = jnp.concatenate(
            [
                embed_ref[1:],
                embed_ref[:1],
                bias_ref[...],
                jnp.zeros((BANDS_PAD - 2, hidden), F32),
            ],
            axis=0,
        )
        embed_parts[...] = narrow(embed.T, 1)
        hidden_parts[...] = narrow(hidden_ref[...], 1)
        for k in range(2):
            freq_cols[k] = column(freq_ref[k : k + 1, :])

    lag = lag_row(step, lax.axis_index("dp") & 1, total)
    length = total // 2
    phase = ((factor_ref[...] * lag) & (total - 1)).astype(F32) * (2.0 * math.pi / total)
    sine, cosine = sine_cosine(phase)
    scaled = lag.astype(F32) / length
    row = lax.broadcasted_iota(jnp.int32, (BANDS_PAD, STEP), 0)
    extra = jnp.where(row == 0, scaled, jnp.where(row == 1, 1.0, 0.0))
    table = jnp.concatenate([sine, cosine, extra], axis=0)
    table_ref[...] = stacked(table, 0)
    first, cos1 = sine_cosine(freq_cols[0] * dot(embed_parts[...], wide(table, 0)))
    first_ref[...] = stacked(first, 0)
    cos1_ref[...] = cos1
    second, cos2 = sine_cosine(freq_cols[1] * dot(hidden_parts[...], wide(first, 0)))
    second_ref[...] = stacked(second, 0)
    cos2_ref[...] = cos2


def network(embed_weight, embed_bias, hidden_weight, frequency, total):
    hidden, features = embed_weight.shape
    bands = (features - 1) // 2
    factors = np.array(
        [[max(1, int(0.45 * total * 10000.0 ** (-band / bands)))] for band in range(bands)], np.int32
    )
    args = (jnp.asarray(factors), embed_weight.T, embed_bias[None], hidden_weight, frequency)
    whole = [pl.BlockSpec(a.shape, lambda i: (0, 0)) for a in args]
    depth = 2 * bands + BANDS_PAD
    heights = ((2 * depth, BF16), (2 * hidden, BF16), (2 * hidden, BF16), (hidden, F32), (hidden, F32))
    return pl.pallas_call(
        functools.partial(network_kernel, total=total),
        grid=(total // 2 // STEP,),
        in_specs=whole,
        out_specs=[pl.BlockSpec((h, STEP), lambda i: (0, i)) for h, _ in heights],
        out_shape=[jax.ShapeDtypeStruct((h, total // 2), t) for h, t in heights],
        scratch_shapes=[
            pltpu.VMEM((hidden, 3 * depth), BF16),
            pltpu.VMEM((hidden, 3 * hidden), BF16),
            pltpu.VMEM((2, hidden, 1), F32),
        ],
        cost_estimate=pl.CostEstimate(
            flops=total * hidden * 600, bytes_accessed=total * hidden * 20, transcendentals=0
        ),
        name="network",
    )(*args)


def backward_kernel(place_ref, second_ref, lags_ref, *refs, others, total, pack):
    other_refs, refs = refs[:others], refs[others:]
    backward_body(place_ref, second_ref, lags_ref, other_refs, *refs, total=total, pack=pack)


def backward_body(
    place_ref, second_ref, lags_ref, other_refs, table_ref, layer1_ref, layer2_ref, cos1_ref, cos2_ref,
    decay_ref, output_ref, hidden_ref, freq_ref,
    out_ref, output_parts, hidden_parts, decay_col, own_ref, sum1_ref, sum3_ref, sum5_ref, *, total, pack,
):
    step = pl.program_id(0)
    owners, own, _ = lags_ref.shape
    own = 2 * own
    hidden = hidden_ref.shape[0]
    first, second_of_pair = place_ref[0], second_ref[0]

    @pl.when(step == 0)
    def _():
        for ref in (sum1_ref, sum3_ref, sum5_ref):
            ref[...] = jnp.zeros_like(ref)
        channels = output_ref.shape[1]
        own_ref[...] = pltpu.roll(output_ref[...], channels - first, 1)[:, :own]
        output_parts[...] = narrow(own_ref[...], 1)
        hidden_parts[...] = narrow((hidden_ref[...] * column(freq_ref[1:2, :])).T, 1)
        place = [lax.broadcasted_iota(jnp.int32, (own, channels), d) for d in (0, 1)]
        decay_col[...] = jnp.sum(
            jnp.where(place[1] == place[0] + first, decay_ref[...], 0.0), axis=1, keepdims=True
        )

    mine = jnp.concatenate([lags_ref[k] for k in range(owners)], axis=1)
    others = jnp.concatenate(
        [jnp.concatenate([ref[k] for k in range(owners)], axis=1) for ref in other_refs], axis=0
    )
    upper = second_of_pair != 0
    lags = jnp.concatenate(
        [jnp.where(upper, others, mine), jnp.where(upper, mine, others)], axis=0
    )
    length = total // 2
    distance = jnp.abs(lag_row(step, second_of_pair, total)).astype(F32)
    window = jnp.exp(-decay_col[...] * distance / length)
    shaped = lags * window * (1.0 / math.sqrt(total))
    far = shaped * (distance / length)
    sum1_ref[...] += dot_lanes(stacked(jnp.concatenate([shaped, far], axis=0), 0), layer2_ref[...])
    second = dot(output_parts[...], wide(shaped, 0)) * cos2_ref[...]
    high, low = split(second)
    sum3_ref[...] += dot_lanes(jnp.concatenate([high, low], axis=0), layer1_ref[...])
    below = dot(hidden_parts[...], jnp.concatenate([high, high, low], axis=0)) * cos1_ref[...]
    sum5_ref[...] += dot_lanes(stacked(below, 0), table_ref[...])

    @pl.when(step == pl.num_programs(0) - 1)
    def _():
        def joined(ref):
            rows, cols = ref.shape[0] // 2, ref.shape[1] // 2
            return ref[:rows, :cols] + ref[:rows, cols:] + ref[rows:, :cols]

        net = jnp.concatenate([joined(sum3_ref), joined(sum5_ref)], axis=1)
        out_ref[:hidden] = jnp.concatenate(
            [net, jnp.zeros((hidden, LANES - net.shape[1]), F32)], axis=1
        )
        sums = joined(sum1_ref)
        decay_grad = -jnp.sum(own_ref[...].T * sums[own:], axis=1, keepdims=True)
        height = out_ref.shape[0] - hidden - own // pack
        place = lax.broadcasted_iota(jnp.int32, (height, LANES), 0) * LANES
        place = place + lax.broadcasted_iota(jnp.int32, (height, LANES), 1) - first
        decays = jnp.zeros((height, LANES), F32)
        for c in range(own):
            decays = jnp.where(place == c, decay_grad[c : c + 1], decays)
        out_ref[pl.ds(hidden, height), :] = decays
        per = own // pack
        parts = [sums[k * per : (k + 1) * per] for k in range(pack)]
        parts += [jnp.zeros((per, LANES - pack * hidden), F32)] if pack * hidden < LANES else []
        out_ref[hidden + height :] = jnp.concatenate(parts, axis=1)


def packing(own, hidden):
    return 2 if own % 16 == 0 and 2 * hidden <= LANES else 1


def summed_rows(hidden, channels):
    return hidden + -(-channels // (8 * LANES)) * 8


def backward(first, second, lags, others, saved, decay_rate, output_weight, hidden_weight, frequency, total):
    _, own, lag_count = lags.shape
    own = 2 * own
    hidden = hidden_weight.shape[0]
    pack = packing(own, hidden)
    height = summed_rows(hidden, decay_rate.shape[0]) + own // pack
    steps = total // 2 // STEP
    args = (decay_rate[None], output_weight.T, hidden_weight, frequency)
    specs = [
        pl.BlockSpec((STEP // lag_count, own // 2, lag_count), lambda i, at, second: (i + second[0] * steps, 0, 0))
    ]
    specs += [
        pl.BlockSpec((STEP // lag_count, *a.shape[1:]), lambda i, at, second: (i, 0, 0)) for a in others
    ]
    specs += [pl.BlockSpec((a.shape[0], STEP), lambda i, at, second: (0, i)) for a in saved]
    specs += [pl.BlockSpec(a.shape, lambda i, at, second: (0, 0)) for a in args]
    return pl.pallas_call(
        functools.partial(backward_kernel, others=len(others), total=total, pack=pack),
        grid_spec=pltpu.PrefetchScalarGridSpec(
            num_scalar_prefetch=2,
            grid=(steps,),
            in_specs=specs,
            out_specs=pl.BlockSpec((height, LANES), lambda i, at, second: (0, 0)),
            scratch_shapes=[
                pltpu.VMEM((hidden, 3 * own), BF16),
                pltpu.VMEM((hidden, 3 * hidden), BF16),
                pltpu.VMEM((own, 1), F32),
                pltpu.VMEM((hidden, own), F32),
                pltpu.VMEM((4 * own, 2 * hidden), F32),
                pltpu.VMEM((2 * hidden, 2 * hidden), F32),
                pltpu.VMEM((2 * hidden, saved[0].shape[0]), F32),
            ],
        ),
        out_shape=jax.ShapeDtypeStruct((height, LANES), F32),
        cost_estimate=pl.CostEstimate(
            flops=total * hidden * 1000, bytes_accessed=total * hidden * 10, transcendentals=0
        ),
        name="backward",
    )(first.reshape(1), second.reshape(1), lags, *others, *saved, *args)


def rounds():
    steps = []
    for axis in ("dp", "chan"):
        bits = [1 << b for b in range(lax.axis_size(axis).bit_length() - 1)]
        for group in [bits[b : b + 2] for b in range(axis == "dp", len(bits), 2)]:
            masks = [0]
            for bit in group:
                masks += [mask | bit for mask in masks]
            if len(masks) > 1:
                steps.append((axis, masks))
    return steps


def share(both, summed):
    steps = rounds()
    size = lax.axis_size("dp")
    both = both + lax.ppermute(both, "dp", [(i, i ^ 1) for i in range(size)])
    for axis, masks in steps:
        size = lax.axis_size(axis)
        parts = [both]
        for mask in masks[1:]:
            parts.append(lax.ppermute(both, axis, [(i, i ^ mask) for i in range(size)]))
        total = sum(part[:summed] for part in parts)
        both = jnp.concatenate([total, *(part[summed:] for part in parts)], axis=0)
    return parts


def finish_kernel(*refs, own, pack):
    steps = rounds()
    part_refs, refs = refs[: len(steps[-1][1])], refs[len(steps[-1][1]) :]
    embed_ref, bias_ref, hidden_ref, freq_ref = refs[:4]
    embed_grad, bias_grad, hidden_grad, frequency_grad, output_grad, decay_grad, rows_ref = refs[4:]
    hidden, features = hidden_ref.shape[0], embed_ref.shape[0]
    summed = summed_rows(hidden, output_grad.shape[1])
    total = sum(ref[:summed] for ref in part_refs)
    net = total[:hidden]
    turned = net.T
    decay_grad[...] = total[hidden : hidden + decay_grad.shape[0]]
    unit = own // pack
    count = output_grad.shape[1] // own
    here = {axis: lax.axis_index(axis) for axis in ("dp", "chan")}
    each = count // len(part_refs)
    for k in range(count):
        there, rest = dict(here), k
        for axis, masks in steps:
            there[axis] = there[axis] ^ masks[rest % len(masks)]
            rest //= len(masks)
        place = there["chan"] * (lax.axis_size("dp") // 2) + (there["dp"] >> 1)
        for n in range(pack):
            rows_ref[pl.ds(pl.multiple_of(place * own + n * unit, unit), unit), :] = part_refs[
                k // each
            ][pl.ds(summed + k % each * unit, unit), n * hidden : (n + 1) * hidden]
    output_grad[...] = rows_ref[...].T
    table = turned[hidden:]
    embed = jnp.concatenate([table[features - 1 : features], table[: features - 1]], axis=0)
    bias = table[features : features + 1]
    embed_grad[...] = freq_ref[:1] * embed
    bias_grad[...] = freq_ref[:1] * bias
    hidden_grad[...] = column(freq_ref[1:2, :]) * net[:, :hidden]
    frequency_grad[:1] = (
        jnp.sum(embed_ref[...] * embed, axis=0, keepdims=True) + bias_ref[...] * bias
    )
    frequency_grad[1:2] = jnp.sum(hidden_ref[...].T * turned[:hidden], axis=0, keepdims=True)


def finish(parts, embed_weight, embed_bias, hidden_weight, frequency, channels, own):
    hidden, features = embed_weight.shape
    shapes = (
        (features, hidden), (1, hidden), (hidden, hidden), (2, hidden), (hidden, channels),
        (-(-channels // LANES), LANES),
    )
    embed, bias, hid, freq, output, decay = pl.pallas_call(
        functools.partial(finish_kernel, own=own, pack=packing(own, hidden)),
        out_shape=[jax.ShapeDtypeStruct(shape, F32) for shape in shapes],
        scratch_shapes=[pltpu.VMEM((channels, hidden), F32)],
        compiler_params=pltpu.CompilerParams(vmem_limit_bytes=8 * 2**20),
        name="finish",
    )(*parts, embed_weight.T, embed_bias[None], hidden_weight, frequency)
    return embed.T, bias[0], hid, freq, output.T, decay.reshape(-1)[:channels]


def work(
    signal,
    signal_grad,
    embed_weight,
    embed_bias,
    hidden_weight,
    frequency,
    output_weight,
    decay_rate,
):
    seq_local, chan_local, length = signal.shape
    total = 2 * length
    dp, chan = lax.axis_size("dp"), lax.axis_size("chan")
    own = chan_local // dp
    count = dp * chan
    hidden = hidden_weight.shape[0]
    channels = chan * chan_local
    scale = 1.0 / math.sqrt(seq_local * dp * length)
    at_dp, at_chan = lax.axis_index("dp"), lax.axis_index("chan")

    partners = sorted(
        range(1, dp), key=lambda p: (p != 1, -bin(p >> 1).count("1"), p & 1, p)
    )
    chunks = 2 if own % 16 == 0 and dp > 2 else 1
    per = own // chunks
    late = partners[-2:] if chunks > 1 else []
    soon = [p for p in (0, *partners) if p not in late]
    items = [(p, 0, own) for p in (*partners[1:3], partners[0], *soon[4:], 0)]
    items += [(p, q * per, per) for q in range(chunks) for p in late]
    made, pieces = [], {}
    for some in (tuple(items[:2]), tuple(items[2:])):
        made = pick(signal, signal_grad, some, own, made[:1])
        for (p, start, _), sent in zip(some, made):
            swap = [(i, i ^ p) for i in range(dp)]
            pieces[p, start] = lax.ppermute(sent, "dp", swap) if p else sent
    lags = spectrum = None
    step = max(2, dp // 4)
    for at in range(0, len(soon), step):
        end = not late and at + step >= len(soon)
        spectrum = correlate(
            [pieces[p, 0] for p in soon[at : at + step]], spectrum, scale, count if end else 0
        )
    lags, others = (None, []) if late else (spectrum[0], [spectrum[1]])
    for q in range(chunks if late else 0):
        lags, other = correlate(
            [pieces[p, q * per] for p in late], spectrum, scale, count, lags, q, chunks
        )
        others.append(other)
    for q, other in enumerate(others):
        others[q] = lax.ppermute(other, "dp", [(i, i ^ 1) for i in range(dp)])

    saved = network(embed_weight, embed_bias, hidden_weight, frequency, total)
    shared = lax.all_to_all(lags, ("dp", "chan"), 0, 0, tiled=True)
    first = at_chan * chan_local + (at_dp & -2) * own
    both = backward(first, at_dp & 1, lags, others, saved, decay_rate, output_weight, hidden_weight, frequency, total)
    parts = share(both, summed_rows(hidden, channels))
    filter_grad = jnp.swapaxes(shared.reshape(dp, chan, own, -1), 0, 1)
    filter_grad = filter_grad.reshape(channels, -1)
    return (
        filter_grad,
        *finish(parts, embed_weight, embed_bias, hidden_weight, frequency, channels, 2 * own),
    )


def solution(mesh):
    placed = (P("dp", "chan", None), P("dp", "chan", None), P(), P(), P(), P(), P(), P())
    return jax.shard_map(
        work,
        mesh=mesh,
        in_specs=placed,
        out_specs=(P(None, ("dp", "chan")), P(), P(), P(), P(), P(), P()),
        check_vma=False,
    )
```

```python
import functools
import math

import jax
import jax.numpy as jnp
import numpy as np
from jax import lax
from jax.experimental import pallas as pl
from jax.experimental.pallas import tpu as pltpu
from jax.sharding import PartitionSpec as P


LANES = 128
F32 = jnp.float32
BF16 = jnp.bfloat16


def split(values):
    high = values.astype(BF16)
    return high, (values - high.astype(F32)).astype(BF16)


def split_table(values):
    high = values.astype(BF16)
    return high, (values - high.astype(np.float64)).astype(BF16)


def tables(rows, scale):
    total = 2 * rows * LANES
    odd = 2 * np.arange(rows) + 1
    angle = np.pi * (odd[:, None] * np.arange(2 * rows)[None, :] % (4 * rows)) / (2 * rows)
    first = np.concatenate([np.cos(angle[:, :rows]), -np.sin(angle[:, :rows])], axis=0)
    first = np.concatenate(split_table(first), axis=1)
    turn = np.pi * (odd[:, None] * np.arange(LANES)[None, :]) / total
    twist = np.stack([np.cos(turn), -np.sin(turn)]).astype(np.float32)
    untwist = (np.stack([np.cos(turn), np.sin(turn)]) * scale).astype(np.float32)
    fine = 2 * np.pi * (np.arange(LANES)[:, None] * np.arange(LANES)[None, :] % LANES) / LANES
    cosine, sine = np.cos(fine), np.sin(fine)
    second = np.block([[cosine, -sine], [sine, cosine]])
    sign = np.where(np.arange(2 * rows) < rows, 1.0, -1.0)[:, None]
    last = np.concatenate([np.cos(angle).T, -np.sin(angle).T], axis=1) * sign
    last_high, last_low = split_table(last)
    last = np.concatenate([last_high, last_low, last_high], axis=1)
    second, back = (
        np.concatenate([high, high, low], axis=0)
        for high, low in (split_table(second), split_table(second.T))
    )
    return first, twist, untwist, second, back, last


def dot(a, b):
    return jnp.dot(a, b, preferred_element_type=F32)


def stacked(values, axis):
    high, low = split(values)
    return jnp.concatenate([high, low], axis=axis)


def narrow(values, axis):
    high, low = split(values)
    return jnp.concatenate([high, low, high], axis=axis)


def wide(values, axis):
    high, low = split(values)
    return jnp.concatenate([high, high, low], axis=axis)


def dot_lanes(a, b):
    return lax.dot_general(a, b, (((1,), (1,)), ((), ())), preferred_element_type=F32)


def sine_cosine(angle):
    turns = (angle * (1.0 / math.pi) + 12582912.0) - 12582912.0
    rest = (angle - turns * 3.140625) - turns * 9.67653589793e-4
    sign = jnp.where((turns.astype(jnp.int32) & 1) != 0, -1.0, 1.0)
    square = rest * rest
    rest = rest * sign
    sine = (2.6000244184306192e-6 * square - 1.9806601562034863e-4) * square + 8.333017104043598e-3
    sine = (sine * square - 0.1666665708890745) * square * rest + rest
    cosine = (-2.6076816602017467e-7 * square + 2.4761870623092258e-5) * square
    cosine = ((cosine - 1.3888403220356624e-3) * square + 4.1666640707487275e-2) * square
    cosine = (cosine - 0.49999999549109586) * square + 1.0
    return sine, cosine * sign


def column(row):
    size = row.shape[1]
    at = [lax.broadcasted_iota(jnp.int32, (size, size), d) for d in (0, 1)]
    return jnp.sum(jnp.where(at[0] == at[1], row, 0.0), axis=1, keepdims=True)


def pick_kernel(x_ref, g_ref, *refs, items, own, after):
    refs = refs[after:]
    outs, held = refs[: len(items)], refs[len(items) : 2 * len(items)]
    in_sem, out_sem = refs[2 * len(items) :]
    arrivals, departures = [], []
    for k, (partner, start, count) in enumerate(items):
        first = pl.multiple_of((lax.axis_index("dp") ^ partner) * own + start, count)
        for at, ref in enumerate((x_ref, g_ref)):
            arrivals.append(
                pltpu.make_async_copy(
                    ref.at[:, pl.ds(first, count), :], held[k].at[at], in_sem.at[k, at]
                )
            )
            arrivals[-1].start()
    for k in range(len(items)):
        arrivals[2 * k].wait()
        arrivals[2 * k + 1].wait()
        departures.append(pltpu.make_async_copy(held[k], outs[k], out_sem.at[k]))
        departures[-1].start()
    for departure in departures:
        departure.wait()


def pick(x, g, items, own, after=()):
    seqs, _, length = x.shape
    if own % 8:
        return [
            jnp.stack(
                [
                    lax.dynamic_slice_in_dim(
                        v, (lax.axis_index("dp") ^ partner) * own + start, count, 1
                    )
                    for v in (x, g)
                ]
            )
            for partner, start, count in items
        ]
    shapes = [(2, seqs, count, length) for _, _, count in items]
    anywhere = pl.BlockSpec(memory_space=pl.ANY)
    return pl.pallas_call(
        functools.partial(pick_kernel, items=items, own=own, after=len(after)),
        in_specs=[anywhere] * (2 + len(after)),
        out_specs=[anywhere] * len(items),
        out_shape=[jax.ShapeDtypeStruct(shape, BF16) for shape in shapes],
        scratch_shapes=[
            *[pltpu.VMEM(shape, BF16) for shape in shapes],
            pltpu.SemaphoreType.DMA((len(items), 2)),
            pltpu.SemaphoreType.DMA((len(items),)),
        ],
        cost_estimate=pl.CostEstimate(
            flops=0, bytes_accessed=4 * sum(math.prod(shape) for shape in shapes), transcendentals=0
        ),
        name="pick",
    )(x, g, *after)


def correlate_kernel(*refs, pieces, held, lags, last):
    piece_refs, refs = refs[:pieces], refs[pieces:]
    held_ref, refs = (refs[0], refs[1:]) if held else (None, refs)
    refs = refs[lags:]
    first_ref, twist_ref, second_ref = refs[:3]
    if last:
        untwist_ref, back_ref, last_ref, out_ref, other_ref, lag_ref, cross_ref = refs[3:10]
    else:
        out_ref = refs[3]
    turn_ref, high_ref, low_ref, spec_ref = refs[-4:]
    _, seqs_each, channels, length = piece_refs[0].shape
    rows = length // LANES
    seqs = pieces * seqs_each
    step = pl.program_id(0)
    each = high_ref.shape[0] // (2 * seqs * rows)

    @pl.when(step == 0)
    def _():
        for s in range(seqs):
            for at in range(2):
                for row in range(rows):
                    turn_ref[at * seqs + s, pl.ds(row * channels, channels), :] = piece_refs[
                        s // seqs_each
                    ][at, s % seqs_each, :, pl.ds(row * LANES, LANES)].astype(F32)

    cosine = jnp.concatenate([twist_ref[0]] * 2, axis=1)
    sine = jnp.concatenate([twist_ref[1]] * 2, axis=1)
    first = first_ref[...]

    def line(at, s, k):
        return pl.ds(((k * 2 + at) * seqs + s) * rows, rows)

    for k in range(each):
        for s in range(seqs):
            pair = jnp.concatenate(
                [
                    turn_ref[
                        at * seqs + s, pl.ds(step * each + k, rows, stride=channels), :
                    ].astype(BF16)
                    for at in range(2)
                ],
                axis=1,
            )
            both = dot(first, jnp.concatenate([pair, pair], axis=0))
            real, imag = both[:rows], both[rows:]
            real, imag = real * cosine - imag * sine, real * sine + imag * cosine
            for at, part in ((0, slice(0, LANES)), (1, slice(LANES, 2 * LANES))):
                row = jnp.concatenate([real[:, part], imag[:, part]], axis=1)
                high_ref[line(at, s, k), :], low_ref[line(at, s, k), :] = split(row)
    spec_ref[...] = dot(
        jnp.concatenate([high_ref[...], low_ref[...], high_ref[...]], axis=1), second_ref[...]
    )
    for k in range(each):
        if held:
            real, imag = held_ref[k, :, :LANES], held_ref[k, :, LANES:]
        else:
            real = imag = jnp.zeros((rows, LANES), F32)
        for s in range(seqs):
            a, b = spec_ref[line(0, s, k), :], spec_ref[line(1, s, k), :]
            a_real, a_imag, b_real, b_imag = a[:, :LANES], a[:, LANES:], b[:, :LANES], b[:, LANES:]
            real = real + (a_real * b_real + a_imag * b_imag)
            imag = imag + (a_real * b_imag - a_imag * b_real)
        if last:
            cross_line = pl.ds(pl.multiple_of((step * each + k) * rows, rows), rows)
            cross_ref[cross_line, :LANES] = real
            cross_ref[cross_line, LANES:] = imag
        else:
            out_ref[k, :, :LANES] = real
            out_ref[k, :, LANES:] = imag
    if not last:
        return

    @pl.when(step == pl.num_programs(0) - 1)
    def _():
        owners, channels, lag_count = out_ref.shape
        back_cos, back_sin = untwist_ref[0], untwist_ref[1]
        group = math.gcd(channels, 4)
        for start in range(0, channels, group):
            high, low = split(cross_ref[pl.ds(start * rows, group * rows), :])
            back = dot(jnp.concatenate([high, low, high], axis=1), back_ref[...])
            for c in range(0, group, 2):
                turned = []
                for k in range(c, c + 2):
                    real = back[k * rows : (k + 1) * rows, :LANES]
                    imag = back[k * rows : (k + 1) * rows, LANES:]
                    turned.append(
                        jnp.concatenate(
                            [real * back_cos - imag * back_sin, real * back_sin + imag * back_cos],
                            axis=0,
                        )
                    )
                lags = dot(last_ref[...], wide(jnp.concatenate(turned, axis=1), 0))
                for k in range(2):
                    lag_ref[pl.ds((start + c + k) * 2 * rows, 2 * rows), :] = lags[
                        :, k * LANES : (k + 1) * LANES
                    ]
        wide_rows = lag_count // LANES
        for owner in range(owners):
            for k in range(wide_rows):
                out_ref[owner, :, pl.ds(k * LANES, LANES)] = lag_ref[
                    pl.ds(owner * wide_rows + k, channels, stride=2 * rows), :
                ]
        half = owners // 2
        other_ref[...] = out_ref[pl.ds((1 - (lax.axis_index("dp") & 1)) * half, half)]


def correlate(pieces, held, scale, owners, lags=None, chunk=0, chunks=1):
    _, seqs_each, channels, length = pieces[0].shape
    lanes, rows = LANES, length // LANES
    seqs = seqs_each * len(pieces)
    total = 2 * length
    each = max(1, min(channels, 8 // seqs))
    first, twist, untwist, second, back, last = (
        jnp.asarray(t) for t in tables(rows, 2.0 * scale / total)
    )
    consts = [first, twist, second] + ([untwist, back, last] if owners else [])
    skip = chunk * (channels // each)
    spectrum = pl.BlockSpec((each, rows, 2 * lanes), lambda c: (c + skip, 0, 0))
    lags = [] if lags is None else [lags]
    held = [] if held is None else [held]
    block = pl.BlockSpec(pieces[0].shape, lambda c: (0, 0, 0, 0))
    whole = [
        pl.BlockSpec(t.shape, functools.partial(lambda n, c: (0,) * n, t.ndim)) for t in consts
    ]
    if owners:
        shape = (owners, channels * chunks, total // owners)
        part = (owners // 2, channels, total // owners)
        out_spec = [
            pl.BlockSpec((owners, channels, total // owners), lambda c: (0, chunk, 0)),
            pl.BlockSpec(part, lambda c: (0, 0, 0)),
        ]
        out_shape = [jax.ShapeDtypeStruct(shape, F32), jax.ShapeDtypeStruct(part, F32)]
    else:
        shape = (channels, rows, 2 * lanes)
        out_spec = spectrum
        out_shape = jax.ShapeDtypeStruct(shape, F32)
    scratch = []
    if owners:
        scratch = [
            pltpu.VMEM((channels * 2 * rows, lanes), F32),
            pltpu.VMEM((channels * rows, 2 * lanes), F32),
        ]
    scratch += [
        pltpu.VMEM((2 * seqs, rows * channels, lanes), F32),
        pltpu.VMEM((each * 2 * seqs * rows, 2 * lanes), BF16),
        pltpu.VMEM((each * 2 * seqs * rows, 2 * lanes), BF16),
        pltpu.VMEM((each * 2 * seqs * rows, 2 * lanes), F32),
    ]
    return pl.pallas_call(
        functools.partial(
            correlate_kernel,
            pieces=len(pieces),
            held=len(held),
            lags=len(lags),
            last=bool(owners),
        ),
        grid=(channels // each,),
        in_specs=[block] * len(pieces)
        + [spectrum] * len(held)
        + [pl.BlockSpec(memory_space=pl.ANY)] * len(lags)
        + whole,
        input_output_aliases={len(pieces) + len(held): 0} if lags else {},
        out_specs=out_spec,
        out_shape=out_shape,
        scratch_shapes=scratch,
        cost_estimate=pl.CostEstimate(
            flops=channels * seqs * 2 * rows * lanes * lanes * 36,
            bytes_accessed=channels * (seqs * rows * lanes * 4 + total * 4),
            transcendentals=0,
        ),
        compiler_params=pltpu.CompilerParams(vmem_limit_bytes=24 * 2**20),
        name="correlate",
    )(*pieces, *held, *lags, *consts)


STEP = 2048
BANDS_PAD = 8


def lag_row(step, second, total):
    return step * STEP + lax.broadcasted_iota(jnp.int32, (1, STEP), 1) - second * (total // 2)


def network_kernel(
    factor_ref, embed_ref, bias_ref, hidden_ref, freq_ref,
    table_ref, first_ref, second_ref, cos1_ref, cos2_ref,
    embed_parts, hidden_parts, freq_cols, *, total,
):
    hidden = hidden_ref.shape[0]
    step = pl.program_id(0)

    @pl.when(step == 0)
    def _():
        embed = jnp.concatenate(
            [
                embed_ref[1:],
                embed_ref[:1],
                bias_ref[...],
                jnp.zeros((BANDS_PAD - 2, hidden), F32),
            ],
            axis=0,
        )
        embed_parts[...] = narrow(embed.T, 1)
        hidden_parts[...] = narrow(hidden_ref[...], 1)
        for k in range(2):
            freq_cols[k] = column(freq_ref[k : k + 1, :])

    lag = lag_row(step, lax.axis_index("dp") & 1, total)
    length = total // 2
    phase = ((factor_ref[...] * lag) & (total - 1)).astype(F32) * (2.0 * math.pi / total)
    sine, cosine = sine_cosine(phase)
    scaled = lag.astype(F32) / length
    row = lax.broadcasted_iota(jnp.int32, (BANDS_PAD, STEP), 0)
    extra = jnp.where(row == 0, scaled, jnp.where(row == 1, 1.0, 0.0))
    table = jnp.concatenate([sine, cosine, extra], axis=0)
    table_ref[...] = stacked(table, 0)
    first, cos1 = sine_cosine(freq_cols[0] * dot(embed_parts[...], wide(table, 0)))
    first_ref[...] = stacked(first, 0)
    cos1_ref[...] = cos1
    second, cos2 = sine_cosine(freq_cols[1] * dot(hidden_parts[...], wide(first, 0)))
    second_ref[...] = stacked(second, 0)
    cos2_ref[...] = cos2


def network(embed_weight, embed_bias, hidden_weight, frequency, total):
    hidden, features = embed_weight.shape
    bands = (features - 1) // 2
    factors = np.array(
        [[max(1, int(0.45 * total * 10000.0 ** (-band / bands)))] for band in range(bands)], np.int32
    )
    args = (jnp.asarray(factors), embed_weight.T, embed_bias[None], hidden_weight, frequency)
    whole = [pl.BlockSpec(a.shape, lambda i: (0, 0)) for a in args]
    depth = 2 * bands + BANDS_PAD
    heights = ((2 * depth, BF16), (2 * hidden, BF16), (2 * hidden, BF16), (hidden, F32), (hidden, F32))
    return pl.pallas_call(
        functools.partial(network_kernel, total=total),
        grid=(total // 2 // STEP,),
        in_specs=whole,
        out_specs=[pl.BlockSpec((h, STEP), lambda i: (0, i)) for h, _ in heights],
        out_shape=[jax.ShapeDtypeStruct((h, total // 2), t) for h, t in heights],
        scratch_shapes=[
            pltpu.VMEM((hidden, 3 * depth), BF16),
            pltpu.VMEM((hidden, 3 * hidden), BF16),
            pltpu.VMEM((2, hidden, 1), F32),
        ],
        cost_estimate=pl.CostEstimate(
            flops=total * hidden * 600, bytes_accessed=total * hidden * 20, transcendentals=0
        ),
        name="network",
    )(*args)


def backward_kernel(place_ref, second_ref, lags_ref, *refs, others, total, pack):
    other_refs, refs = refs[:others], refs[others:]
    backward_body(place_ref, second_ref, lags_ref, other_refs, *refs, total=total, pack=pack)


def backward_body(
    place_ref, second_ref, lags_ref, other_refs, table_ref, layer1_ref, layer2_ref, cos1_ref, cos2_ref,
    decay_ref, output_ref, hidden_ref, freq_ref,
    keep_ref, send_ref, output_parts, hidden_parts, decay_col, own_ref, sum1_ref, sum3_ref, sum5_ref, *, total, pack,
):
    step = pl.program_id(0)
    owners, own, _ = lags_ref.shape
    own = 2 * own
    hidden = hidden_ref.shape[0]
    first, second_of_pair = place_ref[0], second_ref[0]

    @pl.when(step == 0)
    def _():
        for ref in (sum1_ref, sum3_ref, sum5_ref):
            ref[...] = jnp.zeros_like(ref)
        channels = output_ref.shape[1]
        own_ref[...] = pltpu.roll(output_ref[...], channels - first, 1)[:, :own]
        output_parts[...] = narrow(own_ref[...], 1)
        hidden_parts[...] = narrow((hidden_ref[...] * column(freq_ref[1:2, :])).T, 1)
        place = [lax.broadcasted_iota(jnp.int32, (own, channels), d) for d in (0, 1)]
        decay_col[...] = jnp.sum(
            jnp.where(place[1] == place[0] + first, decay_ref[...], 0.0), axis=1, keepdims=True
        )

    mine = jnp.concatenate([lags_ref[k] for k in range(owners)], axis=1)
    others = jnp.concatenate(
        [jnp.concatenate([ref[k] for k in range(owners)], axis=1) for ref in other_refs], axis=0
    )
    upper = second_of_pair != 0
    lags = jnp.concatenate(
        [jnp.where(upper, others, mine), jnp.where(upper, mine, others)], axis=0
    )
    length = total // 2
    distance = jnp.abs(lag_row(step, second_of_pair, total)).astype(F32)
    window = jnp.exp(-decay_col[...] * distance / length)
    shaped = lags * window * (1.0 / math.sqrt(total))
    far = shaped * (distance / length)
    sum1_ref[...] += dot_lanes(stacked(jnp.concatenate([shaped, far], axis=0), 0), layer2_ref[...])
    second = dot(output_parts[...], wide(shaped, 0)) * cos2_ref[...]
    high, low = split(second)
    sum3_ref[...] += dot_lanes(jnp.concatenate([high, low], axis=0), layer1_ref[...])
    below = dot(hidden_parts[...], jnp.concatenate([high, high, low], axis=0)) * cos1_ref[...]
    sum5_ref[...] += dot_lanes(stacked(below, 0), table_ref[...])

    @pl.when(step == pl.num_programs(0) - 1)
    def _():
        def joined(ref):
            rows, cols = ref.shape[0] // 2, ref.shape[1] // 2
            return ref[:rows, :cols] + ref[:rows, cols:] + ref[rows:, :cols]

        net = jnp.concatenate([joined(sum3_ref), joined(sum5_ref)], axis=1)
        net = jnp.concatenate([net, jnp.zeros((hidden, LANES - net.shape[1]), F32)], axis=1)
        sums = joined(sum1_ref)
        decay_grad = -jnp.sum(own_ref[...].T * sums[own:], axis=1, keepdims=True)
        per, half = own // pack, keep_ref.shape[0]
        summed = half - per // 2
        height = 2 * summed - hidden
        place = lax.broadcasted_iota(jnp.int32, (height, LANES), 0) * LANES
        place = place + lax.broadcasted_iota(jnp.int32, (height, LANES), 1) - first
        decays = jnp.zeros((height, LANES), F32)
        for c in range(own):
            decays = jnp.where(place == c, decay_grad[c : c + 1], decays)
        parts = [sums[k * per : (k + 1) * per] for k in range(pack)]
        parts += [jnp.zeros((per, LANES - pack * hidden), F32)] if pack * hidden < LANES else []
        rows = jnp.concatenate(parts, axis=1)
        total_rows = jnp.concatenate([net, decays], axis=0)
        low = jnp.concatenate([total_rows[:summed], rows[: per // 2]], axis=0)
        high = jnp.concatenate([total_rows[summed:], rows[per // 2 :]], axis=0)
        keep_ref[...] = jnp.where(upper, high, low)
        send_ref[...] = jnp.where(upper, low, high)


def packing(own, hidden):
    return 2 if own % 16 == 0 and 2 * hidden <= LANES else 1


def summed_rows(hidden, channels):
    return -(-(hidden + -(-channels // LANES)) // 16) * 8


def backward(first, second, lags, others, saved, decay_rate, output_weight, hidden_weight, frequency, total):
    _, own, lag_count = lags.shape
    own = 2 * own
    hidden = hidden_weight.shape[0]
    pack = packing(own, hidden)
    height = summed_rows(hidden, decay_rate.shape[0]) + own // pack // 2
    steps = total // 2 // STEP
    args = (decay_rate[None], output_weight.T, hidden_weight, frequency)
    specs = [
        pl.BlockSpec((STEP // lag_count, own // 2, lag_count), lambda i, at, second: (i + second[0] * steps, 0, 0))
    ]
    specs += [
        pl.BlockSpec((STEP // lag_count, *a.shape[1:]), lambda i, at, second: (i, 0, 0)) for a in others
    ]
    specs += [pl.BlockSpec((a.shape[0], STEP), lambda i, at, second: (0, i)) for a in saved]
    specs += [pl.BlockSpec(a.shape, lambda i, at, second: (0, 0)) for a in args]
    return pl.pallas_call(
        functools.partial(backward_kernel, others=len(others), total=total, pack=pack),
        grid_spec=pltpu.PrefetchScalarGridSpec(
            num_scalar_prefetch=2,
            grid=(steps,),
            in_specs=specs,
            out_specs=[pl.BlockSpec((height, LANES), lambda i, at, second: (0, 0))] * 2,
            scratch_shapes=[
                pltpu.VMEM((hidden, 3 * own), BF16),
                pltpu.VMEM((hidden, 3 * hidden), BF16),
                pltpu.VMEM((own, 1), F32),
                pltpu.VMEM((hidden, own), F32),
                pltpu.VMEM((4 * own, 2 * hidden), F32),
                pltpu.VMEM((2 * hidden, 2 * hidden), F32),
                pltpu.VMEM((2 * hidden, saved[0].shape[0]), F32),
            ],
        ),
        out_shape=[jax.ShapeDtypeStruct((height, LANES), F32)] * 2,
        cost_estimate=pl.CostEstimate(
            flops=total * hidden * 1000, bytes_accessed=total * hidden * 10, transcendentals=0
        ),
        name="backward",
    )(first.reshape(1), second.reshape(1), lags, *others, *saved, *args)


def rounds():
    steps = []
    for axis in ("dp", "chan"):
        bits = [1 << b for b in range(lax.axis_size(axis).bit_length() - 1)]
        for group in [bits[b : b + 2] for b in range(axis == "dp", len(bits), 2)]:
            masks = [0]
            for bit in group:
                masks += [mask | bit for mask in masks]
            if len(masks) > 1:
                steps.append((axis, masks))
    return steps


def share(keep, send, summed):
    steps = rounds()
    pair = [(i, i ^ 1) for i in range(lax.axis_size("dp"))]
    both = keep + lax.ppermute(send, "dp", pair)
    for axis, masks in steps:
        size = lax.axis_size(axis)
        parts = [both]
        for mask in masks[1:]:
            parts.append(lax.ppermute(both, axis, [(i, i ^ mask) for i in range(size)]))
        total = sum(part[:summed] for part in parts)
        both = jnp.concatenate([total, *(part[summed:] for part in parts)], axis=0)
    return both, lax.ppermute(both, "dp", pair)


def finish_kernel(*refs, own, pack):
    steps = rounds()
    mine_ref, theirs_ref, embed_ref, bias_ref, hidden_ref, freq_ref = refs[:6]
    embed_grad, bias_grad, hidden_grad, frequency_grad, output_grad, decay_grad, rows_ref = refs[6:]
    hidden, features = hidden_ref.shape[0], embed_ref.shape[0]
    summed = summed_rows(hidden, output_grad.shape[1])
    upper = (lax.axis_index("dp") & 1) != 0
    low = jnp.where(upper, theirs_ref[...], mine_ref[...])
    high = jnp.where(upper, mine_ref[...], theirs_ref[...])
    total = jnp.concatenate([low[:summed], high[:summed]], axis=0)
    net = total[:hidden]
    turned = net.T
    decay_grad[...] = total[hidden : hidden + decay_grad.shape[0]]
    unit = own // pack // 2
    count = output_grad.shape[1] // own
    here = {axis: lax.axis_index(axis) for axis in ("dp", "chan")}
    for k in range(count):
        there, rest = dict(here), k
        for axis, masks in steps:
            there[axis] = there[axis] ^ masks[rest % len(masks)]
            rest //= len(masks)
        place = there["chan"] * (lax.axis_size("dp") // 2) + (there["dp"] >> 1)
        for n in range(pack):
            for m, half in enumerate((low, high)):
                at = pl.multiple_of(place * own + (2 * n + m) * unit, unit)
                rows_ref[pl.ds(at, unit), :] = half[
                    summed + k * unit : summed + (k + 1) * unit, n * hidden : (n + 1) * hidden
                ]
    output_grad[...] = rows_ref[...].T
    table = turned[hidden:]
    embed = jnp.concatenate([table[features - 1 : features], table[: features - 1]], axis=0)
    bias = table[features : features + 1]
    embed_grad[...] = freq_ref[:1] * embed
    bias_grad[...] = freq_ref[:1] * bias
    hidden_grad[...] = column(freq_ref[1:2, :]) * net[:, :hidden]
    frequency_grad[:1] = (
        jnp.sum(embed_ref[...] * embed, axis=0, keepdims=True) + bias_ref[...] * bias
    )
    frequency_grad[1:2] = jnp.sum(hidden_ref[...].T * turned[:hidden], axis=0, keepdims=True)


def finish(mine, theirs, embed_weight, embed_bias, hidden_weight, frequency, channels, own):
    hidden, features = embed_weight.shape
    shapes = (
        (features, hidden), (1, hidden), (hidden, hidden), (2, hidden), (hidden, channels),
        (-(-channels // LANES), LANES),
    )
    embed, bias, hid, freq, output, decay = pl.pallas_call(
        functools.partial(finish_kernel, own=own, pack=packing(own, hidden)),
        out_shape=[jax.ShapeDtypeStruct(shape, F32) for shape in shapes],
        scratch_shapes=[pltpu.VMEM((channels, hidden), F32)],
        compiler_params=pltpu.CompilerParams(vmem_limit_bytes=8 * 2**20),
        name="finish",
    )(mine, theirs, embed_weight.T, embed_bias[None], hidden_weight, frequency)
    return embed.T, bias[0], hid, freq, output.T, decay.reshape(-1)[:channels]


def work(
    signal,
    signal_grad,
    embed_weight,
    embed_bias,
    hidden_weight,
    frequency,
    output_weight,
    decay_rate,
):
    seq_local, chan_local, length = signal.shape
    total = 2 * length
    dp, chan = lax.axis_size("dp"), lax.axis_size("chan")
    own = chan_local // dp
    count = dp * chan
    hidden = hidden_weight.shape[0]
    channels = chan * chan_local
    scale = 1.0 / math.sqrt(seq_local * dp * length)
    at_dp, at_chan = lax.axis_index("dp"), lax.axis_index("chan")

    partners = sorted(
        range(1, dp), key=lambda p: (p != 1, -bin(p >> 1).count("1"), p & 1, p)
    )
    chunks = 2 if own % 16 == 0 and dp > 2 else 1
    per = own // chunks
    late = partners[-2:] if chunks > 1 else []
    soon = [p for p in (0, *partners) if p not in late]
    items = [(p, 0, own) for p in (*partners[1:3], partners[0], *soon[4:], 0)]
    items += [(p, q * per, per) for q in range(chunks) for p in late]
    made, pieces = [], {}
    for some in (tuple(items[:2]), tuple(items[2:])):
        made = pick(signal, signal_grad, some, own, made[:1])
        for (p, start, _), sent in zip(some, made):
            swap = [(i, i ^ p) for i in range(dp)]
            pieces[p, start] = lax.ppermute(sent, "dp", swap) if p else sent
    lags = spectrum = None
    step = max(2, dp // 4)
    for at in range(0, len(soon), step):
        end = not late and at + step >= len(soon)
        spectrum = correlate(
            [pieces[p, 0] for p in soon[at : at + step]], spectrum, scale, count if end else 0
        )
    lags, others = (None, []) if late else (spectrum[0], [spectrum[1]])
    for q in range(chunks if late else 0):
        lags, other = correlate(
            [pieces[p, q * per] for p in late], spectrum, scale, count, lags, q, chunks
        )
        others.append(other)
    for q, other in enumerate(others):
        others[q] = lax.ppermute(other, "dp", [(i, i ^ 1) for i in range(dp)])

    saved = network(embed_weight, embed_bias, hidden_weight, frequency, total)
    shared = lax.all_to_all(lags, ("dp", "chan"), 0, 0, tiled=True)
    first = at_chan * chan_local + (at_dp & -2) * own
    keep, send = backward(
        first, at_dp & 1, lags, others, saved, decay_rate, output_weight, hidden_weight, frequency, total
    )
    mine, theirs = share(keep, send, summed_rows(hidden, channels))
    filter_grad = jnp.swapaxes(shared.reshape(dp, chan, own, -1), 0, 1)
    filter_grad = filter_grad.reshape(channels, -1)
    return (
        filter_grad,
        *finish(mine, theirs, embed_weight, embed_bias, hidden_weight, frequency, channels, 2 * own),
    )


def solution(mesh):
    placed = (P("dp", "chan", None), P("dp", "chan", None), P(), P(), P(), P(), P(), P())
    return jax.shard_map(
        work,
        mesh=mesh,
        in_specs=placed,
        out_specs=(P(None, ("dp", "chan")), P(), P(), P(), P(), P(), P()),
        check_vma=False,
    )
```

```python
import functools
import math

import jax
import jax.numpy as jnp
import numpy as np
from jax import lax
from jax.experimental import pallas as pl
from jax.experimental.pallas import tpu as pltpu
from jax.sharding import PartitionSpec as P


LANES = 128
F32 = jnp.float32
BF16 = jnp.bfloat16


def split(values):
    high = values.astype(BF16)
    return high, (values - high.astype(F32)).astype(BF16)


def split_table(values):
    high = values.astype(BF16)
    return high, (values - high.astype(np.float64)).astype(BF16)


def tables(rows, scale):
    total = 2 * rows * LANES
    odd = 2 * np.arange(rows) + 1
    angle = np.pi * (odd[:, None] * np.arange(2 * rows)[None, :] % (4 * rows)) / (2 * rows)
    first = np.concatenate([np.cos(angle[:, :rows]), -np.sin(angle[:, :rows])], axis=0)
    first = np.concatenate(split_table(first), axis=1)
    turn = np.pi * (odd[:, None] * np.arange(LANES)[None, :]) / total
    twist = np.stack([np.cos(turn), -np.sin(turn)]).astype(np.float32)
    untwist = (np.stack([np.cos(turn), np.sin(turn)]) * scale).astype(np.float32)
    fine = 2 * np.pi * (np.arange(LANES)[:, None] * np.arange(LANES)[None, :] % LANES) / LANES
    cosine, sine = np.cos(fine), np.sin(fine)
    second = np.block([[cosine, -sine], [sine, cosine]])
    sign = np.where(np.arange(2 * rows) < rows, 1.0, -1.0)[:, None]
    last = np.concatenate([np.cos(angle).T, -np.sin(angle).T], axis=1) * sign
    last_high, last_low = split_table(last)
    last = np.concatenate([last_high, last_low, last_high], axis=1)
    second, back = (
        np.concatenate([high, high, low], axis=0)
        for high, low in (split_table(second), split_table(second.T))
    )
    return first, twist, untwist, second, back, last


def dot(a, b):
    return jnp.dot(a, b, preferred_element_type=F32)


def stacked(values, axis):
    high, low = split(values)
    return jnp.concatenate([high, low], axis=axis)


def narrow(values, axis):
    high, low = split(values)
    return jnp.concatenate([high, low, high], axis=axis)


def wide(values, axis):
    high, low = split(values)
    return jnp.concatenate([high, high, low], axis=axis)


def thirds(values):
    high, rest = values.astype(BF16), values
    rest = rest - high.astype(F32)
    middle = rest.astype(BF16)
    return high, middle, (rest - middle.astype(F32)).astype(BF16)


def narrow_exact(values, axis):
    high, middle, low = thirds(values)
    return jnp.concatenate([high, high, middle, middle, high, low], axis=axis)


def wide_exact(values, axis):
    high, middle, low = thirds(values)
    return jnp.concatenate([high, middle, high, middle, low, high], axis=axis)


def dot_lanes(a, b):
    return lax.dot_general(a, b, (((1,), (1,)), ((), ())), preferred_element_type=F32)


def sine_cosine(angle):
    turns = (angle * (1.0 / math.pi) + 12582912.0) - 12582912.0
    rest = (angle - turns * 3.140625) - turns * 9.67653589793e-4
    sign = jnp.where((turns.astype(jnp.int32) & 1) != 0, -1.0, 1.0)
    square = rest * rest
    rest = rest * sign
    sine = (2.6000244184306192e-6 * square - 1.9806601562034863e-4) * square + 8.333017104043598e-3
    sine = (sine * square - 0.1666665708890745) * square * rest + rest
    cosine = (-2.6076816602017467e-7 * square + 2.4761870623092258e-5) * square
    cosine = ((cosine - 1.3888403220356624e-3) * square + 4.1666640707487275e-2) * square
    cosine = (cosine - 0.49999999549109586) * square + 1.0
    return sine, cosine * sign


def column(row):
    size = row.shape[1]
    at = [lax.broadcasted_iota(jnp.int32, (size, size), d) for d in (0, 1)]
    return jnp.sum(jnp.where(at[0] == at[1], row, 0.0), axis=1, keepdims=True)


def pick_kernel(x_ref, g_ref, *refs, items, own, after):
    refs = refs[after:]
    outs, held = refs[: len(items)], refs[len(items) : 2 * len(items)]
    in_sem, out_sem = refs[2 * len(items) :]
    arrivals, departures = [], []
    for k, (partner, start, count) in enumerate(items):
        first = pl.multiple_of((lax.axis_index("dp") ^ partner) * own + start, count)
        for at, ref in enumerate((x_ref, g_ref)):
            arrivals.append(
                pltpu.make_async_copy(
                    ref.at[:, pl.ds(first, count), :], held[k].at[at], in_sem.at[k, at]
                )
            )
            arrivals[-1].start()
    for k in range(len(items)):
        arrivals[2 * k].wait()
        arrivals[2 * k + 1].wait()
        departures.append(pltpu.make_async_copy(held[k], outs[k], out_sem.at[k]))
        departures[-1].start()
    for departure in departures:
        departure.wait()


def pick(x, g, items, own, after=()):
    seqs, _, length = x.shape
    if own % 8:
        return [
            jnp.stack(
                [
                    lax.dynamic_slice_in_dim(
                        v, (lax.axis_index("dp") ^ partner) * own + start, count, 1
                    )
                    for v in (x, g)
                ]
            )
            for partner, start, count in items
        ]
    shapes = [(2, seqs, count, length) for _, _, count in items]
    anywhere = pl.BlockSpec(memory_space=pl.ANY)
    return pl.pallas_call(
        functools.partial(pick_kernel, items=items, own=own, after=len(after)),
        in_specs=[anywhere] * (2 + len(after)),
        out_specs=[anywhere] * len(items),
        out_shape=[jax.ShapeDtypeStruct(shape, BF16) for shape in shapes],
        scratch_shapes=[
            *[pltpu.VMEM(shape, BF16) for shape in shapes],
            pltpu.SemaphoreType.DMA((len(items), 2)),
            pltpu.SemaphoreType.DMA((len(items),)),
        ],
        cost_estimate=pl.CostEstimate(
            flops=0, bytes_accessed=4 * sum(math.prod(shape) for shape in shapes), transcendentals=0
        ),
        name="pick",
    )(x, g, *after)


def correlate_kernel(*refs, pieces, held, lags, last):
    piece_refs, refs = refs[:pieces], refs[pieces:]
    held_ref, refs = (refs[0], refs[1:]) if held else (None, refs)
    refs = refs[lags:]
    first_ref, twist_ref, second_ref = refs[:3]
    if last:
        untwist_ref, back_ref, last_ref, out_ref, other_ref, lag_ref, cross_ref = refs[3:10]
    else:
        out_ref = refs[3]
    turn_ref, high_ref, low_ref, spec_ref = refs[-4:]
    _, seqs_each, channels, length = piece_refs[0].shape
    rows = length // LANES
    seqs = pieces * seqs_each
    step = pl.program_id(0)
    each = high_ref.shape[0] // (2 * seqs * rows)

    @pl.when(step == 0)
    def _():
        for s in range(seqs):
            for at in range(2):
                for row in range(rows):
                    turn_ref[at * seqs + s, pl.ds(row * channels, channels), :] = piece_refs[
                        s // seqs_each
                    ][at, s % seqs_each, :, pl.ds(row * LANES, LANES)].astype(F32)

    cosine = jnp.concatenate([twist_ref[0]] * 2, axis=1)
    sine = jnp.concatenate([twist_ref[1]] * 2, axis=1)
    first = first_ref[...]

    def line(at, s, k):
        return pl.ds(((k * 2 + at) * seqs + s) * rows, rows)

    for k in range(each):
        for s in range(seqs):
            pair = jnp.concatenate(
                [
                    turn_ref[
                        at * seqs + s, pl.ds(step * each + k, rows, stride=channels), :
                    ].astype(BF16)
                    for at in range(2)
                ],
                axis=1,
            )
            both = dot(first, jnp.concatenate([pair, pair], axis=0))
            real, imag = both[:rows], both[rows:]
            real, imag = real * cosine - imag * sine, real * sine + imag * cosine
            for at, part in ((0, slice(0, LANES)), (1, slice(LANES, 2 * LANES))):
                row = jnp.concatenate([real[:, part], imag[:, part]], axis=1)
                high_ref[line(at, s, k), :], low_ref[line(at, s, k), :] = split(row)
    spec_ref[...] = dot(
        jnp.concatenate([high_ref[...], low_ref[...], high_ref[...]], axis=1), second_ref[...]
    )
    for k in range(each):
        if held:
            real, imag = held_ref[k, :, :LANES], held_ref[k, :, LANES:]
        else:
            real = imag = jnp.zeros((rows, LANES), F32)
        for s in range(seqs):
            a, b = spec_ref[line(0, s, k), :], spec_ref[line(1, s, k), :]
            a_real, a_imag, b_real, b_imag = a[:, :LANES], a[:, LANES:], b[:, :LANES], b[:, LANES:]
            real = real + (a_real * b_real + a_imag * b_imag)
            imag = imag + (a_real * b_imag - a_imag * b_real)
        if last:
            cross_line = pl.ds(pl.multiple_of((step * each + k) * rows, rows), rows)
            cross_ref[cross_line, :LANES] = real
            cross_ref[cross_line, LANES:] = imag
        else:
            out_ref[k, :, :LANES] = real
            out_ref[k, :, LANES:] = imag
    if not last:
        return

    @pl.when(step == pl.num_programs(0) - 1)
    def _():
        owners, channels, lag_count = out_ref.shape
        back_cos, back_sin = untwist_ref[0], untwist_ref[1]
        group = math.gcd(channels, 4)
        for start in range(0, channels, group):
            high, low = split(cross_ref[pl.ds(start * rows, group * rows), :])
            back = dot(jnp.concatenate([high, low, high], axis=1), back_ref[...])
            for c in range(0, group, 2):
                turned = []
                for k in range(c, c + 2):
                    real = back[k * rows : (k + 1) * rows, :LANES]
                    imag = back[k * rows : (k + 1) * rows, LANES:]
                    turned.append(
                        jnp.concatenate(
                            [real * back_cos - imag * back_sin, real * back_sin + imag * back_cos],
                            axis=0,
                        )
                    )
                lags = dot(last_ref[...], wide(jnp.concatenate(turned, axis=1), 0))
                for k in range(2):
                    lag_ref[pl.ds((start + c + k) * 2 * rows, 2 * rows), :] = lags[
                        :, k * LANES : (k + 1) * LANES
                    ]
        wide_rows = lag_count // LANES
        for owner in range(owners):
            for k in range(wide_rows):
                out_ref[owner, :, pl.ds(k * LANES, LANES)] = lag_ref[
                    pl.ds(owner * wide_rows + k, channels, stride=2 * rows), :
                ]
        half = owners // 2
        other_ref[...] = out_ref[pl.ds((1 - (lax.axis_index("dp") & 1)) * half, half)]


def correlate(pieces, held, scale, owners, lags=None, chunk=0, chunks=1):
    _, seqs_each, channels, length = pieces[0].shape
    lanes, rows = LANES, length // LANES
    seqs = seqs_each * len(pieces)
    total = 2 * length
    each = max(1, min(channels, 8 // seqs))
    first, twist, untwist, second, back, last = (
        jnp.asarray(t) for t in tables(rows, 2.0 * scale / total)
    )
    consts = [first, twist, second] + ([untwist, back, last] if owners else [])
    skip = chunk * (channels // each)
    spectrum = pl.BlockSpec((each, rows, 2 * lanes), lambda c: (c + skip, 0, 0))
    lags = [] if lags is None else [lags]
    held = [] if held is None else [held]
    block = pl.BlockSpec(pieces[0].shape, lambda c: (0, 0, 0, 0))
    whole = [
        pl.BlockSpec(t.shape, functools.partial(lambda n, c: (0,) * n, t.ndim)) for t in consts
    ]
    if owners:
        shape = (owners, channels * chunks, total // owners)
        part = (owners // 2, channels, total // owners)
        out_spec = [
            pl.BlockSpec((owners, channels, total // owners), lambda c: (0, chunk, 0)),
            pl.BlockSpec(part, lambda c: (0, 0, 0)),
        ]
        out_shape = [jax.ShapeDtypeStruct(shape, F32), jax.ShapeDtypeStruct(part, F32)]
    else:
        shape = (channels, rows, 2 * lanes)
        out_spec = spectrum
        out_shape = jax.ShapeDtypeStruct(shape, F32)
    scratch = []
    if owners:
        scratch = [
            pltpu.VMEM((channels * 2 * rows, lanes), F32),
            pltpu.VMEM((channels * rows, 2 * lanes), F32),
        ]
    scratch += [
        pltpu.VMEM((2 * seqs, rows * channels, lanes), F32),
        pltpu.VMEM((each * 2 * seqs * rows, 2 * lanes), BF16),
        pltpu.VMEM((each * 2 * seqs * rows, 2 * lanes), BF16),
        pltpu.VMEM((each * 2 * seqs * rows, 2 * lanes), F32),
    ]
    return pl.pallas_call(
        functools.partial(
            correlate_kernel,
            pieces=len(pieces),
            held=len(held),
            lags=len(lags),
            last=bool(owners),
        ),
        grid=(channels // each,),
        in_specs=[block] * len(pieces)
        + [spectrum] * len(held)
        + [pl.BlockSpec(memory_space=pl.ANY)] * len(lags)
        + whole,
        input_output_aliases={len(pieces) + len(held): 0} if lags else {},
        out_specs=out_spec,
        out_shape=out_shape,
        scratch_shapes=scratch,
        cost_estimate=pl.CostEstimate(
            flops=channels * seqs * 2 * rows * lanes * lanes * 36,
            bytes_accessed=channels * (seqs * rows * lanes * 4 + total * 4),
            transcendentals=0,
        ),
        compiler_params=pltpu.CompilerParams(vmem_limit_bytes=24 * 2**20),
        name="correlate",
    )(*pieces, *held, *lags, *consts)


STEP = 2048
BANDS_PAD = 8


def lag_row(step, second, total):
    return step * STEP + lax.broadcasted_iota(jnp.int32, (1, STEP), 1) - second * (total // 2)


def network_kernel(
    factor_ref, embed_ref, bias_ref, hidden_ref, freq_ref,
    table_ref, first_ref, second_ref, cos1_ref, cos2_ref,
    embed_parts, hidden_parts, freq_cols, *, total,
):
    hidden = hidden_ref.shape[0]
    step = pl.program_id(0)

    @pl.when(step == 0)
    def _():
        embed = jnp.concatenate(
            [
                embed_ref[1:],
                embed_ref[:1],
                bias_ref[...],
                jnp.zeros((BANDS_PAD - 2, hidden), F32),
            ],
            axis=0,
        )
        embed_parts[...] = narrow_exact(embed.T, 1)
        hidden_parts[...] = narrow_exact(hidden_ref[...], 1)
        for k in range(2):
            freq_cols[k] = column(freq_ref[k : k + 1, :])

    lag = lag_row(step, lax.axis_index("dp") & 1, total)
    length = total // 2
    phase = ((factor_ref[...] * lag) & (total - 1)).astype(F32) * (2.0 * math.pi / total)
    sine, cosine = sine_cosine(phase)
    scaled = lag.astype(F32) / length
    row = lax.broadcasted_iota(jnp.int32, (BANDS_PAD, STEP), 0)
    extra = jnp.where(row == 0, scaled, jnp.where(row == 1, 1.0, 0.0))
    table = jnp.concatenate([sine, cosine, extra], axis=0)
    table_ref[...] = stacked(table, 0)
    first, cos1 = sine_cosine(freq_cols[0] * dot(embed_parts[...], wide_exact(table, 0)))
    first_ref[...] = stacked(first, 0)
    cos1_ref[...] = cos1
    second, cos2 = sine_cosine(freq_cols[1] * dot(hidden_parts[...], wide_exact(first, 0)))
    second_ref[...] = stacked(second, 0)
    cos2_ref[...] = cos2


def network(embed_weight, embed_bias, hidden_weight, frequency, total):
    hidden, features = embed_weight.shape
    bands = (features - 1) // 2
    factors = np.array(
        [[max(1, int(0.45 * total * 10000.0 ** (-band / bands)))] for band in range(bands)], np.int32
    )
    args = (jnp.asarray(factors), embed_weight.T, embed_bias[None], hidden_weight, frequency)
    whole = [pl.BlockSpec(a.shape, lambda i: (0, 0)) for a in args]
    depth = 2 * bands + BANDS_PAD
    heights = ((2 * depth, BF16), (2 * hidden, BF16), (2 * hidden, BF16), (hidden, F32), (hidden, F32))
    return pl.pallas_call(
        functools.partial(network_kernel, total=total),
        grid=(total // 2 // STEP,),
        in_specs=whole,
        out_specs=[pl.BlockSpec((h, STEP), lambda i: (0, i)) for h, _ in heights],
        out_shape=[jax.ShapeDtypeStruct((h, total // 2), t) for h, t in heights],
        scratch_shapes=[
            pltpu.VMEM((hidden, 6 * depth), BF16),
            pltpu.VMEM((hidden, 6 * hidden), BF16),
            pltpu.VMEM((2, hidden, 1), F32),
        ],
        cost_estimate=pl.CostEstimate(
            flops=total * hidden * 600, bytes_accessed=total * hidden * 20, transcendentals=0
        ),
        name="network",
    )(*args)


def backward_kernel(place_ref, second_ref, lags_ref, *refs, others, total, pack):
    other_refs, refs = refs[:others], refs[others:]
    backward_body(place_ref, second_ref, lags_ref, other_refs, *refs, total=total, pack=pack)


def backward_body(
    place_ref, second_ref, lags_ref, other_refs, table_ref, layer1_ref, layer2_ref, cos1_ref, cos2_ref,
    decay_ref, output_ref, hidden_ref, freq_ref,
    keep_ref, send_ref, output_parts, hidden_parts, decay_col, own_ref, sum1_ref, sum3_ref, sum5_ref, *, total, pack,
):
    step = pl.program_id(0)
    owners, own, _ = lags_ref.shape
    own = 2 * own
    hidden = hidden_ref.shape[0]
    first, second_of_pair = place_ref[0], second_ref[0]

    @pl.when(step == 0)
    def _():
        for ref in (sum1_ref, sum3_ref, sum5_ref):
            ref[...] = jnp.zeros_like(ref)
        channels = output_ref.shape[1]
        own_ref[...] = pltpu.roll(output_ref[...], channels - first, 1)[:, :own]
        output_parts[...] = narrow(own_ref[...], 1)
        hidden_parts[...] = narrow((hidden_ref[...] * column(freq_ref[1:2, :])).T, 1)
        place = [lax.broadcasted_iota(jnp.int32, (own, channels), d) for d in (0, 1)]
        decay_col[...] = jnp.sum(
            jnp.where(place[1] == place[0] + first, decay_ref[...], 0.0), axis=1, keepdims=True
        )

    mine = jnp.concatenate([lags_ref[k] for k in range(owners)], axis=1)
    others = jnp.concatenate(
        [jnp.concatenate([ref[k] for k in range(owners)], axis=1) for ref in other_refs], axis=0
    )
    upper = second_of_pair != 0
    lags = jnp.concatenate(
        [jnp.where(upper, others, mine), jnp.where(upper, mine, others)], axis=0
    )
    length = total // 2
    distance = jnp.abs(lag_row(step, second_of_pair, total)).astype(F32)
    window = jnp.exp(-decay_col[...] * distance / length)
    shaped = lags * window * (1.0 / math.sqrt(total))
    far = shaped * (distance / length)
    sum1_ref[...] += dot_lanes(stacked(jnp.concatenate([shaped, far], axis=0), 0), layer2_ref[...])
    second = dot(output_parts[...], wide(shaped, 0)) * cos2_ref[...]
    high, low = split(second)
    sum3_ref[...] += dot_lanes(jnp.concatenate([high, low], axis=0), layer1_ref[...])
    below = dot(hidden_parts[...], jnp.concatenate([high, high, low], axis=0)) * cos1_ref[...]
    sum5_ref[...] += dot_lanes(stacked(below, 0), table_ref[...])

    @pl.when(step == pl.num_programs(0) - 1)
    def _():
        def joined(ref):
            rows, cols = ref.shape[0] // 2, ref.shape[1] // 2
            return ref[:rows, :cols] + ref[:rows, cols:] + ref[rows:, :cols]

        net = jnp.concatenate([joined(sum3_ref), joined(sum5_ref)], axis=1)
        net = jnp.concatenate([net, jnp.zeros((hidden, LANES - net.shape[1]), F32)], axis=1)
        sums = joined(sum1_ref)
        decay_grad = -jnp.sum(own_ref[...].T * sums[own:], axis=1, keepdims=True)
        per, half = own // pack, keep_ref.shape[0]
        summed = half - per // 2
        height = 2 * summed - hidden
        place = lax.broadcasted_iota(jnp.int32, (height, LANES), 0) * LANES
        place = place + lax.broadcasted_iota(jnp.int32, (height, LANES), 1) - first
        decays = jnp.zeros((height, LANES), F32)
        for c in range(own):
            decays = jnp.where(place == c, decay_grad[c : c + 1], decays)
        parts = [sums[k * per : (k + 1) * per] for k in range(pack)]
        parts += [jnp.zeros((per, LANES - pack * hidden), F32)] if pack * hidden < LANES else []
        rows = jnp.concatenate(parts, axis=1)
        total_rows = jnp.concatenate([net, decays], axis=0)
        low = jnp.concatenate([total_rows[:summed], rows[: per // 2]], axis=0)
        high = jnp.concatenate([total_rows[summed:], rows[per // 2 :]], axis=0)
        keep_ref[...] = jnp.where(upper, high, low)
        send_ref[...] = jnp.where(upper, low, high)


def packing(own, hidden):
    return 2 if own % 16 == 0 and 2 * hidden <= LANES else 1


def summed_rows(hidden, channels):
    return -(-(hidden + -(-channels // LANES)) // 16) * 8


def backward(first, second, lags, others, saved, decay_rate, output_weight, hidden_weight, frequency, total):
    _, own, lag_count = lags.shape
    own = 2 * own
    hidden = hidden_weight.shape[0]
    pack = packing(own, hidden)
    height = summed_rows(hidden, decay_rate.shape[0]) + own // pack // 2
    steps = total // 2 // STEP
    args = (decay_rate[None], output_weight.T, hidden_weight, frequency)
    specs = [
        pl.BlockSpec((STEP // lag_count, own // 2, lag_count), lambda i, at, second: (i + second[0] * steps, 0, 0))
    ]
    specs += [
        pl.BlockSpec((STEP // lag_count, *a.shape[1:]), lambda i, at, second: (i, 0, 0)) for a in others
    ]
    specs += [pl.BlockSpec((a.shape[0], STEP), lambda i, at, second: (0, i)) for a in saved]
    specs += [pl.BlockSpec(a.shape, lambda i, at, second: (0, 0)) for a in args]
    return pl.pallas_call(
        functools.partial(backward_kernel, others=len(others), total=total, pack=pack),
        grid_spec=pltpu.PrefetchScalarGridSpec(
            num_scalar_prefetch=2,
            grid=(steps,),
            in_specs=specs,
            out_specs=[pl.BlockSpec((height, LANES), lambda i, at, second: (0, 0))] * 2,
            scratch_shapes=[
                pltpu.VMEM((hidden, 3 * own), BF16),
                pltpu.VMEM((hidden, 3 * hidden), BF16),
                pltpu.VMEM((own, 1), F32),
                pltpu.VMEM((hidden, own), F32),
                pltpu.VMEM((4 * own, 2 * hidden), F32),
                pltpu.VMEM((2 * hidden, 2 * hidden), F32),
                pltpu.VMEM((2 * hidden, saved[0].shape[0]), F32),
            ],
        ),
        out_shape=[jax.ShapeDtypeStruct((height, LANES), F32)] * 2,
        cost_estimate=pl.CostEstimate(
            flops=total * hidden * 1000, bytes_accessed=total * hidden * 10, transcendentals=0
        ),
        name="backward",
    )(first.reshape(1), second.reshape(1), lags, *others, *saved, *args)


def rounds():
    steps = []
    for axis in ("dp", "chan"):
        bits = [1 << b for b in range(lax.axis_size(axis).bit_length() - 1)]
        for group in [bits[b : b + 2] for b in range(axis == "dp", len(bits), 2)]:
            masks = [0]
            for bit in group:
                masks += [mask | bit for mask in masks]
            if len(masks) > 1:
                steps.append((axis, masks))
    return steps


def share(keep, send, summed):
    steps = rounds()
    pair = [(i, i ^ 1) for i in range(lax.axis_size("dp"))]
    both = keep + lax.ppermute(send, "dp", pair)
    for axis, masks in steps:
        size = lax.axis_size(axis)
        parts = [both]
        for mask in masks[1:]:
            parts.append(lax.ppermute(both, axis, [(i, i ^ mask) for i in range(size)]))
        total = sum(part[:summed] for part in parts)
        both = jnp.concatenate([total, *(part[summed:] for part in parts)], axis=0)
    return both, lax.ppermute(both, "dp", pair)


def finish_kernel(*refs, own, pack):
    steps = rounds()
    mine_ref, theirs_ref, embed_ref, bias_ref, hidden_ref, freq_ref = refs[:6]
    embed_grad, bias_grad, hidden_grad, frequency_grad, output_grad, decay_grad, rows_ref = refs[6:]
    hidden, features = hidden_ref.shape[0], embed_ref.shape[0]
    summed = summed_rows(hidden, output_grad.shape[1])
    upper = (lax.axis_index("dp") & 1) != 0
    low = jnp.where(upper, theirs_ref[...], mine_ref[...])
    high = jnp.where(upper, mine_ref[...], theirs_ref[...])
    total = jnp.concatenate([low[:summed], high[:summed]], axis=0)
    net = total[:hidden]
    turned = net.T
    decay_grad[...] = total[hidden : hidden + decay_grad.shape[0]]
    unit = own // pack // 2
    count = output_grad.shape[1] // own
    here = {axis: lax.axis_index(axis) for axis in ("dp", "chan")}
    for k in range(count):
        there, rest = dict(here), k
        for axis, masks in steps:
            there[axis] = there[axis] ^ masks[rest % len(masks)]
            rest //= len(masks)
        place = there["chan"] * (lax.axis_size("dp") // 2) + (there["dp"] >> 1)
        for n in range(pack):
            for m, half in enumerate((low, high)):
                at = pl.multiple_of(place * own + (2 * n + m) * unit, unit)
                rows_ref[pl.ds(at, unit), :] = half[
                    summed + k * unit : summed + (k + 1) * unit, n * hidden : (n + 1) * hidden
                ]
    output_grad[...] = rows_ref[...].T
    table = turned[hidden:]
    embed = jnp.concatenate([table[features - 1 : features], table[: features - 1]], axis=0)
    bias = table[features : features + 1]
    embed_grad[...] = freq_ref[:1] * embed
    bias_grad[...] = freq_ref[:1] * bias
    hidden_grad[...] = column(freq_ref[1:2, :]) * net[:, :hidden]
    frequency_grad[:1] = (
        jnp.sum(embed_ref[...] * embed, axis=0, keepdims=True) + bias_ref[...] * bias
    )
    frequency_grad[1:2] = jnp.sum(hidden_ref[...].T * turned[:hidden], axis=0, keepdims=True)


def finish(mine, theirs, embed_weight, embed_bias, hidden_weight, frequency, channels, own):
    hidden, features = embed_weight.shape
    shapes = (
        (features, hidden), (1, hidden), (hidden, hidden), (2, hidden), (hidden, channels),
        (-(-channels // LANES), LANES),
    )
    embed, bias, hid, freq, output, decay = pl.pallas_call(
        functools.partial(finish_kernel, own=own, pack=packing(own, hidden)),
        out_shape=[jax.ShapeDtypeStruct(shape, F32) for shape in shapes],
        scratch_shapes=[pltpu.VMEM((channels, hidden), F32)],
        compiler_params=pltpu.CompilerParams(vmem_limit_bytes=8 * 2**20),
        name="finish",
    )(mine, theirs, embed_weight.T, embed_bias[None], hidden_weight, frequency)
    return embed.T, bias[0], hid, freq, output.T, decay.reshape(-1)[:channels]


def work(
    signal,
    signal_grad,
    embed_weight,
    embed_bias,
    hidden_weight,
    frequency,
    output_weight,
    decay_rate,
):
    seq_local, chan_local, length = signal.shape
    total = 2 * length
    dp, chan = lax.axis_size("dp"), lax.axis_size("chan")
    own = chan_local // dp
    count = dp * chan
    hidden = hidden_weight.shape[0]
    channels = chan * chan_local
    scale = 1.0 / math.sqrt(seq_local * dp * length)
    at_dp, at_chan = lax.axis_index("dp"), lax.axis_index("chan")

    partners = sorted(
        range(1, dp), key=lambda p: (p != 1, -bin(p >> 1).count("1"), p & 1, p)
    )
    chunks = 2 if own % 16 == 0 and dp > 2 else 1
    per = own // chunks
    late = partners[-2:] if chunks > 1 else []
    soon = [p for p in (0, *partners) if p not in late]
    items = [(p, 0, own) for p in (*partners[1:3], partners[0], *soon[4:], 0)]
    items += [(p, q * per, per) for q in range(chunks) for p in late]
    made, pieces = [], {}
    for some in (tuple(items[:2]), tuple(items[2:])):
        made = pick(signal, signal_grad, some, own, made[:1])
        for (p, start, _), sent in zip(some, made):
            swap = [(i, i ^ p) for i in range(dp)]
            pieces[p, start] = lax.ppermute(sent, "dp", swap) if p else sent
    lags = spectrum = None
    step = max(2, dp // 4)
    for at in range(0, len(soon), step):
        end = not late and at + step >= len(soon)
        spectrum = correlate(
            [pieces[p, 0] for p in soon[at : at + step]], spectrum, scale, count if end else 0
        )
    lags, others = (None, []) if late else (spectrum[0], [spectrum[1]])
    for q in range(chunks if late else 0):
        lags, other = correlate(
            [pieces[p, q * per] for p in late], spectrum, scale, count, lags, q, chunks
        )
        others.append(other)
    for q, other in enumerate(others):
        others[q] = lax.ppermute(other, "dp", [(i, i ^ 1) for i in range(dp)])

    saved = network(embed_weight, embed_bias, hidden_weight, frequency, total)
    shared = lax.all_to_all(lags, ("dp", "chan"), 0, 0, tiled=True)
    first = at_chan * chan_local + (at_dp & -2) * own
    keep, send = backward(
        first, at_dp & 1, lags, others, saved, decay_rate, output_weight, hidden_weight, frequency, total
    )
    mine, theirs = share(keep, send, summed_rows(hidden, channels))
    filter_grad = jnp.swapaxes(shared.reshape(dp, chan, own, -1), 0, 1)
    filter_grad = filter_grad.reshape(channels, -1)
    return (
        filter_grad,
        *finish(mine, theirs, embed_weight, embed_bias, hidden_weight, frequency, channels, 2 * own),
    )


def solution(mesh):
    placed = (P("dp", "chan", None), P("dp", "chan", None), P(), P(), P(), P(), P(), P())
    return jax.shard_map(
        work,
        mesh=mesh,
        in_specs=placed,
        out_specs=(P(None, ("dp", "chan")), P(), P(), P(), P(), P(), P()),
        check_vma=False,
    )
```
